32 devices in a mesh: gx: 8 (over y, x, core), gy: 4 (over z).
Axes of the slice: x: 2, y: 2, z: 4, core: 2. Of those that a mesh axis runs over, the one named last changes fastest.
Arguments:
- pressure: float32 [64, 128, 128], P('gx', 'gy'), may hold values from -6 to 6
- source: float32 [64, 128, 128], P('gx', 'gy'), may hold values from -8 to 8, as said below
- coefficient: float32 [64, 128, 128], P('gx', 'gy'), may hold values from 0.1 to 1
Outputs:
- corrected: float32 [64, 128, 128], P('gx', 'gy')
The draws below stay inside these ranges and needn't reach their ends.
Inputs may be any that keep to these rules, and one draw needn't show every extreme that they name: `source`: a rough field with a smooth part.
All inputs are finite; a program needn't handle non-finite values.
Results may differ from the reference program's by a relative error of at most 0.0001.
Values sent between devices are 32-bit elements; how exact they have to be, the bound alone decides.
No kernel may reach another device: no remote copies, remote signals or barrier semaphores. Data moves between devices by JAX's collectives and lax.ppermute only.
A program may use at most 128 MiB of HBM per device.

```python
import math
import jax
import jax.numpy as jnp
from jax import lax

CZ = 128
SWEEPS = 2
CSWEEPS = 4
NX = 64
NY = 128


def draw_source(key, part):
    rough = jnp.clip(jax.random.normal(key, (NX, NY, CZ), jnp.float32), -5.0, 5.0)
    amplitude = 0.03
    along_x = jnp.sin(jnp.pi * (jnp.arange(NX, dtype=jnp.float32) + 0.5) / NX)
    along_y = jnp.sin(jnp.pi * (jnp.arange(NY, dtype=jnp.float32) + 0.5) / NY)
    along_z = jnp.sin(jnp.pi * (jnp.arange(CZ, dtype=jnp.float32) + 0.5) / CZ)
    smooth = along_x[:, None, None] * along_y[None, :, None] * along_z[None, None, :]
    return rough + amplitude * 8.0 * smooth


def steps_of(own_key, dims, split, least, top_value):
    loudness = 1.0
    for position, parts in split:
        heights = jax.random.uniform(jax.random.fold_in(jax.random.fold_in(own_key, 6), position), (parts,), jnp.float32, least / len(split), top_value / len(split))
        loudness = loudness * jnp.repeat(jnp.exp(heights), dims[position] // parts).reshape((-1,) + (1,) * (len(dims) - 1 - position))
    return loudness


def bell_draw(stream_key, dims, width, bound, cuts=(), held_as=jnp.bfloat16):
    level = steps_of(stream_key, dims, cuts, -0.22, 0.18) if cuts else 1.0
    entries = jax.random.normal(stream_key, dims, jnp.float32) * width * level
    return jnp.minimum(jnp.maximum(entries, -bound), bound).astype(held_as)


def setup_inputs(seed: int = 0) -> dict:
    arg_keys = jax.random.split(jax.random.key(seed), 4)
    return {
        "pressure": bell_draw(arg_keys[0], (NX, NY, CZ), 1.0, 6.0, ((0, 8), (1, 4)), jnp.float32),
        "source": draw_source(jax.random.fold_in(arg_keys[3], 71), 0),
        "coefficient": jnp.clip(jnp.exp(math.log(1.0) - 2.3025851 * jax.random.uniform(arg_keys[2], (NX, NY, CZ), jnp.float32) ** steps_of(arg_keys[2], (NX, NY, CZ), ((0, 8), (1, 4)), -0.2, 0.2)), 0.1, 1.0),
    }


def restrict(field):
    size_x, size_y, size_z = field.shape
    return field.reshape(size_x // 2, 2, size_y // 2, 2, size_z // 2, 2).mean(axis=(1, 3, 5))


def pad_plane(field):
    return jnp.pad(field, ((1, 1), (1, 1), (0, 0)))


def pad_depth(field):
    return jnp.pad(field, ((0, 0), (0, 0), (1, 1)))


def level_weights(coef_pad):
    padded = pad_depth(coef_pad)
    east_west = (padded[1:, 1:-1, 1:-1] + padded[:-1, 1:-1, 1:-1]) * 0.5
    north_south = (padded[1:-1, 1:, 1:-1] + padded[1:-1, :-1, 1:-1]) * 0.5
    up_down = (padded[1:-1, 1:-1, 1:] + padded[1:-1, 1:-1, :-1]) * 0.5
    diagonal = east_west[1:] + east_west[:-1] + north_south[:, 1:] + north_south[:, :-1] + up_down[:, :, 1:] + up_down[:, :, :-1]
    return (east_west, north_south, up_down), diagonal


def neighbour_sum(field_pad, weights):
    east_west, north_south, up_down = weights
    padded = pad_depth(field_pad)
    total = east_west[:-1] * padded[:-2, 1:-1, 1:-1] + east_west[1:] * padded[2:, 1:-1, 1:-1]
    total = total + north_south[:, :-1] * padded[1:-1, :-2, 1:-1] + north_south[:, 1:] * padded[1:-1, 2:, 1:-1]
    total = total + up_down[:, :, :-1] * padded[1:-1, 1:-1, :-2] + up_down[:, :, 1:] * padded[1:-1, 1:-1, 2:]
    return total


def parity_of(shape):
    summed = lax.broadcasted_iota(jnp.int32, shape, 0) + lax.broadcasted_iota(jnp.int32, shape, 1) + lax.broadcasted_iota(jnp.int32, shape, 2)
    return summed % 2


def sweep(field, rhs, weights, diagonal, level, faces):
    scale_up = 4.0 ** level
    parity = parity_of(field.shape)
    for colour in (0, 1):
        total = neighbour_sum(faces(field), weights)
        fresh = (rhs * scale_up + total) / diagonal
        field = jnp.where(parity == colour, fresh, field)
    return field


def residual_of(field, rhs, weights, diagonal, level, faces):
    total = neighbour_sum(faces(field), weights)
    return rhs - (diagonal * field - total) * (4.0 ** (-level))


def coarse_solve(rhs, weights, diagonal):
    scale_down = 4.0 ** (-3)
    error = jnp.zeros_like(rhs)
    remain = rhs
    direction = rhs
    norm_now = jnp.sum(remain * remain)
    for repeat in range(CSWEEPS):
        image = (diagonal * direction - neighbour_sum(pad_plane(direction), weights)) * scale_down
        alpha = norm_now / jnp.sum(direction * image)
        error = error + alpha * direction
        remain = remain - alpha * image
        norm_next = jnp.sum(remain * remain)
        direction = remain + (norm_next / norm_now) * direction
        norm_now = norm_next
    return error


def prolong_axis(padded, axis):
    length = padded.shape[axis]
    middle = lax.slice_in_dim(padded, 1, length - 1, axis=axis)
    before = lax.slice_in_dim(padded, 0, length - 2, axis=axis)
    after = lax.slice_in_dim(padded, 2, length, axis=axis)
    lower = 0.75 * middle + 0.25 * before
    upper = 0.75 * middle + 0.25 * after
    joined = jnp.stack([lower, upper], axis=axis + 1)
    shape = list(middle.shape)
    shape[axis] = 2 * shape[axis]
    return joined.reshape(shape)


def prolong3(plane_pad):
    padded = pad_depth(plane_pad)
    padded = prolong_axis(padded, 0)
    padded = prolong_axis(padded, 1)
    return prolong_axis(padded, 2)


def reference(pressure, source, coefficient):
    coef_one = restrict(coefficient)
    coef_two = restrict(coef_one)
    coef_three = restrict(coef_two)
    weights0, diagonal0 = level_weights(pad_plane(coefficient))
    weights1, diagonal1 = level_weights(pad_plane(coef_one))
    weights2, diagonal2 = level_weights(pad_plane(coef_two))
    weights3, diagonal3 = level_weights(pad_plane(coef_three))
    smoothed = pressure
    for repeat in range(SWEEPS):
        smoothed = sweep(smoothed, source, weights0, diagonal0, 0, pad_plane)
    rhs_one = restrict(residual_of(smoothed, source, weights0, diagonal0, 0, pad_plane))
    error_one = sweep(jnp.zeros_like(rhs_one), rhs_one, weights1, diagonal1, 1, pad_plane)
    rhs_two = restrict(residual_of(error_one, rhs_one, weights1, diagonal1, 1, pad_plane))
    error_two = sweep(jnp.zeros_like(rhs_two), rhs_two, weights2, diagonal2, 2, pad_plane)
    rhs_three = restrict(residual_of(error_two, rhs_two, weights2, diagonal2, 2, pad_plane))
    error_three = coarse_solve(rhs_three, weights3, diagonal3)
    error_two = error_two + prolong3(pad_plane(error_three))
    error_one = error_one + prolong3(pad_plane(error_two))
    return smoothed + prolong3(pad_plane(error_one))
```

```python
import functools
import jax
import jax.numpy as jnp
from jax import lax
from jax.experimental import pallas as pl
from jax.experimental.pallas import tpu as pltpu
from jax.sharding import PartitionSpec as P

CSWEEPS = 4
REACH = 9
ORIGIN = 16
VMEM_LIMIT = 48 * 1024 * 1024


def y_rows(distance):
    return REACH if distance <= 2 else REACH + 2 - distance


def y_plan(cells_x):
    pieces = []
    start = 0
    for array in range(3):
        for plane in range(cells_x + 2 * REACH):
            x = plane - REACH
            distance = max(0, -x, x - cells_x + 1)
            if array == 1 and distance == REACH:
                continue
            rows = y_rows(distance)
            pieces.append((array, plane, start, rows))
            start += rows
    return pieces, -(-start // 8) * 8


def shifts(axis, step):
    count = lax.axis_size(axis)
    return [(i, i + step) for i in range(count) if 0 <= i + step < count]


def plane_source(array, plane, cells_x, own, low, high, low2, high2):
    x = plane - REACH
    far = 0 if array == 0 else 1
    if x < -cells_x:
        return low2, far
    if x < 0:
        return low, array * cells_x + cells_x + x
    if x < cells_x:
        return own[array], x
    if x < 2 * cells_x:
        return high, array * cells_x + x - cells_x
    return high2, far


def pack_kernel(p, f, k, low, high, low2, high2, to_up, to_down):
    cells_x, cells_y, _ = p.shape
    pieces, _ = y_plan(cells_x)
    for array, plane, start, rows in pieces:
        ref, index = plane_source(array, plane, cells_x, (p, f, k), low, high, low2, high2)
        to_up[pl.ds(start, rows), :] = ref[index, pl.ds(cells_y - rows, rows), :]
        to_down[pl.ds(start, rows), :] = ref[index, pl.ds(0, rows), :]


def fine_halo(pressure, source, coefficient):
    cells_x, _, depth = pressure.shape
    block = jnp.concatenate([pressure, source, coefficient], 0)
    far_up = jnp.concatenate([pressure[-1:], coefficient[-1:]], 0)
    far_down = jnp.concatenate([pressure[:1], coefficient[:1]], 0)
    low = lax.ppermute(block, "gx", shifts("gx", 1))
    high = lax.ppermute(block, "gx", shifts("gx", -1))
    low2 = lax.ppermute(far_up, "gx", shifts("gx", 2))
    high2 = lax.ppermute(far_down, "gx", shifts("gx", -2))
    _, length = y_plan(cells_x)
    packed = jax.ShapeDtypeStruct((length, depth), jnp.float32)
    to_up, to_down = pl.pallas_call(
        pack_kernel,
        out_shape=(packed, packed),
        compiler_params=pltpu.CompilerParams(vmem_limit_bytes=VMEM_LIMIT),
        name="pack_halo",
    )(pressure, source, coefficient, low, high, low2, high2)
    below = lax.ppermute(to_up, "gy", shifts("gy", 1))
    above = lax.ppermute(to_down, "gy", shifts("gy", -1))
    return low, high, low2, high2, below, above


def smooth_kernel(
    p, f, k, low, high, low2, high2, below, above,
    out, error_one, tiles,
    vp, vf, vk, wx, wy, zl, zh, dg, inv, va, vb,
    t0, t1, f1, k1, inv1, g1, h1, q2,
):
    cells_x, cells_y, depth = p.shape
    planes = cells_x + 2 * REACH
    own_rows = pl.ds(ORIGIN, cells_y)
    top = ORIGIN - REACH + 1
    rows = cells_y + 2 * (REACH - 1)
    body = pl.ds(top, rows)

    for array, window in ((0, vp), (1, vf), (2, vk)):
        for plane in range(planes):
            if array == 1 and plane in (0, planes - 1):
                continue
            ref, index = plane_source(array, plane, cells_x, (p, f, k), low, high, low2, high2)
            value = ref[index]
            window[plane, own_rows, :] = value + value if array == 1 else value
    pieces, _ = y_plan(cells_x)
    for array, plane, start, count in pieces:
        window = (vp, vf, vk)[array]
        before = below[pl.ds(start, count), :]
        after = above[pl.ds(start, count), :]
        if array == 1:
            before = before + before
            after = after + after
        window[plane, pl.ds(ORIGIN - count, count), :] = before
        window[plane, pl.ds(ORIGIN + cells_y, count), :] = after

    def lanes(count):
        return lax.broadcasted_iota(jnp.int32, (count, depth), 1)

    def rows_of(first, count):
        return lax.broadcasted_iota(jnp.int32, (count, depth), 0) + (first - ORIGIN)

    lane = lanes(rows)

    def weigh(plane, _):
        centre = vk[plane, body, :]
        west = centre + vk[plane - 1, body, :]
        wx[plane, body, :] = west
        east = centre + vk[plane + 1, body, :]
        south = centre + vk[plane, pl.ds(top - 1, rows), :]
        north = centre + vk[plane, pl.ds(top + 1, rows), :]
        wy[plane, body, :] = south
        wy[plane, pl.ds(top + rows, 1), :] = north[rows - 1:, :]
        down = jnp.where(lane > 0, pltpu.roll(centre, 1, 1), 0.0)
        up = jnp.where(lane < depth - 1, pltpu.roll(centre, depth - 1, 1), 0.0)
        total = west + east + south + north + (centre + down) + (centre + up)
        zl[plane, body, :] = jnp.where(lane > 0, centre + down, 0.0)
        zh[plane, body, :] = jnp.where(lane < depth - 1, centre + up, 0.0)
        dg[plane, body, :] = total
        inside = centre > 0.0
        inv[plane, body, :] = jnp.where(inside, 1.0 / jnp.where(inside, total, 1.0), 0.0)
        return 0

    lax.fori_loop(1, planes - 1, weigh, 0)
    wx[planes - 1, body, :] = vk[planes - 1, body, :] + vk[planes - 2, body, :]

    def stencil(v, plane, first, count):
        here = pl.ds(first, count)
        centre = v[plane, here, :]
        total = wx[plane, here, :] * v[plane - 1, here, :] + wx[plane + 1, here, :] * v[plane + 1, here, :]
        total += wy[plane, here, :] * v[plane, pl.ds(first - 1, count), :]
        total += wy[plane, pl.ds(first + 1, count), :] * v[plane, pl.ds(first + 1, count), :]
        total += zl[plane, here, :] * pltpu.roll(centre, 1, 1)
        total += zh[plane, here, :] * pltpu.roll(centre, depth - 1, 1)
        return total

    def relax(source_ref, target, reach):
        def one(plane, _):
            total = stencil(source_ref, plane, top, rows)
            target[plane, body, :] = inv[plane, body, :] * (vf[plane, body, :] + total)
            return 0

        lax.fori_loop(REACH - reach, REACH + cells_x + reach, one, 0)

    relax(vp, va, REACH - 1)
    relax(va, vb, REACH - 2)
    relax(vb, va, REACH - 3)
    relax(va, vb, REACH - 4)

    own_lane = lanes(cells_y)
    own_row = rows_of(ORIGIN, cells_y)
    for x in range(cells_x):
        even = ((own_row + own_lane + x) & 1) == 0
        out[x] = jnp.where(even, va[REACH + x, own_rows, :], vb[REACH + x, own_rows, :])

    planes_one = cells_x // 2
    first = ORIGIN - 4
    count = cells_y + 8
    lane = lanes(count)
    row = rows_of(first, count)

    def pair_lane(value, stride, lane):
        up = pltpu.roll(value, depth - stride, 1)
        down = pltpu.roll(value, stride, 1)
        return value + jnp.where((lane & stride) == 0, up, down)

    def pair_row(ref, index, first, count, stride, row):
        centre = ref[index, pl.ds(first, count), :]
        up = ref[index, pl.ds(first + stride, count), :]
        down = ref[index, pl.ds(first - stride, count), :]
        return centre + jnp.where((row & stride) == 0, up, down)

    def residual(plane_one, _):
        total = jnp.zeros((count, depth), jnp.float32)
        for half in range(2):
            plane = 2 * plane_one + REACH - 4 + half
            here = pl.ds(first, count)
            twice = vf[plane, here, :] - dg[plane, here, :] * va[plane, here, :] + stencil(vb, plane, first, count)
            even = ((row + lane + half) & 1) == 0
            total += jnp.where(even, twice, 0.0)
        t0[plane_one, pl.ds(first, count), :] = pair_lane(total, 1, lane)
        return 0

    lax.fori_loop(0, planes_one + 4, residual, 0)
    for x in range(planes_one + 4):
        f1[x, pl.ds(first, count), :] = 0.5 * pair_row(t0, x, first, count, 1, row)

    first_k = ORIGIN - 6
    count_k = cells_y + 16
    lane_k = lanes(count_k)
    row_k = rows_of(first_k, count_k)
    for x in range(planes_one + 6):
        plane = 2 * x + REACH - 6
        here = pl.ds(first_k, count_k)
        t1[x, here, :] = pair_lane(vk[plane, here, :] + vk[plane + 1, here, :], 1, lane_k)
    for x in range(planes_one + 6):
        k1[x, pl.ds(first_k, count_k), :] = 0.125 * pair_row(t1, x, first_k, count_k, 1, row_k)

    def down2(value, lane):
        return jnp.where(lane >= 2, pltpu.roll(value, 2, 1), 0.0)

    def up2(value, lane):
        return jnp.where(lane < depth - 2, pltpu.roll(value, depth - 2, 1), 0.0)

    here = pl.ds(first, count)
    for x in range(planes_one + 4):
        centre = k1[x + 1, here, :]
        total = 6.0 * centre + (k1[x, here, :] + k1[x + 2, here, :])
        total += k1[x + 1, pl.ds(first - 2, count), :] + k1[x + 1, pl.ds(first + 2, count), :]
        total += down2(centre, lane) + up2(centre, lane)
        inside = centre > 0.0
        inverse = jnp.where(inside, 1.0 / jnp.where(inside, total, 1.0), 0.0)
        inv1[x, here, :] = inverse
        g1[x, here, :] = inverse * f1[x, here, :]

    def stencil_one(v, x, v_x, first, count, lane):
        here = pl.ds(first, count)
        south = pl.ds(first - 2, count)
        north = pl.ds(first + 2, count)
        kc = k1[x, here, :]
        vc = v[v_x, here, :]
        total = (kc + k1[x - 1, here, :]) * v[v_x - 1, here, :] + (kc + k1[x + 1, here, :]) * v[v_x + 1, here, :]
        total += (kc + k1[x, south, :]) * v[v_x, south, :] + (kc + k1[x, north, :]) * v[v_x, north, :]
        total += (kc + down2(kc, lane)) * down2(vc, lane) + (kc + up2(kc, lane)) * up2(vc, lane)
        return total

    first_h = ORIGIN - 2
    count_h = cells_y + 8
    lane_h = lanes(count_h)
    row_h = rows_of(first_h, count_h)
    for x in range(planes_one + 2):
        here = pl.ds(first_h, count_h)
        total = stencil_one(g1, x + 2, x + 1, first_h, count_h, lane_h)
        odd = inv1[x + 1, here, :] * (f1[x + 1, here, :] + total)
        h1[x, here, :] = odd
        even_cell = ((x - 1 + (row_h >> 1) + (lane_h >> 1)) & 1) == 0
        error_one[x, pl.ds(first_h - 8, count_h), :] = jnp.where(even_cell, g1[x + 1, here, :], odd)

    own2 = own_lane
    row2 = own_row
    for x in range(planes_one // 2):
        sum_r = jnp.zeros((cells_y, depth), jnp.float32)
        for half in range(2):
            x1 = 2 * x + half
            total = stencil_one(h1, x1 + 3, x1 + 1, ORIGIN, cells_y, own2)
            even_cell = ((x1 + (row2 >> 1) + (own2 >> 1)) & 1) == 0
            sum_r += jnp.where(even_cell, total, 0.0)
        sum_k = k1[2 * x + 3, own_rows, :] + k1[2 * x + 4, own_rows, :]
        t0[x, own_rows, :] = pair_lane(sum_r, 2, own2)
        t1[x, own_rows, :] = pair_lane(sum_k, 2, own2)
    lane8 = lanes(cells_y // 4)
    tile = jnp.zeros((cells_y // 4, depth), jnp.float32)
    for x in range(planes_one // 2):
        q2[0] = (1.0 / 64.0) * pair_row(t0, x, ORIGIN, cells_y, 2, row2)
        q2[1] = 0.125 * pair_row(t1, x, ORIGIN, cells_y, 2, row2)
        for field in range(2):
            kept = q2[field, pl.ds(0, cells_y // 4, stride=4), :]
            tile = jnp.where((lane8 & 3) == 2 * field + x, kept, tile)
    tiles[...] = jnp.broadcast_to(tile[None], tiles.shape)


def smooth(copies, pressure, source, coefficient, halo):
    cells_x, cells_y, depth = pressure.shape
    planes = cells_x + 2 * REACH
    tall = cells_y + 2 * ORIGIN
    planes_one = cells_x // 2
    window = pltpu.VMEM((planes, tall, depth), jnp.float32)

    def level_one(count):
        return pltpu.VMEM((count, tall, depth), jnp.float32)

    return pl.pallas_call(
        smooth_kernel,
        out_shape=(
            jax.ShapeDtypeStruct((cells_x, cells_y, depth), jnp.float32),
            jax.ShapeDtypeStruct((planes_one + 2, cells_y + 16, depth), jnp.float32),
            jax.ShapeDtypeStruct((copies, cells_y // 4, depth), jnp.float32),
        ),
        scratch_shapes=[window] * 11
        + [
            level_one(planes_one + 4),
            level_one(planes_one + 6),
            level_one(planes_one + 4),
            level_one(planes_one + 6),
            level_one(planes_one + 4),
            level_one(planes_one + 4),
            level_one(planes_one + 2),
            pltpu.VMEM((2, cells_y, depth), jnp.float32),
        ],
        compiler_params=pltpu.CompilerParams(vmem_limit_bytes=VMEM_LIMIT),
        name="smooth",
    )(pressure, source, coefficient, *halo)


def ring(value, shift, axis):
    return pltpu.roll(value, shift % value.shape[axis], axis)


def before_x(v):
    return jnp.concatenate([jnp.zeros_like(v[:1]), v[:-1]], 0)


def after_x(v):
    return jnp.concatenate([v[1:], jnp.zeros_like(v[:1])], 0)


class Places:
    def __init__(self, shape):
        self.row = lax.broadcasted_iota(jnp.int32, shape, 1)
        self.lane = lax.broadcasted_iota(jnp.int32, shape, 2)
        self.part = self.lane & 3
        self.depth = shape[2]

    def before_y(self, v, stride):
        turned = ring(v, stride, 1)
        return jnp.where(self.row >= stride, turned, ring(turned, 1, 2))

    def after_y(self, v, stride):
        turned = ring(v, -stride, 1)
        return jnp.where(self.row < 8 - stride, turned, ring(turned, -1, 2))

    def has_before_y(self, stride):
        return (self.row >= stride) | (self.part > 0)

    def has_after_y(self, stride):
        return (self.row < 8 - stride) | (self.part < 3)

    def has_before_z(self, stride):
        return self.lane >= 4 * stride

    def has_after_z(self, stride):
        return self.lane < self.depth - 4 * stride


def whole_weights(k, places, stride):
    west = k + before_x(k)
    east = k + after_x(k)
    masks = (
        places.has_before_y(stride),
        places.has_after_y(stride),
        places.has_before_z(stride),
        places.has_after_z(stride),
    )
    near = (
        places.before_y(k, stride),
        places.after_y(k, stride),
        ring(k, 4 * stride, 2),
        ring(k, -4 * stride, 2),
    )
    diagonal = west + east
    weights = [west, east]
    for mask, value in zip(masks, near):
        diagonal += k + jnp.where(mask, value, 0.0)
        weights.append(jnp.where(mask, k + value, 0.0))
    return weights, diagonal


def whole_sum(v, weights, places, stride):
    total = weights[0] * before_x(v) + weights[1] * after_x(v)
    total += weights[2] * places.before_y(v, stride) + weights[3] * places.after_y(v, stride)
    total += weights[4] * ring(v, 4 * stride, 2) + weights[5] * ring(v, -4 * stride, 2)
    return total


def whole_solve(k2, rhs2):
    planes = k2.shape[0]
    places = Places(k2.shape)
    weights, diagonal = whole_weights(k2, places, 1)
    parity = lax.broadcasted_iota(jnp.int32, k2.shape, 0) + places.row + (places.lane >> 2)
    even = (parity & 1) == 0
    inverse = 1.0 / diagonal
    scaled = 32.0 * rhs2
    even_values = inverse * scaled
    odd_values = inverse * (scaled + whole_sum(even_values, weights, places, 1))
    error_two = jnp.where(even, even_values, odd_values)
    left = jnp.where(even, whole_sum(odd_values, weights, places, 1), 0.0)

    half = places.row[: planes // 2] , places.lane[: planes // 2]
    first_row = (half[0] & 1) == 0
    first_lane = (half[1] & 4) == 0

    def coarse(v):
        v = v.reshape(planes // 2, 2, *v.shape[1:])
        v = v[:, 0] + v[:, 1]
        v = v + jnp.where(first_row, ring(v, -1, 1), ring(v, 1, 1))
        return v + jnp.where(first_lane, ring(v, -4, 2), ring(v, 4, 2))

    remain = (1.0 / 256.0) * coarse(left)
    k3 = 0.125 * coarse(k2)
    places3 = Places(k3.shape)
    weights3, diagonal3 = whole_weights(k3, places3, 2)

    def total(v):
        return jnp.sum(jnp.sum(v, axis=0, keepdims=True), axis=(1, 2), keepdims=True)

    error = jnp.zeros_like(remain)
    direction = remain
    norm_now = total(remain * remain)
    for repeat in range(CSWEEPS):
        image = (diagonal3 * direction - whole_sum(direction, weights3, places3, 2)) * (1.0 / 128.0)
        alpha = norm_now / total(direction * image)
        error = error + alpha * direction
        if repeat == CSWEEPS - 1:
            break
        remain = remain - alpha * image
        norm_next = total(remain * remain)
        direction = remain + norm_next / norm_now * direction
        norm_now = norm_next

    lower = 0.75 * error + 0.25 * before_x(error)
    upper = 0.75 * error + 0.25 * after_x(error)
    fine = jnp.stack([lower, upper], 1).reshape(k2.shape)
    near = jnp.where(
        (places.row & 1) == 0,
        jnp.where(places.has_before_y(1), places.before_y(fine, 1), 0.0),
        jnp.where(places.has_after_y(1), places.after_y(fine, 1), 0.0),
    )
    fine = 0.75 * fine + 0.25 * near
    near = jnp.where(
        (places.lane & 4) == 0,
        jnp.where(places.has_before_z(1), ring(fine, 4, 2), 0.0),
        jnp.where(places.has_after_z(1), ring(fine, -4, 2), 0.0),
    )
    return error_two + (0.75 * fine + 0.25 * near)


def finish(grid, wide, smoothed, error_one, out, e1, e0):
    cells_x, cells_y, depth = smoothed.shape
    i, j = lax.axis_index("gx"), lax.axis_index("gy")
    first = 8 - 2
    count = cells_y + 8
    lane = lax.broadcasted_iota(jnp.int32, (count, depth), 1)
    row = lax.broadcasted_iota(jnp.int32, (count, depth), 0) - 2

    def widen_z(value, stride, lane):
        down = jnp.where(lane >= stride, pltpu.roll(value, stride, 1), 0.0)
        up = jnp.where(lane < depth - stride, pltpu.roll(value, depth - stride, 1), 0.0)
        return 0.75 * value + 0.25 * jnp.where((lane & stride) == 0, down, up)

    def widen_y(ref, index, first, count, stride, row):
        centre = ref[index, pl.ds(first, count), :]
        down = ref[index, pl.ds(first - stride, count), :]
        up = ref[index, pl.ds(first + stride, count), :]
        return 0.75 * centre + 0.25 * jnp.where((row & stride) == 0, down, up)

    low_row = jnp.where(j > 0, -cells_y, 0)
    high_row = jnp.where(j < grid[1] - 1, 2 * cells_y, cells_y)
    inside = (row >= low_row) & (row < high_row)
    planes_two = cells_x // 4 + 2
    mid = [widen_z(widen_y(wide, x, first, count, 2, row), 2, lane) for x in range(planes_two)]
    for x in range(cells_x // 2 + 2):
        centre = (x + 1) // 2
        near = centre + (1 if x % 2 == 0 else -1)
        value = jnp.where(inside, 0.75 * mid[centre] + 0.25 * mid[near], 0.0)
        if x == 0:
            value = jnp.where(i > 0, value, 0.0)
        if x == cells_x // 2 + 1:
            value = jnp.where(i < grid[0] - 1, value, 0.0)
        here = pl.ds(first, count)
        e1[x, here, :] = error_one[x, here, :] + value

    lane = lax.broadcasted_iota(jnp.int32, (cells_y, depth), 1)
    row = lax.broadcasted_iota(jnp.int32, (cells_y, depth), 0)
    for x in range(cells_x // 2 + 2):
        e0[x] = widen_z(widen_y(e1, x, 8, cells_y, 1, row), 1, lane)
    for x in range(cells_x):
        centre = x // 2 + 1
        near = centre + (-1 if x % 2 == 0 else 1)
        out[x] = smoothed[x] + (0.75 * e0[centre] + 0.25 * e0[near])


def correct_kernel(grid, gathered, smoothed, error_one, out, whole, strip, wide, e1, e0):
    cells_y = smoothed.shape[1]
    nx, ny = grid
    i, j = lax.axis_index("gx"), lax.axis_index("gy")
    lane = lax.broadcasted_iota(jnp.int32, (8, 128), 1) & 3
    fields = [[], []]
    for column in range(nx):
        parts = [gathered[column * ny + part] for part in range(ny)]
        for field in range(2):
            for x in range(2):
                place = 2 * field + x
                plane = None
                for part in range(ny):
                    turned = parts[part] if part == place else ring(parts[part], part - place, 1)
                    plane = turned if plane is None else jnp.where(lane == part, turned, plane)
                fields[field].append(plane)
    rhs2 = jnp.stack(fields[0], 0)
    k2 = jnp.stack(fields[1], 0)
    planes = 2 * nx
    whole[0] = jnp.zeros((8, 128), jnp.float32)
    whole[planes + 1] = jnp.zeros((8, 128), jnp.float32)
    whole[pl.ds(1, planes)] = whole_solve(k2, rhs2)

    for x in range(4):
        centre = pltpu.roll(whole[2 * i + x], lax.rem(128 - j, 128), 1)
        below = jnp.where(j > 0, ring(centre, 1, 1), 0.0)
        above = jnp.where(j < ny - 1, ring(centre, -1, 1), 0.0)
        for index, value in enumerate((below, centre, above)):
            value = jnp.where(lane == 0, value, 0.0)
            value = value + ring(value, 1, 1)
            strip[x, pl.ds(8 * index, 8), :] = value + ring(value, 2, 1)
        for place in range(4):
            wide[x, pl.ds(4 + place, 8, stride=4), :] = strip[x, pl.ds(7, 8), :]
            wide[x, pl.ds(36 + place, 2, stride=4), :] = strip[x, pl.ds(15, 2), :]
    finish(grid, wide, smoothed, error_one, out, e1, e0)


def finish_kernel(grid, wide, smoothed, error_one, out, e1, e0):
    finish(grid, wide, smoothed, error_one, out, e1, e0)


def last_scratch(cells_x, cells_y, depth):
    count = cells_x // 2 + 2
    return [
        pltpu.VMEM((count, cells_y + 16, depth), jnp.float32),
        pltpu.VMEM((count, cells_y, depth), jnp.float32),
    ]


def correct_whole(grid, tiles, smoothed, error_one):
    gathered = lax.all_to_all(tiles, ("gx", "gy"), 0, 0, tiled=False)
    cells_x, cells_y, depth = smoothed.shape
    return pl.pallas_call(
        functools.partial(correct_kernel, grid),
        out_shape=jax.ShapeDtypeStruct(smoothed.shape, jnp.float32),
        scratch_shapes=[
            pltpu.VMEM((2 * grid[0] + 2, 8, depth), jnp.float32),
            pltpu.VMEM((4, 24, depth), jnp.float32),
            pltpu.VMEM((4, cells_y + 16, depth), jnp.float32),
        ]
        + last_scratch(cells_x, cells_y, depth),
        compiler_params=pltpu.CompilerParams(vmem_limit_bytes=VMEM_LIMIT),
        name="correct",
    )(gathered, smoothed, error_one)


def with_faces(shard):
    for axis, dim in (("gx", 0), ("gy", 1)):
        length = shard.shape[dim]
        last = lax.slice_in_dim(shard, length - 1, length, axis=dim)
        initial = lax.slice_in_dim(shard, 0, 1, axis=dim)
        before = lax.ppermute(last, axis, shifts(axis, 1))
        after = lax.ppermute(initial, axis, shifts(axis, -1))
        shard = jnp.concatenate([before, shard, after], axis=dim)
    return shard


def with_zeros(field):
    return jnp.pad(field, ((1, 1), (1, 1), (0, 0)))


def pad_depth(field):
    return jnp.pad(field, ((0, 0), (0, 0), (1, 1)))


def restrict(field):
    size_x, size_y, size_z = field.shape
    return field.reshape(size_x // 2, 2, size_y // 2, 2, size_z // 2, 2).mean(axis=(1, 3, 5))


def level_weights(coef_pad):
    c = pad_depth(coef_pad)
    wx = (c[1:, 1:-1, 1:-1] + c[:-1, 1:-1, 1:-1]) * 0.5
    wy = (c[1:-1, 1:, 1:-1] + c[1:-1, :-1, 1:-1]) * 0.5
    wz = (c[1:-1, 1:-1, 1:] + c[1:-1, 1:-1, :-1]) * 0.5
    diagonal = wx[1:] + wx[:-1] + wy[:, 1:] + wy[:, :-1] + wz[:, :, 1:] + wz[:, :, :-1]
    return (wx, wy, wz), diagonal


def neighbour_sum(field_pad, weights):
    wx, wy, wz = weights
    v = pad_depth(field_pad)
    total = wx[:-1] * v[:-2, 1:-1, 1:-1] + wx[1:] * v[2:, 1:-1, 1:-1]
    total = total + wy[:, :-1] * v[1:-1, :-2, 1:-1] + wy[:, 1:] * v[1:-1, 2:, 1:-1]
    return total + wz[:, :, :-1] * v[1:-1, 1:-1, :-2] + wz[:, :, 1:] * v[1:-1, 1:-1, 2:]


def prolong_axis(padded, axis):
    length = padded.shape[axis]
    middle = lax.slice_in_dim(padded, 1, length - 1, axis=axis)
    before = lax.slice_in_dim(padded, 0, length - 2, axis=axis)
    after = lax.slice_in_dim(padded, 2, length, axis=axis)
    joined = jnp.stack([0.75 * middle + 0.25 * before, 0.75 * middle + 0.25 * after], axis=axis + 1)
    shape = list(middle.shape)
    shape[axis] = 2 * shape[axis]
    return joined.reshape(shape)


def coarse_solve(rhs, weights, diagonal):
    error = jnp.zeros_like(rhs)
    remain = rhs
    direction = rhs
    norm_now = jnp.sum(remain * remain)
    for _ in range(CSWEEPS):
        image = (diagonal * direction - neighbour_sum(with_zeros(direction), weights)) * 4.0**-3
        alpha = norm_now / jnp.sum(direction * image)
        error = error + alpha * direction
        remain = remain - alpha * image
        norm_next = jnp.sum(remain * remain)
        direction = remain + norm_next / norm_now * direction
        norm_now = norm_next
    return error


def correct_spread(grid, tiles, smoothed, error_one):
    cells_x, cells_y, depth = smoothed.shape
    shape2 = (cells_x // 4, cells_y // 4, depth // 4)
    own = tiles[0].reshape(shape2[1], shape2[2], 2, shape2[0]).transpose(2, 3, 0, 1)
    rhs2, k2 = own[0], own[1]
    weights, diagonal = level_weights(with_faces(k2))
    parity = sum(lax.broadcasted_iota(jnp.int32, shape2, d) for d in range(3)) % 2
    error_two = jnp.where(parity == 0, rhs2 * 16.0 / diagonal, 0.0)
    total = neighbour_sum(with_faces(error_two), weights)
    error_two = jnp.where(parity == 1, (rhs2 * 16.0 + total) / diagonal, error_two)
    total = neighbour_sum(with_faces(error_two), weights)
    rhs3 = restrict(rhs2 - (diagonal * error_two - total) * 4.0**-2)
    merged = jnp.stack([rhs3, restrict(k2)])
    merged = lax.all_gather(merged, "gx", axis=1, tiled=True)
    merged = lax.all_gather(merged, "gy", axis=2, tiled=True)
    weights3, diagonal3 = level_weights(with_zeros(merged[1]))
    error_three = coarse_solve(merged[0], weights3, diagonal3)
    start_x = lax.axis_index("gx") * rhs3.shape[0]
    start_y = lax.axis_index("gy") * rhs3.shape[1]
    window = lax.dynamic_slice(
        with_zeros(error_three),
        (start_x, start_y, jnp.int32(0)),
        (rhs3.shape[0] + 2, rhs3.shape[1] + 2, rhs3.shape[2]),
    )
    finer = pad_depth(window)
    for axis in range(3):
        finer = prolong_axis(finer, axis)
    wide = with_faces(error_two + finer)
    wide = jnp.repeat(jnp.repeat(wide, 4, axis=1), 4, axis=2)
    wide = jnp.pad(wide, ((0, 0), (4, 4), (0, 0)))
    return pl.pallas_call(
        functools.partial(finish_kernel, grid),
        out_shape=jax.ShapeDtypeStruct(smoothed.shape, jnp.float32),
        scratch_shapes=last_scratch(cells_x, cells_y, depth),
        compiler_params=pltpu.CompilerParams(vmem_limit_bytes=VMEM_LIMIT),
        name="finish",
    )(wide, smoothed, error_one)


def on_device(pressure, source, coefficient):
    grid = (lax.axis_size("gx"), lax.axis_size("gy"))
    _, cells_y, depth = pressure.shape
    fits = grid[1] == 4 and cells_y == 32 and depth == 128
    halo = fine_halo(pressure, source, coefficient)
    copies = grid[0] * grid[1] if fits else 1
    smoothed, error_one, tiles = smooth(copies, pressure, source, coefficient, halo)
    correct = correct_whole if fits else correct_spread
    return correct(grid, tiles, smoothed, error_one)


def solution(mesh):
    spec = P("gx", "gy", None)
    return jax.shard_map(on_device, mesh=mesh, in_specs=(spec, spec, spec), out_specs=spec, check_vma=False)
```

```python
import functools
import jax
import jax.numpy as jnp
from jax import lax
from jax.experimental import pallas as pl
from jax.experimental.pallas import tpu as pltpu
from jax.sharding import PartitionSpec as P

CSWEEPS = 4
REACH = 9
ORIGIN = 16
VMEM_LIMIT = 48 * 1024 * 1024


def y_rows(distance):
    return REACH if distance <= 2 else REACH + 2 - distance


def y_plan(cells_x):
    pieces = []
    start = 0
    for array in range(3):
        for plane in range(cells_x + 2 * REACH):
            x = plane - REACH
            distance = max(0, -x, x - cells_x + 1)
            if array == 1 and distance == REACH:
                continue
            rows = y_rows(distance)
            pieces.append((array, plane, start, rows))
            start += rows
    return pieces, -(-start // 8) * 8


def shifts(axis, step):
    count = lax.axis_size(axis)
    return [(i, i + step) for i in range(count) if 0 <= i + step < count]


def plane_source(array, plane, cells_x, own, low, high, low2, high2):
    x = plane - REACH
    far = 0 if array == 0 else 1
    if x < -cells_x:
        return low2, far
    if x < 0:
        return low, array * cells_x + cells_x + x
    if x < cells_x:
        return own[array], x
    if x < 2 * cells_x:
        return high, array * cells_x + x - cells_x
    return high2, far


def pack_kernel(p, f, k, low, high, low2, high2, to_up, to_down):
    cells_x, cells_y, _ = p.shape
    pieces, _ = y_plan(cells_x)
    for array, plane, start, rows in pieces:
        ref, index = plane_source(array, plane, cells_x, (p, f, k), low, high, low2, high2)
        to_up[pl.ds(start, rows), :] = ref[index, pl.ds(cells_y - rows, rows), :]
        to_down[pl.ds(start, rows), :] = ref[index, pl.ds(0, rows), :]


def fine_halo(pressure, source, coefficient):
    cells_x, _, depth = pressure.shape
    block = jnp.concatenate([pressure, source, coefficient], 0)
    far_up = jnp.concatenate([pressure[-1:], coefficient[-1:]], 0)
    far_down = jnp.concatenate([pressure[:1], coefficient[:1]], 0)
    low = lax.ppermute(block, "gx", shifts("gx", 1))
    high = lax.ppermute(block, "gx", shifts("gx", -1))
    low2 = lax.ppermute(far_up, "gx", shifts("gx", 2))
    high2 = lax.ppermute(far_down, "gx", shifts("gx", -2))
    _, length = y_plan(cells_x)
    packed = jax.ShapeDtypeStruct((length, depth), jnp.float32)
    to_up, to_down = pl.pallas_call(
        pack_kernel,
        out_shape=(packed, packed),
        compiler_params=pltpu.CompilerParams(vmem_limit_bytes=VMEM_LIMIT),
        name="pack_halo",
    )(pressure, source, coefficient, low, high, low2, high2)
    below = lax.ppermute(to_up, "gy", shifts("gy", 1))
    above = lax.ppermute(to_down, "gy", shifts("gy", -1))
    return low, high, low2, high2, below, above


def smooth_kernel(
    p, f, k, low, high, low2, high2, below, above,
    out, error_one, tiles,
    vp, vf, vk, wx, wy, zl, zh, dg, inv, va, vb,
    t0, t1, f1, k1, inv1, g1, h1, q2,
):
    cells_x, cells_y, depth = p.shape
    planes = cells_x + 2 * REACH
    own_rows = pl.ds(ORIGIN, cells_y)
    top = ORIGIN - REACH + 1
    rows = cells_y + 2 * (REACH - 1)
    body = pl.ds(top, rows)

    for array, window in ((0, vp), (1, vf), (2, vk)):
        for plane in range(planes):
            if array == 1 and plane in (0, planes - 1):
                continue
            ref, index = plane_source(array, plane, cells_x, (p, f, k), low, high, low2, high2)
            value = ref[index]
            window[plane, own_rows, :] = value + value if array == 1 else value
    pieces, _ = y_plan(cells_x)
    for array, plane, start, count in pieces:
        window = (vp, vf, vk)[array]
        before = below[pl.ds(start, count), :]
        after = above[pl.ds(start, count), :]
        if array == 1:
            before = before + before
            after = after + after
        window[plane, pl.ds(ORIGIN - count, count), :] = before
        window[plane, pl.ds(ORIGIN + cells_y, count), :] = after

    def lanes(count):
        return lax.broadcasted_iota(jnp.int32, (count, depth), 1)

    def rows_of(first, count):
        return lax.broadcasted_iota(jnp.int32, (count, depth), 0) + (first - ORIGIN)

    lane = lanes(rows)

    def weigh(plane, _):
        centre = vk[plane, body, :]
        west = centre + vk[plane - 1, body, :]
        wx[plane, body, :] = west
        east = centre + vk[plane + 1, body, :]
        south = centre + vk[plane, pl.ds(top - 1, rows), :]
        north = centre + vk[plane, pl.ds(top + 1, rows), :]
        wy[plane, body, :] = south
        wy[plane, pl.ds(top + rows, 1), :] = north[rows - 1:, :]
        down = jnp.where(lane > 0, pltpu.roll(centre, 1, 1), 0.0)
        up = jnp.where(lane < depth - 1, pltpu.roll(centre, depth - 1, 1), 0.0)
        total = west + east + south + north + (centre + down) + (centre + up)
        zl[plane, body, :] = jnp.where(lane > 0, centre + down, 0.0)
        zh[plane, body, :] = jnp.where(lane < depth - 1, centre + up, 0.0)
        dg[plane, body, :] = total
        inside = centre > 0.0
        inv[plane, body, :] = jnp.where(inside, 1.0 / jnp.where(inside, total, 1.0), 0.0)
        return 0

    lax.fori_loop(1, planes - 1, weigh, 0, unroll=True)
    wx[planes - 1, body, :] = vk[planes - 1, body, :] + vk[planes - 2, body, :]

    def stencil(v, plane, first, count):
        here = pl.ds(first, count)
        centre = v[plane, here, :]
        total = wx[plane, here, :] * v[plane - 1, here, :] + wx[plane + 1, here, :] * v[plane + 1, here, :]
        total += wy[plane, here, :] * v[plane, pl.ds(first - 1, count), :]
        total += wy[plane, pl.ds(first + 1, count), :] * v[plane, pl.ds(first + 1, count), :]
        total += zl[plane, here, :] * pltpu.roll(centre, 1, 1)
        total += zh[plane, here, :] * pltpu.roll(centre, depth - 1, 1)
        return total

    def relax(source_ref, target, reach):
        def one(plane, _):
            total = stencil(source_ref, plane, top, rows)
            target[plane, body, :] = inv[plane, body, :] * (vf[plane, body, :] + total)
            return 0

        lax.fori_loop(REACH - reach, REACH + cells_x + reach, one, 0, unroll=True)

    relax(vp, va, REACH - 1)
    relax(va, vb, REACH - 2)
    relax(vb, va, REACH - 3)
    relax(va, vb, REACH - 4)

    own_lane = lanes(cells_y)
    own_row = rows_of(ORIGIN, cells_y)
    for x in range(cells_x):
        even = ((own_row + own_lane + x) & 1) == 0
        out[x] = jnp.where(even, va[REACH + x, own_rows, :], vb[REACH + x, own_rows, :])

    planes_one = cells_x // 2
    first = ORIGIN - 4
    count = cells_y + 8
    lane = lanes(count)
    row = rows_of(first, count)

    def pair_lane(value, stride, lane):
        up = pltpu.roll(value, depth - stride, 1)
        down = pltpu.roll(value, stride, 1)
        return value + jnp.where((lane & stride) == 0, up, down)

    def pair_row(ref, index, first, count, stride, row):
        centre = ref[index, pl.ds(first, count), :]
        up = ref[index, pl.ds(first + stride, count), :]
        down = ref[index, pl.ds(first - stride, count), :]
        return centre + jnp.where((row & stride) == 0, up, down)

    def residual(plane_one, _):
        total = jnp.zeros((count, depth), jnp.float32)
        for half in range(2):
            plane = 2 * plane_one + REACH - 4 + half
            here = pl.ds(first, count)
            twice = vf[plane, here, :] - dg[plane, here, :] * va[plane, here, :] + stencil(vb, plane, first, count)
            even = ((row + lane + half) & 1) == 0
            total += jnp.where(even, twice, 0.0)
        t0[plane_one, pl.ds(first, count), :] = pair_lane(total, 1, lane)
        return 0

    lax.fori_loop(0, planes_one + 4, residual, 0, unroll=True)
    for x in range(planes_one + 4):
        f1[x, pl.ds(first, count), :] = 0.5 * pair_row(t0, x, first, count, 1, row)

    first_k = ORIGIN - 6
    count_k = cells_y + 16
    lane_k = lanes(count_k)
    row_k = rows_of(first_k, count_k)
    for x in range(planes_one + 6):
        plane = 2 * x + REACH - 6
        here = pl.ds(first_k, count_k)
        t1[x, here, :] = pair_lane(vk[plane, here, :] + vk[plane + 1, here, :], 1, lane_k)
    for x in range(planes_one + 6):
        k1[x, pl.ds(first_k, count_k), :] = 0.125 * pair_row(t1, x, first_k, count_k, 1, row_k)

    def down2(value, lane):
        return jnp.where(lane >= 2, pltpu.roll(value, 2, 1), 0.0)

    def up2(value, lane):
        return jnp.where(lane < depth - 2, pltpu.roll(value, depth - 2, 1), 0.0)

    here = pl.ds(first, count)
    for x in range(planes_one + 4):
        centre = k1[x + 1, here, :]
        total = 6.0 * centre + (k1[x, here, :] + k1[x + 2, here, :])
        total += k1[x + 1, pl.ds(first - 2, count), :] + k1[x + 1, pl.ds(first + 2, count), :]
        total += down2(centre, lane) + up2(centre, lane)
        inside = centre > 0.0
        inverse = jnp.where(inside, 1.0 / jnp.where(inside, total, 1.0), 0.0)
        inv1[x, here, :] = inverse
        g1[x, here, :] = inverse * f1[x, here, :]

    def stencil_one(v, x, v_x, first, count, lane):
        here = pl.ds(first, count)
        south = pl.ds(first - 2, count)
        north = pl.ds(first + 2, count)
        kc = k1[x, here, :]
        vc = v[v_x, here, :]
        total = (kc + k1[x - 1, here, :]) * v[v_x - 1, here, :] + (kc + k1[x + 1, here, :]) * v[v_x + 1, here, :]
        total += (kc + k1[x, south, :]) * v[v_x, south, :] + (kc + k1[x, north, :]) * v[v_x, north, :]
        total += (kc + down2(kc, lane)) * down2(vc, lane) + (kc + up2(kc, lane)) * up2(vc, lane)
        return total

    first_h = ORIGIN - 2
    count_h = cells_y + 8
    lane_h = lanes(count_h)
    row_h = rows_of(first_h, count_h)
    for x in range(planes_one + 2):
        here = pl.ds(first_h, count_h)
        total = stencil_one(g1, x + 2, x + 1, first_h, count_h, lane_h)
        odd = inv1[x + 1, here, :] * (f1[x + 1, here, :] + total)
        h1[x, here, :] = odd
        even_cell = ((x - 1 + (row_h >> 1) + (lane_h >> 1)) & 1) == 0
        error_one[x, pl.ds(first_h - 8, count_h), :] = jnp.where(even_cell, g1[x + 1, here, :], odd)

    own2 = own_lane
    row2 = own_row
    for x in range(planes_one // 2):
        sum_r = jnp.zeros((cells_y, depth), jnp.float32)
        for half in range(2):
            x1 = 2 * x + half
            total = stencil_one(h1, x1 + 3, x1 + 1, ORIGIN, cells_y, own2)
            even_cell = ((x1 + (row2 >> 1) + (own2 >> 1)) & 1) == 0
            sum_r += jnp.where(even_cell, total, 0.0)
        sum_k = k1[2 * x + 3, own_rows, :] + k1[2 * x + 4, own_rows, :]
        t0[x, own_rows, :] = pair_lane(sum_r, 2, own2)
        t1[x, own_rows, :] = pair_lane(sum_k, 2, own2)
    lane8 = lanes(cells_y // 4)
    tile = jnp.zeros((cells_y // 4, depth), jnp.float32)
    for x in range(planes_one // 2):
        q2[0] = (1.0 / 64.0) * pair_row(t0, x, ORIGIN, cells_y, 2, row2)
        q2[1] = 0.125 * pair_row(t1, x, ORIGIN, cells_y, 2, row2)
        for field in range(2):
            kept = q2[field, pl.ds(0, cells_y // 4, stride=4), :]
            tile = jnp.where((lane8 & 3) == 2 * field + x, kept, tile)
    tiles[...] = jnp.broadcast_to(tile[None], tiles.shape)


def smooth(copies, pressure, source, coefficient, halo):
    cells_x, cells_y, depth = pressure.shape
    planes = cells_x + 2 * REACH
    tall = cells_y + 2 * ORIGIN
    planes_one = cells_x // 2
    window = pltpu.VMEM((planes, tall, depth), jnp.float32)

    def level_one(count):
        return pltpu.VMEM((count, tall, depth), jnp.float32)

    return pl.pallas_call(
        smooth_kernel,
        out_shape=(
            jax.ShapeDtypeStruct((cells_x, cells_y, depth), jnp.float32),
            jax.ShapeDtypeStruct((planes_one + 2, cells_y + 16, depth), jnp.float32),
            jax.ShapeDtypeStruct((copies, cells_y // 4, depth), jnp.float32),
        ),
        scratch_shapes=[window] * 11
        + [
            level_one(planes_one + 4),
            level_one(planes_one + 6),
            level_one(planes_one + 4),
            level_one(planes_one + 6),
            level_one(planes_one + 4),
            level_one(planes_one + 4),
            level_one(planes_one + 2),
            pltpu.VMEM((2, cells_y, depth), jnp.float32),
        ],
        compiler_params=pltpu.CompilerParams(vmem_limit_bytes=VMEM_LIMIT),
        name="smooth",
    )(pressure, source, coefficient, *halo)


def ring(value, shift, axis):
    return pltpu.roll(value, shift % value.shape[axis], axis)


def before_x(v):
    return jnp.concatenate([jnp.zeros_like(v[:1]), v[:-1]], 0)


def after_x(v):
    return jnp.concatenate([v[1:], jnp.zeros_like(v[:1])], 0)


class Places:
    def __init__(self, shape):
        self.row = lax.broadcasted_iota(jnp.int32, shape, 1)
        self.lane = lax.broadcasted_iota(jnp.int32, shape, 2)
        self.part = self.lane & 3
        self.depth = shape[2]

    def before_y(self, v, stride):
        turned = ring(v, stride, 1)
        return jnp.where(self.row >= stride, turned, ring(turned, 1, 2))

    def after_y(self, v, stride):
        turned = ring(v, -stride, 1)
        return jnp.where(self.row < 8 - stride, turned, ring(turned, -1, 2))

    def has_before_y(self, stride):
        return (self.row >= stride) | (self.part > 0)

    def has_after_y(self, stride):
        return (self.row < 8 - stride) | (self.part < 3)

    def has_before_z(self, stride):
        return self.lane >= 4 * stride

    def has_after_z(self, stride):
        return self.lane < self.depth - 4 * stride


def whole_weights(k, places, stride):
    west = k + before_x(k)
    east = k + after_x(k)
    masks = (
        places.has_before_y(stride),
        places.has_after_y(stride),
        places.has_before_z(stride),
        places.has_after_z(stride),
    )
    near = (
        places.before_y(k, stride),
        places.after_y(k, stride),
        ring(k, 4 * stride, 2),
        ring(k, -4 * stride, 2),
    )
    diagonal = west + east
    weights = [west, east]
    for mask, value in zip(masks, near):
        diagonal += k + jnp.where(mask, value, 0.0)
        weights.append(jnp.where(mask, k + value, 0.0))
    return weights, diagonal


def whole_sum(v, weights, places, stride):
    total = weights[0] * before_x(v) + weights[1] * after_x(v)
    total += weights[2] * places.before_y(v, stride) + weights[3] * places.after_y(v, stride)
    total += weights[4] * ring(v, 4 * stride, 2) + weights[5] * ring(v, -4 * stride, 2)
    return total


def whole_solve(k2, rhs2):
    planes = k2.shape[0]
    places = Places(k2.shape)
    weights, diagonal = whole_weights(k2, places, 1)
    parity = lax.broadcasted_iota(jnp.int32, k2.shape, 0) + places.row + (places.lane >> 2)
    even = (parity & 1) == 0
    inverse = 1.0 / diagonal
    scaled = 32.0 * rhs2
    even_values = inverse * scaled
    odd_values = inverse * (scaled + whole_sum(even_values, weights, places, 1))
    error_two = jnp.where(even, even_values, odd_values)
    left = jnp.where(even, whole_sum(odd_values, weights, places, 1), 0.0)

    half = places.row[: planes // 2] , places.lane[: planes // 2]
    first_row = (half[0] & 1) == 0
    first_lane = (half[1] & 4) == 0

    def coarse(v):
        v = v.reshape(planes // 2, 2, *v.shape[1:])
        v = v[:, 0] + v[:, 1]
        v = v + jnp.where(first_row, ring(v, -1, 1), ring(v, 1, 1))
        return v + jnp.where(first_lane, ring(v, -4, 2), ring(v, 4, 2))

    remain = (1.0 / 256.0) * coarse(left)
    k3 = 0.125 * coarse(k2)
    places3 = Places(k3.shape)
    weights3, diagonal3 = whole_weights(k3, places3, 2)

    def total(v):
        return jnp.sum(jnp.sum(v, axis=0, keepdims=True), axis=(1, 2), keepdims=True)

    error = jnp.zeros_like(remain)
    direction = remain
    norm_now = total(remain * remain)
    for repeat in range(CSWEEPS):
        image = (diagonal3 * direction - whole_sum(direction, weights3, places3, 2)) * (1.0 / 128.0)
        alpha = norm_now / total(direction * image)
        error = error + alpha * direction
        if repeat == CSWEEPS - 1:
            break
        remain = remain - alpha * image
        norm_next = total(remain * remain)
        direction = remain + norm_next / norm_now * direction
        norm_now = norm_next

    lower = 0.75 * error + 0.25 * before_x(error)
    upper = 0.75 * error + 0.25 * after_x(error)
    fine = jnp.stack([lower, upper], 1).reshape(k2.shape)
    near = jnp.where(
        (places.row & 1) == 0,
        jnp.where(places.has_before_y(1), places.before_y(fine, 1), 0.0),
        jnp.where(places.has_after_y(1), places.after_y(fine, 1), 0.0),
    )
    fine = 0.75 * fine + 0.25 * near
    near = jnp.where(
        (places.lane & 4) == 0,
        jnp.where(places.has_before_z(1), ring(fine, 4, 2), 0.0),
        jnp.where(places.has_after_z(1), ring(fine, -4, 2), 0.0),
    )
    return error_two + (0.75 * fine + 0.25 * near)


def finish(grid, wide, smoothed, error_one, out, e1, e0):
    cells_x, cells_y, depth = smoothed.shape
    i, j = lax.axis_index("gx"), lax.axis_index("gy")
    first = 8 - 2
    count = cells_y + 8
    lane = lax.broadcasted_iota(jnp.int32, (count, depth), 1)
    row = lax.broadcasted_iota(jnp.int32, (count, depth), 0) - 2

    def widen_z(value, stride, lane):
        down = jnp.where(lane >= stride, pltpu.roll(value, stride, 1), 0.0)
        up = jnp.where(lane < depth - stride, pltpu.roll(value, depth - stride, 1), 0.0)
        return 0.75 * value + 0.25 * jnp.where((lane & stride) == 0, down, up)

    def widen_y(ref, index, first, count, stride, row):
        centre = ref[index, pl.ds(first, count), :]
        down = ref[index, pl.ds(first - stride, count), :]
        up = ref[index, pl.ds(first + stride, count), :]
        return 0.75 * centre + 0.25 * jnp.where((row & stride) == 0, down, up)

    low_row = jnp.where(j > 0, -cells_y, 0)
    high_row = jnp.where(j < grid[1] - 1, 2 * cells_y, cells_y)
    inside = (row >= low_row) & (row < high_row)
    planes_two = cells_x // 4 + 2
    mid = [widen_z(widen_y(wide, x, first, count, 2, row), 2, lane) for x in range(planes_two)]
    for x in range(cells_x // 2 + 2):
        centre = (x + 1) // 2
        near = centre + (1 if x % 2 == 0 else -1)
        value = jnp.where(inside, 0.75 * mid[centre] + 0.25 * mid[near], 0.0)
        if x == 0:
            value = jnp.where(i > 0, value, 0.0)
        if x == cells_x // 2 + 1:
            value = jnp.where(i < grid[0] - 1, value, 0.0)
        here = pl.ds(first, count)
        e1[x, here, :] = error_one[x, here, :] + value

    lane = lax.broadcasted_iota(jnp.int32, (cells_y, depth), 1)
    row = lax.broadcasted_iota(jnp.int32, (cells_y, depth), 0)
    for x in range(cells_x // 2 + 2):
        e0[x] = widen_z(widen_y(e1, x, 8, cells_y, 1, row), 1, lane)
    for x in range(cells_x):
        centre = x // 2 + 1
        near = centre + (-1 if x % 2 == 0 else 1)
        out[x] = smoothed[x] + (0.75 * e0[centre] + 0.25 * e0[near])


def correct_kernel(grid, gathered, smoothed, error_one, out, whole, strip, wide, e1, e0):
    cells_y = smoothed.shape[1]
    nx, ny = grid
    i, j = lax.axis_index("gx"), lax.axis_index("gy")
    lane = lax.broadcasted_iota(jnp.int32, (8, 128), 1) & 3
    fields = [[], []]
    for column in range(nx):
        parts = [gathered[column * ny + part] for part in range(ny)]
        for field in range(2):
            for x in range(2):
                place = 2 * field + x
                plane = None
                for part in range(ny):
                    turned = parts[part] if part == place else ring(parts[part], part - place, 1)
                    plane = turned if plane is None else jnp.where(lane == part, turned, plane)
                fields[field].append(plane)
    rhs2 = jnp.stack(fields[0], 0)
    k2 = jnp.stack(fields[1], 0)
    planes = 2 * nx
    whole[0] = jnp.zeros((8, 128), jnp.float32)
    whole[planes + 1] = jnp.zeros((8, 128), jnp.float32)
    whole[pl.ds(1, planes)] = whole_solve(k2, rhs2)

    for x in range(4):
        centre = pltpu.roll(whole[2 * i + x], lax.rem(128 - j, 128), 1)
        below = jnp.where(j > 0, ring(centre, 1, 1), 0.0)
        above = jnp.where(j < ny - 1, ring(centre, -1, 1), 0.0)
        for index, value in enumerate((below, centre, above)):
            value = jnp.where(lane == 0, value, 0.0)
            value = value + ring(value, 1, 1)
            strip[x, pl.ds(8 * index, 8), :] = value + ring(value, 2, 1)
        for place in range(4):
            wide[x, pl.ds(4 + place, 8, stride=4), :] = strip[x, pl.ds(7, 8), :]
            wide[x, pl.ds(36 + place, 2, stride=4), :] = strip[x, pl.ds(15, 2), :]
    finish(grid, wide, smoothed, error_one, out, e1, e0)


def finish_kernel(grid, wide, smoothed, error_one, out, e1, e0):
    finish(grid, wide, smoothed, error_one, out, e1, e0)


def last_scratch(cells_x, cells_y, depth):
    count = cells_x // 2 + 2
    return [
        pltpu.VMEM((count, cells_y + 16, depth), jnp.float32),
        pltpu.VMEM((count, cells_y, depth), jnp.float32),
    ]


def correct_whole(grid, tiles, smoothed, error_one):
    gathered = lax.all_to_all(tiles, ("gx", "gy"), 0, 0, tiled=False)
    cells_x, cells_y, depth = smoothed.shape
    return pl.pallas_call(
        functools.partial(correct_kernel, grid),
        out_shape=jax.ShapeDtypeStruct(smoothed.shape, jnp.float32),
        scratch_shapes=[
            pltpu.VMEM((2 * grid[0] + 2, 8, depth), jnp.float32),
            pltpu.VMEM((4, 24, depth), jnp.float32),
            pltpu.VMEM((4, cells_y + 16, depth), jnp.float32),
        ]
        + last_scratch(cells_x, cells_y, depth),
        compiler_params=pltpu.CompilerParams(vmem_limit_bytes=VMEM_LIMIT),
        name="correct",
    )(gathered, smoothed, error_one)


def with_faces(shard):
    for axis, dim in (("gx", 0), ("gy", 1)):
        length = shard.shape[dim]
        last = lax.slice_in_dim(shard, length - 1, length, axis=dim)
        initial = lax.slice_in_dim(shard, 0, 1, axis=dim)
        before = lax.ppermute(last, axis, shifts(axis, 1))
        after = lax.ppermute(initial, axis, shifts(axis, -1))
        shard = jnp.concatenate([before, shard, after], axis=dim)
    return shard


def with_zeros(field):
    return jnp.pad(field, ((1, 1), (1, 1), (0, 0)))


def pad_depth(field):
    return jnp.pad(field, ((0, 0), (0, 0), (1, 1)))


def restrict(field):
    size_x, size_y, size_z = field.shape
    return field.reshape(size_x // 2, 2, size_y // 2, 2, size_z // 2, 2).mean(axis=(1, 3, 5))


def level_weights(coef_pad):
    c = pad_depth(coef_pad)
    wx = (c[1:, 1:-1, 1:-1] + c[:-1, 1:-1, 1:-1]) * 0.5
    wy = (c[1:-1, 1:, 1:-1] + c[1:-1, :-1, 1:-1]) * 0.5
    wz = (c[1:-1, 1:-1, 1:] + c[1:-1, 1:-1, :-1]) * 0.5
    diagonal = wx[1:] + wx[:-1] + wy[:, 1:] + wy[:, :-1] + wz[:, :, 1:] + wz[:, :, :-1]
    return (wx, wy, wz), diagonal


def neighbour_sum(field_pad, weights):
    wx, wy, wz = weights
    v = pad_depth(field_pad)
    total = wx[:-1] * v[:-2, 1:-1, 1:-1] + wx[1:] * v[2:, 1:-1, 1:-1]
    total = total + wy[:, :-1] * v[1:-1, :-2, 1:-1] + wy[:, 1:] * v[1:-1, 2:, 1:-1]
    return total + wz[:, :, :-1] * v[1:-1, 1:-1, :-2] + wz[:, :, 1:] * v[1:-1, 1:-1, 2:]


def prolong_axis(padded, axis):
    length = padded.shape[axis]
    middle = lax.slice_in_dim(padded, 1, length - 1, axis=axis)
    before = lax.slice_in_dim(padded, 0, length - 2, axis=axis)
    after = lax.slice_in_dim(padded, 2, length, axis=axis)
    joined = jnp.stack([0.75 * middle + 0.25 * before, 0.75 * middle + 0.25 * after], axis=axis + 1)
    shape = list(middle.shape)
    shape[axis] = 2 * shape[axis]
    return joined.reshape(shape)


def coarse_solve(rhs, weights, diagonal):
    error = jnp.zeros_like(rhs)
    remain = rhs
    direction = rhs
    norm_now = jnp.sum(remain * remain)
    for _ in range(CSWEEPS):
        image = (diagonal * direction - neighbour_sum(with_zeros(direction), weights)) * 4.0**-3
        alpha = norm_now / jnp.sum(direction * image)
        error = error + alpha * direction
        remain = remain - alpha * image
        norm_next = jnp.sum(remain * remain)
        direction = remain + norm_next / norm_now * direction
        norm_now = norm_next
    return error


def correct_spread(grid, tiles, smoothed, error_one):
    cells_x, cells_y, depth = smoothed.shape
    shape2 = (cells_x // 4, cells_y // 4, depth // 4)
    own = tiles[0].reshape(shape2[1], shape2[2], 2, shape2[0]).transpose(2, 3, 0, 1)
    rhs2, k2 = own[0], own[1]
    weights, diagonal = level_weights(with_faces(k2))
    parity = sum(lax.broadcasted_iota(jnp.int32, shape2, d) for d in range(3)) % 2
    error_two = jnp.where(parity == 0, rhs2 * 16.0 / diagonal, 0.0)
    total = neighbour_sum(with_faces(error_two), weights)
    error_two = jnp.where(parity == 1, (rhs2 * 16.0 + total) / diagonal, error_two)
    total = neighbour_sum(with_faces(error_two), weights)
    rhs3 = restrict(rhs2 - (diagonal * error_two - total) * 4.0**-2)
    merged = jnp.stack([rhs3, restrict(k2)])
    merged = lax.all_gather(merged, "gx", axis=1, tiled=True)
    merged = lax.all_gather(merged, "gy", axis=2, tiled=True)
    weights3, diagonal3 = level_weights(with_zeros(merged[1]))
    error_three = coarse_solve(merged[0], weights3, diagonal3)
    start_x = lax.axis_index("gx") * rhs3.shape[0]
    start_y = lax.axis_index("gy") * rhs3.shape[1]
    window = lax.dynamic_slice(
        with_zeros(error_three),
        (start_x, start_y, jnp.int32(0)),
        (rhs3.shape[0] + 2, rhs3.shape[1] + 2, rhs3.shape[2]),
    )
    finer = pad_depth(window)
    for axis in range(3):
        finer = prolong_axis(finer, axis)
    wide = with_faces(error_two + finer)
    wide = jnp.repeat(jnp.repeat(wide, 4, axis=1), 4, axis=2)
    wide = jnp.pad(wide, ((0, 0), (4, 4), (0, 0)))
    return pl.pallas_call(
        functools.partial(finish_kernel, grid),
        out_shape=jax.ShapeDtypeStruct(smoothed.shape, jnp.float32),
        scratch_shapes=last_scratch(cells_x, cells_y, depth),
        compiler_params=pltpu.CompilerParams(vmem_limit_bytes=VMEM_LIMIT),
        name="finish",
    )(wide, smoothed, error_one)


def on_device(pressure, source, coefficient):
    grid = (lax.axis_size("gx"), lax.axis_size("gy"))
    _, cells_y, depth = pressure.shape
    fits = grid[1] == 4 and cells_y == 32 and depth == 128
    halo = fine_halo(pressure, source, coefficient)
    copies = grid[0] * grid[1] if fits else 1
    smoothed, error_one, tiles = smooth(copies, pressure, source, coefficient, halo)
    correct = correct_whole if fits else correct_spread
    return correct(grid, tiles, smoothed, error_one)


def solution(mesh):
    spec = P("gx", "gy", None)
    return jax.shard_map(on_device, mesh=mesh, in_specs=(spec, spec, spec), out_specs=spec, check_vma=False)
```

```python
import functools
import jax
import jax.numpy as jnp
from jax import lax
from jax.experimental import pallas as pl
from jax.experimental.pallas import tpu as pltpu
from jax.sharding import PartitionSpec as P

CSWEEPS = 4
REACH = 9
ORIGIN = 16
VMEM_LIMIT = 48 * 1024 * 1024


def y_rows(distance):
    return REACH if distance <= 2 else REACH + 2 - distance


def side_entries():
    pairs = [(0, d, (d, d + 1)) for d in range(1, REACH - 1, 2)] + [(0, REACH, (REACH,))]
    return pairs + [(1, d, (d,)) for d in range(1, REACH)] + [(2, d, (d,)) for d in range(1, REACH + 1)]


def x_plan(cells_y):
    first, second = {}, {}
    lengths = [0, 0]

    def put(message, plan, key, row, rows):
        plan.setdefault(key, []).append((row, rows, lengths[message]))
        lengths[message] += rows

    for array, distance, _ in side_entries():
        key = (array, distance)
        ends = y_rows(distance)
        if array != 1 and distance in (1, REACH):
            put(0, first, key, 0, cells_y)
        else:
            put(0, first, key, 0, ends)
            put(0, first, key, cells_y - ends, ends)
            put(1, second, key, ends, cells_y - 2 * ends)
    return first, second, [-(-length // 8) * 8 for length in lengths]


def y_plan(cells_x):
    pieces = []
    start = 0
    inside = [(0, m) for m in range(cells_x)] + [(a, x) for a in (1, 2) for x in range(2 * cells_x)]
    chosen = [("inside", array, index, REACH) for array, index in inside]
    for side in ("low", "high"):
        chosen += [(side, array, distance, y_rows(distance)) for array, distance, _ in side_entries()]
    for side, array, index, rows in chosen:
        pieces.append((side, array, index, rows, start))
        start += rows
    return pieces, -(-start // 8) * 8


def shifts(axis, step):
    count = lax.axis_size(axis)
    return [(i, i + step) for i in range(count) if 0 <= i + step < count]


def swap_pairs():
    return [(i, i ^ 1) for i in range(lax.axis_size("gx"))]


def x_pairs():
    count = lax.axis_size("gx")
    pairs = [(i, i + 1) for i in range(1, count - 1, 2)]
    return pairs + [(j, i) for i, j in pairs]


def y_pairs():
    nx, ny = lax.axis_size("gx"), lax.axis_size("gy")
    pairs = [((i + 1) * ny + j, i * ny + j + 1) for i in range(0, nx, 2) for j in range(ny - 1)]
    return pairs + [(j, i) for i, j in pairs]


def inside_rows(member, own, partner, array, index, first, rows):
    cells_x = own[0].shape[0]
    here = pl.ds(first, rows)

    def plane(x):
        if x // cells_x == member:
            return own[array][x % cells_x, here, :]
        value = partner[array][x % cells_x, here, :]
        return value + value if array == 1 else value

    if array != 0:
        return plane(index)
    depth = own[0].shape[2]
    row = lax.broadcasted_iota(jnp.int32, (rows, depth), 0) + first
    lane = lax.broadcasted_iota(jnp.int32, (rows, depth), 1)
    return jnp.where(((row + lane) & 1) == 1, plane(2 * index), plane(2 * index + 1))


def for_member(body):
    me = lax.axis_index("gx") & 1
    for member in range(2):
        pl.when(me == member)(functools.partial(body, member))


def split_kernel(block, pp, pf, pk, first, second):
    cells_x, cells_y, _ = pp.shape
    p, f, k = views(block, cells_x)
    plans = x_plan(cells_y)

    def body(member):
        for plan, target in zip(plans, (first, second)):
            for (array, distance), pieces in plan.items():
                plane = 2 * cells_x - distance if member == 1 else distance - 1
                index = plane // 2 if array == 0 else plane
                for row, rows, start in pieces:
                    value = inside_rows(member, (p, f, k), (pp, pf, pk), array, index, row, rows)
                    target[pl.ds(start, rows), :] = value

    for_member(body)


def pack_kernel(block, pp, pf, pk, received, passed, message):
    cells_x, cells_y, _ = pp.shape
    p, f, k = views(block, cells_x)
    plan = x_plan(cells_y)[0]

    def body(member):
        sides = {"low": (received, passed)[member], "high": (passed, received)[member]}
        for side, array, index, rows, start in y_plan(cells_x)[0]:
            row = cells_y - rows if member == 1 else 0
            if side == "inside":
                value = inside_rows(member, (p, f, k), (pp, pf, pk), array, index, row, rows)
            else:
                place = [s + row - r for r, count, s in plan[array, index] if r <= row and row + rows <= r + count][0]
                value = sides[side][pl.ds(place, rows), :]
            message[pl.ds(start, rows), :] = value

    for_member(body)


def stacked(pressure, source, coefficient):
    block = jnp.concatenate([pressure, source, coefficient], 0)
    cells_x = pressure.shape[0]
    plane = lax.broadcasted_iota(jnp.int32, block.shape, 0)
    return block * jnp.where((plane >= cells_x) & (plane < 2 * cells_x), 2.0, 1.0)


def views(block, cells_x):
    return tuple(block.at[pl.ds(n * cells_x, cells_x)] for n in range(3))


def fine_halo(own, block):
    cells_x, cells_y, depth = own[0].shape
    params = pltpu.CompilerParams(vmem_limit_bytes=VMEM_LIMIT)

    def packed(length):
        return jax.ShapeDtypeStruct((length, depth), jnp.float32)

    partner = tuple(lax.ppermute(v, "gx", swap_pairs()) for v in own)
    lengths = x_plan(cells_y)[2]
    first, second = pl.pallas_call(
        split_kernel, out_shape=[packed(n) for n in lengths], compiler_params=params, name="split_block"
    )(block, *partner)
    received = lax.ppermute(first, "gx", x_pairs())
    passed = lax.ppermute(received, "gx", swap_pairs())
    message = pl.pallas_call(
        pack_kernel, out_shape=packed(y_plan(cells_x)[1]), compiler_params=params, name="pack_halo"
    )(block, *partner, received, passed)
    second, message = lax.optimization_barrier((second, message))
    along_y = lax.ppermute(message, ("gx", "gy"), y_pairs())
    rest = lax.ppermute(second, "gx", x_pairs())
    along_y, rest = lax.optimization_barrier((along_y, rest))
    other_y = lax.ppermute(along_y, "gx", swap_pairs())
    return *partner, received, passed, rest, along_y, other_y


def smooth_kernel(
    block, pp, pf, pk, received, passed, rest, along_y, other_y,
    out, error_one, tiles,
    vp, vf, vk, wx, wy, zl, zh, dg, inv, va, vb,
    t0, t1, f1, k1, inv1, g1, h1, q2,
):
    cells_x, cells_y, depth = pp.shape
    planes = cells_x + 2 * REACH
    own_rows = pl.ds(ORIGIN, cells_y)
    top = ORIGIN - REACH + 1
    rows = cells_y + 2 * (REACH - 1)
    body = pl.ds(top, rows)

    windows = (vp, vf, vk)
    first_plan, second_plan, _ = x_plan(cells_y)

    def fill(array, x, first, value):
        if x < -REACH or x >= cells_x + REACH or (array == 1 and (x == -REACH or x == cells_x + REACH - 1)):
            return
        windows[array][REACH + x, pl.ds(ORIGIN + first, value.shape[0]), :] = value

    for x in range(cells_x):
        for array, ref in enumerate(views(block, cells_x)):
            fill(array, x, 0, ref[x])

    def fill_member(member):
        offset = cells_x * member

        def outside(side, distance):
            return (-distance if side == "low" else 2 * cells_x - 1 + distance) - offset

        for x in range(cells_x):
            for array, ref in enumerate((pp, pf, pk)):
                value = ref[x]
                fill(array, x + cells_x * (1 - member) - offset, 0, value + value if array == 1 else value)
        away, near = (("low", "high"), ("high", "low"))[member]
        for array, distance, distances in side_entries():
            key = (array, distance)
            for plan, ref in ((first_plan, received), (second_plan, rest)):
                for row, count, start in plan.get(key, []):
                    value = ref[pl.ds(start, count), :]
                    for each in distances:
                        fill(array, outside(away, each), row, value)
            if array != 1 and distance == 1:
                (row, count, start), = first_plan[key]
                fill(array, outside(near, 1), row, passed[pl.ds(start, count), :])
        below, above = ((along_y, other_y), (other_y, along_y))[member]
        spans = {(array, distance): distances for array, distance, distances in side_entries()}
        for side, array, index, count, start in y_plan(cells_x)[0]:
            if side == "inside":
                xs = [x - offset for x in ((2 * index, 2 * index + 1) if array == 0 else (index,))]
            else:
                xs = [outside(side, each) for each in spans[array, index]]
            if not any(-REACH <= x < cells_x + REACH for x in xs):
                continue
            before = below[pl.ds(start, count), :]
            after = above[pl.ds(start, count), :]
            for x in xs:
                fill(array, x, -count, before)
                fill(array, x, cells_y, after)

    for_member(fill_member)

    def lanes(count):
        return lax.broadcasted_iota(jnp.int32, (count, depth), 1)

    def rows_of(first, count):
        return lax.broadcasted_iota(jnp.int32, (count, depth), 0) + (first - ORIGIN)

    lane = lanes(rows)

    def weigh(plane, _):
        centre = vk[plane, body, :]
        west = centre + vk[plane - 1, body, :]
        wx[plane, body, :] = west
        east = centre + vk[plane + 1, body, :]
        south = centre + vk[plane, pl.ds(top - 1, rows), :]
        north = centre + vk[plane, pl.ds(top + 1, rows), :]
        wy[plane, body, :] = south
        wy[plane, pl.ds(top + rows, 1), :] = north[rows - 1:, :]
        down = jnp.where(lane > 0, pltpu.roll(centre, 1, 1), 0.0)
        up = jnp.where(lane < depth - 1, pltpu.roll(centre, depth - 1, 1), 0.0)
        total = west + east + south + north + (centre + down) + (centre + up)
        zl[plane, body, :] = jnp.where(lane > 0, centre + down, 0.0)
        zh[plane, body, :] = jnp.where(lane < depth - 1, centre + up, 0.0)
        dg[plane, body, :] = total
        inside = centre > 0.0
        inv[plane, body, :] = jnp.where(inside, 1.0 / jnp.where(inside, total, 1.0), 0.0)
        return 0

    lax.fori_loop(1, planes - 1, weigh, 0, unroll=True)
    wx[planes - 1, body, :] = vk[planes - 1, body, :] + vk[planes - 2, body, :]

    def stencil(v, plane, first, count):
        here = pl.ds(first, count)
        centre = v[plane, here, :]
        total = wx[plane, here, :] * v[plane - 1, here, :] + wx[plane + 1, here, :] * v[plane + 1, here, :]
        total += wy[plane, here, :] * v[plane, pl.ds(first - 1, count), :]
        total += wy[plane, pl.ds(first + 1, count), :] * v[plane, pl.ds(first + 1, count), :]
        total += zl[plane, here, :] * pltpu.roll(centre, 1, 1)
        total += zh[plane, here, :] * pltpu.roll(centre, depth - 1, 1)
        return total

    def relax(source_ref, target, reach):
        def one(plane, _):
            total = stencil(source_ref, plane, top, rows)
            target[plane, body, :] = inv[plane, body, :] * (vf[plane, body, :] + total)
            return 0

        lax.fori_loop(REACH - reach, REACH + cells_x + reach, one, 0, unroll=True)

    relax(vp, va, REACH - 1)
    relax(va, vb, REACH - 2)
    relax(vb, va, REACH - 3)
    relax(va, vb, REACH - 4)

    own_lane = lanes(cells_y)
    own_row = rows_of(ORIGIN, cells_y)
    for x in range(cells_x):
        even = ((own_row + own_lane + x) & 1) == 0
        out[x] = jnp.where(even, va[REACH + x, own_rows, :], vb[REACH + x, own_rows, :])

    planes_one = cells_x // 2
    first = ORIGIN - 4
    count = cells_y + 8
    lane = lanes(count)
    row = rows_of(first, count)

    def pair_lane(value, stride, lane):
        up = pltpu.roll(value, depth - stride, 1)
        down = pltpu.roll(value, stride, 1)
        return value + jnp.where((lane & stride) == 0, up, down)

    def pair_row(ref, index, first, count, stride, row):
        centre = ref[index, pl.ds(first, count), :]
        up = ref[index, pl.ds(first + stride, count), :]
        down = ref[index, pl.ds(first - stride, count), :]
        return centre + jnp.where((row & stride) == 0, up, down)

    def residual(plane_one, _):
        total = jnp.zeros((count, depth), jnp.float32)
        for half in range(2):
            plane = 2 * plane_one + REACH - 4 + half
            here = pl.ds(first, count)
            twice = vf[plane, here, :] - dg[plane, here, :] * va[plane, here, :] + stencil(vb, plane, first, count)
            even = ((row + lane + half) & 1) == 0
            total += jnp.where(even, twice, 0.0)
        t0[plane_one, pl.ds(first, count), :] = pair_lane(total, 1, lane)
        return 0

    lax.fori_loop(0, planes_one + 4, residual, 0, unroll=True)
    for x in range(planes_one + 4):
        f1[x, pl.ds(first, count), :] = 0.5 * pair_row(t0, x, first, count, 1, row)

    first_k = ORIGIN - 6
    count_k = cells_y + 16
    lane_k = lanes(count_k)
    row_k = rows_of(first_k, count_k)
    for x in range(planes_one + 6):
        plane = 2 * x + REACH - 6
        here = pl.ds(first_k, count_k)
        t1[x, here, :] = pair_lane(vk[plane, here, :] + vk[plane + 1, here, :], 1, lane_k)
    for x in range(planes_one + 6):
        k1[x, pl.ds(first_k, count_k), :] = 0.125 * pair_row(t1, x, first_k, count_k, 1, row_k)

    def down2(value, lane):
        return jnp.where(lane >= 2, pltpu.roll(value, 2, 1), 0.0)

    def up2(value, lane):
        return jnp.where(lane < depth - 2, pltpu.roll(value, depth - 2, 1), 0.0)

    here = pl.ds(first, count)
    for x in range(planes_one + 4):
        centre = k1[x + 1, here, :]
        total = 6.0 * centre + (k1[x, here, :] + k1[x + 2, here, :])
        total += k1[x + 1, pl.ds(first - 2, count), :] + k1[x + 1, pl.ds(first + 2, count), :]
        total += down2(centre, lane) + up2(centre, lane)
        inside = centre > 0.0
        inverse = jnp.where(inside, 1.0 / jnp.where(inside, total, 1.0), 0.0)
        inv1[x, here, :] = inverse
        g1[x, here, :] = inverse * f1[x, here, :]

    def stencil_one(v, x, v_x, first, count, lane):
        here = pl.ds(first, count)
        south = pl.ds(first - 2, count)
        north = pl.ds(first + 2, count)
        kc = k1[x, here, :]
        vc = v[v_x, here, :]
        total = (kc + k1[x - 1, here, :]) * v[v_x - 1, here, :] + (kc + k1[x + 1, here, :]) * v[v_x + 1, here, :]
        total += (kc + k1[x, south, :]) * v[v_x, south, :] + (kc + k1[x, north, :]) * v[v_x, north, :]
        total += (kc + down2(kc, lane)) * down2(vc, lane) + (kc + up2(kc, lane)) * up2(vc, lane)
        return total

    first_h = ORIGIN - 2
    count_h = cells_y + 8
    lane_h = lanes(count_h)
    row_h = rows_of(first_h, count_h)
    for x in range(planes_one + 2):
        here = pl.ds(first_h, count_h)
        total = stencil_one(g1, x + 2, x + 1, first_h, count_h, lane_h)
        odd = inv1[x + 1, here, :] * (f1[x + 1, here, :] + total)
        h1[x, here, :] = odd
        even_cell = ((x - 1 + (row_h >> 1) + (lane_h >> 1)) & 1) == 0
        error_one[x, pl.ds(first_h - 8, count_h), :] = jnp.where(even_cell, g1[x + 1, here, :], odd)

    own2 = own_lane
    row2 = own_row
    for x in range(planes_one // 2):
        sum_r = jnp.zeros((cells_y, depth), jnp.float32)
        for half in range(2):
            x1 = 2 * x + half
            total = stencil_one(h1, x1 + 3, x1 + 1, ORIGIN, cells_y, own2)
            even_cell = ((x1 + (row2 >> 1) + (own2 >> 1)) & 1) == 0
            sum_r += jnp.where(even_cell, total, 0.0)
        sum_k = k1[2 * x + 3, own_rows, :] + k1[2 * x + 4, own_rows, :]
        t0[x, own_rows, :] = pair_lane(sum_r, 2, own2)
        t1[x, own_rows, :] = pair_lane(sum_k, 2, own2)
    lane8 = lanes(cells_y // 4)
    tile = jnp.zeros((cells_y // 4, depth), jnp.float32)
    for x in range(planes_one // 2):
        q2[0] = (1.0 / 64.0) * pair_row(t0, x, ORIGIN, cells_y, 2, row2)
        q2[1] = 0.125 * pair_row(t1, x, ORIGIN, cells_y, 2, row2)
        for field in range(2):
            kept = q2[field, pl.ds(0, cells_y // 4, stride=4), :]
            tile = jnp.where((lane8 & 3) == 2 * field + x, kept, tile)
    tiles[...] = jnp.broadcast_to(tile[None], tiles.shape)


def smooth(copies, block, halo):
    cells_x, cells_y, depth = halo[0].shape
    planes = cells_x + 2 * REACH
    tall = cells_y + 2 * ORIGIN
    planes_one = cells_x // 2
    window = pltpu.VMEM((planes, tall, depth), jnp.float32)

    def level_one(count):
        return pltpu.VMEM((count, tall, depth), jnp.float32)

    return pl.pallas_call(
        smooth_kernel,
        out_shape=(
            jax.ShapeDtypeStruct((cells_x, cells_y, depth), jnp.float32),
            jax.ShapeDtypeStruct((planes_one + 2, cells_y + 16, depth), jnp.float32),
            jax.ShapeDtypeStruct((copies, cells_y // 4, depth), jnp.float32),
        ),
        scratch_shapes=[window] * 11
        + [
            level_one(planes_one + 4),
            level_one(planes_one + 6),
            level_one(planes_one + 4),
            level_one(planes_one + 6),
            level_one(planes_one + 4),
            level_one(planes_one + 4),
            level_one(planes_one + 2),
            pltpu.VMEM((2, cells_y, depth), jnp.float32),
        ],
        compiler_params=pltpu.CompilerParams(vmem_limit_bytes=VMEM_LIMIT),
        name="smooth",
    )(block, *halo)


def ring(value, shift, axis):
    return pltpu.roll(value, shift % value.shape[axis], axis)


def before_x(v):
    return jnp.concatenate([jnp.zeros_like(v[:1]), v[:-1]], 0)


def after_x(v):
    return jnp.concatenate([v[1:], jnp.zeros_like(v[:1])], 0)


class Places:
    def __init__(self, shape):
        self.row = lax.broadcasted_iota(jnp.int32, shape, 1)
        self.lane = lax.broadcasted_iota(jnp.int32, shape, 2)
        self.part = self.lane & 3
        self.depth = shape[2]

    def before_y(self, v, stride):
        turned = ring(v, stride, 1)
        return jnp.where(self.row >= stride, turned, ring(turned, 1, 2))

    def after_y(self, v, stride):
        turned = ring(v, -stride, 1)
        return jnp.where(self.row < 8 - stride, turned, ring(turned, -1, 2))

    def has_before_y(self, stride):
        return (self.row >= stride) | (self.part > 0)

    def has_after_y(self, stride):
        return (self.row < 8 - stride) | (self.part < 3)

    def has_before_z(self, stride):
        return self.lane >= 4 * stride

    def has_after_z(self, stride):
        return self.lane < self.depth - 4 * stride


def whole_weights(k, places, stride):
    west = k + before_x(k)
    east = k + after_x(k)
    masks = (
        places.has_before_y(stride),
        places.has_after_y(stride),
        places.has_before_z(stride),
        places.has_after_z(stride),
    )
    near = (
        places.before_y(k, stride),
        places.after_y(k, stride),
        ring(k, 4 * stride, 2),
        ring(k, -4 * stride, 2),
    )
    diagonal = west + east
    weights = [west, east]
    for mask, value in zip(masks, near):
        diagonal += k + jnp.where(mask, value, 0.0)
        weights.append(jnp.where(mask, k + value, 0.0))
    return weights, diagonal


def whole_sum(v, weights, places, stride):
    total = weights[0] * before_x(v) + weights[1] * after_x(v)
    total += weights[2] * places.before_y(v, stride) + weights[3] * places.after_y(v, stride)
    total += weights[4] * ring(v, 4 * stride, 2) + weights[5] * ring(v, -4 * stride, 2)
    return total


def whole_solve(k2, rhs2):
    planes = k2.shape[0]
    places = Places(k2.shape)
    weights, diagonal = whole_weights(k2, places, 1)
    parity = lax.broadcasted_iota(jnp.int32, k2.shape, 0) + places.row + (places.lane >> 2)
    even = (parity & 1) == 0
    inverse = 1.0 / diagonal
    scaled = 32.0 * rhs2
    even_values = inverse * scaled
    odd_values = inverse * (scaled + whole_sum(even_values, weights, places, 1))
    error_two = jnp.where(even, even_values, odd_values)
    left = jnp.where(even, whole_sum(odd_values, weights, places, 1), 0.0)

    half = places.row[: planes // 2] , places.lane[: planes // 2]
    first_row = (half[0] & 1) == 0
    first_lane = (half[1] & 4) == 0

    def coarse(v):
        v = v.reshape(planes // 2, 2, *v.shape[1:])
        v = v[:, 0] + v[:, 1]
        v = v + jnp.where(first_row, ring(v, -1, 1), ring(v, 1, 1))
        return v + jnp.where(first_lane, ring(v, -4, 2), ring(v, 4, 2))

    remain = (1.0 / 256.0) * coarse(left)
    k3 = 0.125 * coarse(k2)
    places3 = Places(k3.shape)
    weights3, diagonal3 = whole_weights(k3, places3, 2)

    def total(v):
        return jnp.sum(jnp.sum(v, axis=0, keepdims=True), axis=(1, 2), keepdims=True)

    error = jnp.zeros_like(remain)
    direction = remain
    norm_now = total(remain * remain)
    for repeat in range(CSWEEPS):
        image = (diagonal3 * direction - whole_sum(direction, weights3, places3, 2)) * (1.0 / 128.0)
        alpha = norm_now / total(direction * image)
        error = error + alpha * direction
        if repeat == CSWEEPS - 1:
            break
        remain = remain - alpha * image
        norm_next = total(remain * remain)
        direction = remain + norm_next / norm_now * direction
        norm_now = norm_next

    lower = 0.75 * error + 0.25 * before_x(error)
    upper = 0.75 * error + 0.25 * after_x(error)
    fine = jnp.stack([lower, upper], 1).reshape(k2.shape)
    near = jnp.where(
        (places.row & 1) == 0,
        jnp.where(places.has_before_y(1), places.before_y(fine, 1), 0.0),
        jnp.where(places.has_after_y(1), places.after_y(fine, 1), 0.0),
    )
    fine = 0.75 * fine + 0.25 * near
    near = jnp.where(
        (places.lane & 4) == 0,
        jnp.where(places.has_before_z(1), ring(fine, 4, 2), 0.0),
        jnp.where(places.has_after_z(1), ring(fine, -4, 2), 0.0),
    )
    return error_two + (0.75 * fine + 0.25 * near)


def finish(grid, wide, smoothed, error_one, out, e1, e0):
    cells_x, cells_y, depth = smoothed.shape
    i, j = lax.axis_index("gx"), lax.axis_index("gy")
    first = 8 - 2
    count = cells_y + 8
    lane = lax.broadcasted_iota(jnp.int32, (count, depth), 1)
    row = lax.broadcasted_iota(jnp.int32, (count, depth), 0) - 2

    def widen_z(value, stride, lane):
        down = jnp.where(lane >= stride, pltpu.roll(value, stride, 1), 0.0)
        up = jnp.where(lane < depth - stride, pltpu.roll(value, depth - stride, 1), 0.0)
        return 0.75 * value + 0.25 * jnp.where((lane & stride) == 0, down, up)

    def widen_y(ref, index, first, count, stride, row):
        centre = ref[index, pl.ds(first, count), :]
        down = ref[index, pl.ds(first - stride, count), :]
        up = ref[index, pl.ds(first + stride, count), :]
        return 0.75 * centre + 0.25 * jnp.where((row & stride) == 0, down, up)

    low_row = jnp.where(j > 0, -cells_y, 0)
    high_row = jnp.where(j < grid[1] - 1, 2 * cells_y, cells_y)
    inside = (row >= low_row) & (row < high_row)
    planes_two = cells_x // 4 + 2
    mid = [widen_z(widen_y(wide, x, first, count, 2, row), 2, lane) for x in range(planes_two)]
    for x in range(cells_x // 2 + 2):
        centre = (x + 1) // 2
        near = centre + (1 if x % 2 == 0 else -1)
        value = jnp.where(inside, 0.75 * mid[centre] + 0.25 * mid[near], 0.0)
        if x == 0:
            value = jnp.where(i > 0, value, 0.0)
        if x == cells_x // 2 + 1:
            value = jnp.where(i < grid[0] - 1, value, 0.0)
        here = pl.ds(first, count)
        e1[x, here, :] = error_one[x, here, :] + value

    lane = lax.broadcasted_iota(jnp.int32, (cells_y, depth), 1)
    row = lax.broadcasted_iota(jnp.int32, (cells_y, depth), 0)
    for x in range(cells_x // 2 + 2):
        e0[x] = widen_z(widen_y(e1, x, 8, cells_y, 1, row), 1, lane)
    for x in range(cells_x):
        centre = x // 2 + 1
        near = centre + (-1 if x % 2 == 0 else 1)
        out[x] = smoothed[x] + (0.75 * e0[centre] + 0.25 * e0[near])


def correct_kernel(grid, gathered, smoothed, error_one, out, whole, strip, wide, e1, e0):
    cells_y = smoothed.shape[1]
    nx, ny = grid
    i, j = lax.axis_index("gx"), lax.axis_index("gy")
    lane = lax.broadcasted_iota(jnp.int32, (8, 128), 1) & 3
    fields = [[], []]
    for column in range(nx):
        parts = [gathered[column * ny + part] for part in range(ny)]
        for field in range(2):
            for x in range(2):
                place = 2 * field + x
                plane = None
                for part in range(ny):
                    turned = parts[part] if part == place else ring(parts[part], part - place, 1)
                    plane = turned if plane is None else jnp.where(lane == part, turned, plane)
                fields[field].append(plane)
    rhs2 = jnp.stack(fields[0], 0)
    k2 = jnp.stack(fields[1], 0)
    planes = 2 * nx
    whole[0] = jnp.zeros((8, 128), jnp.float32)
    whole[planes + 1] = jnp.zeros((8, 128), jnp.float32)
    whole[pl.ds(1, planes)] = whole_solve(k2, rhs2)

    for x in range(4):
        centre = pltpu.roll(whole[2 * i + x], lax.rem(128 - j, 128), 1)
        below = jnp.where(j > 0, ring(centre, 1, 1), 0.0)
        above = jnp.where(j < ny - 1, ring(centre, -1, 1), 0.0)
        for index, value in enumerate((below, centre, above)):
            value = jnp.where(lane == 0, value, 0.0)
            value = value + ring(value, 1, 1)
            strip[x, pl.ds(8 * index, 8), :] = value + ring(value, 2, 1)
        for place in range(4):
            wide[x, pl.ds(4 + place, 8, stride=4), :] = strip[x, pl.ds(7, 8), :]
            wide[x, pl.ds(36 + place, 2, stride=4), :] = strip[x, pl.ds(15, 2), :]
    finish(grid, wide, smoothed, error_one, out, e1, e0)


def finish_kernel(grid, wide, smoothed, error_one, out, e1, e0):
    finish(grid, wide, smoothed, error_one, out, e1, e0)


def last_scratch(cells_x, cells_y, depth):
    count = cells_x // 2 + 2
    return [
        pltpu.VMEM((count, cells_y + 16, depth), jnp.float32),
        pltpu.VMEM((count, cells_y, depth), jnp.float32),
    ]


def correct_whole(grid, tiles, smoothed, error_one):
    gathered = lax.all_to_all(tiles, ("gx", "gy"), 0, 0, tiled=False)
    cells_x, cells_y, depth = smoothed.shape
    return pl.pallas_call(
        functools.partial(correct_kernel, grid),
        out_shape=jax.ShapeDtypeStruct(smoothed.shape, jnp.float32),
        scratch_shapes=[
            pltpu.VMEM((2 * grid[0] + 2, 8, depth), jnp.float32),
            pltpu.VMEM((4, 24, depth), jnp.float32),
            pltpu.VMEM((4, cells_y + 16, depth), jnp.float32),
        ]
        + last_scratch(cells_x, cells_y, depth),
        compiler_params=pltpu.CompilerParams(vmem_limit_bytes=VMEM_LIMIT),
        name="correct",
    )(gathered, smoothed, error_one)


def with_faces(shard):
    for axis, dim in (("gx", 0), ("gy", 1)):
        length = shard.shape[dim]
        last = lax.slice_in_dim(shard, length - 1, length, axis=dim)
        initial = lax.slice_in_dim(shard, 0, 1, axis=dim)
        before = lax.ppermute(last, axis, shifts(axis, 1))
        after = lax.ppermute(initial, axis, shifts(axis, -1))
        shard = jnp.concatenate([before, shard, after], axis=dim)
    return shard


def with_zeros(field):
    return jnp.pad(field, ((1, 1), (1, 1), (0, 0)))


def pad_depth(field):
    return jnp.pad(field, ((0, 0), (0, 0), (1, 1)))


def restrict(field):
    size_x, size_y, size_z = field.shape
    return field.reshape(size_x // 2, 2, size_y // 2, 2, size_z // 2, 2).mean(axis=(1, 3, 5))


def level_weights(coef_pad):
    c = pad_depth(coef_pad)
    wx = (c[1:, 1:-1, 1:-1] + c[:-1, 1:-1, 1:-1]) * 0.5
    wy = (c[1:-1, 1:, 1:-1] + c[1:-1, :-1, 1:-1]) * 0.5
    wz = (c[1:-1, 1:-1, 1:] + c[1:-1, 1:-1, :-1]) * 0.5
    diagonal = wx[1:] + wx[:-1] + wy[:, 1:] + wy[:, :-1] + wz[:, :, 1:] + wz[:, :, :-1]
    return (wx, wy, wz), diagonal


def neighbour_sum(field_pad, weights):
    wx, wy, wz = weights
    v = pad_depth(field_pad)
    total = wx[:-1] * v[:-2, 1:-1, 1:-1] + wx[1:] * v[2:, 1:-1, 1:-1]
    total = total + wy[:, :-1] * v[1:-1, :-2, 1:-1] + wy[:, 1:] * v[1:-1, 2:, 1:-1]
    return total + wz[:, :, :-1] * v[1:-1, 1:-1, :-2] + wz[:, :, 1:] * v[1:-1, 1:-1, 2:]


def prolong_axis(padded, axis):
    length = padded.shape[axis]
    middle = lax.slice_in_dim(padded, 1, length - 1, axis=axis)
    before = lax.slice_in_dim(padded, 0, length - 2, axis=axis)
    after = lax.slice_in_dim(padded, 2, length, axis=axis)
    joined = jnp.stack([0.75 * middle + 0.25 * before, 0.75 * middle + 0.25 * after], axis=axis + 1)
    shape = list(middle.shape)
    shape[axis] = 2 * shape[axis]
    return joined.reshape(shape)


def coarse_solve(rhs, weights, diagonal):
    error = jnp.zeros_like(rhs)
    remain = rhs
    direction = rhs
    norm_now = jnp.sum(remain * remain)
    for _ in range(CSWEEPS):
        image = (diagonal * direction - neighbour_sum(with_zeros(direction), weights)) * 4.0**-3
        alpha = norm_now / jnp.sum(direction * image)
        error = error + alpha * direction
        remain = remain - alpha * image
        norm_next = jnp.sum(remain * remain)
        direction = remain + norm_next / norm_now * direction
        norm_now = norm_next
    return error


def correct_spread(grid, tiles, smoothed, error_one):
    cells_x, cells_y, depth = smoothed.shape
    shape2 = (cells_x // 4, cells_y // 4, depth // 4)
    own = tiles[0].reshape(shape2[1], shape2[2], 2, shape2[0]).transpose(2, 3, 0, 1)
    rhs2, k2 = own[0], own[1]
    weights, diagonal = level_weights(with_faces(k2))
    parity = sum(lax.broadcasted_iota(jnp.int32, shape2, d) for d in range(3)) % 2
    error_two = jnp.where(parity == 0, rhs2 * 16.0 / diagonal, 0.0)
    total = neighbour_sum(with_faces(error_two), weights)
    error_two = jnp.where(parity == 1, (rhs2 * 16.0 + total) / diagonal, error_two)
    total = neighbour_sum(with_faces(error_two), weights)
    rhs3 = restrict(rhs2 - (diagonal * error_two - total) * 4.0**-2)
    merged = jnp.stack([rhs3, restrict(k2)])
    merged = lax.all_gather(merged, "gx", axis=1, tiled=True)
    merged = lax.all_gather(merged, "gy", axis=2, tiled=True)
    weights3, diagonal3 = level_weights(with_zeros(merged[1]))
    error_three = coarse_solve(merged[0], weights3, diagonal3)
    start_x = lax.axis_index("gx") * rhs3.shape[0]
    start_y = lax.axis_index("gy") * rhs3.shape[1]
    window = lax.dynamic_slice(
        with_zeros(error_three),
        (start_x, start_y, jnp.int32(0)),
        (rhs3.shape[0] + 2, rhs3.shape[1] + 2, rhs3.shape[2]),
    )
    finer = pad_depth(window)
    for axis in range(3):
        finer = prolong_axis(finer, axis)
    wide = with_faces(error_two + finer)
    wide = jnp.repeat(jnp.repeat(wide, 4, axis=1), 4, axis=2)
    wide = jnp.pad(wide, ((0, 0), (4, 4), (0, 0)))
    return pl.pallas_call(
        functools.partial(finish_kernel, grid),
        out_shape=jax.ShapeDtypeStruct(smoothed.shape, jnp.float32),
        scratch_shapes=last_scratch(cells_x, cells_y, depth),
        compiler_params=pltpu.CompilerParams(vmem_limit_bytes=VMEM_LIMIT),
        name="finish",
    )(wide, smoothed, error_one)


def on_device(pressure, source, coefficient):
    grid = (lax.axis_size("gx"), lax.axis_size("gy"))
    _, cells_y, depth = pressure.shape
    fits = grid[1] == 4 and cells_y == 32 and depth == 128
    own = (pressure, source, coefficient)
    block = stacked(*own)
    halo = fine_halo(own, block)
    copies = grid[0] * grid[1] if fits else 1
    smoothed, error_one, tiles = smooth(copies, block, halo)
    correct = correct_whole if fits else correct_spread
    return correct(grid, tiles, smoothed, error_one)


def solution(mesh):
    spec = P("gx", "gy", None)
    return jax.shard_map(on_device, mesh=mesh, in_specs=(spec, spec, spec), out_specs=spec, check_vma=False)
```

```python
import functools
import jax
import jax.numpy as jnp
from jax import lax
from jax.experimental import pallas as pl
from jax.experimental.pallas import tpu as pltpu
from jax.sharding import PartitionSpec as P

CSWEEPS = 4
REACH = 9
ORIGIN = 16
VMEM_LIMIT = 48 * 1024 * 1024


def y_rows(distance, array):
    rows = REACH if distance <= 2 else REACH + 2 - distance
    return rows - 1 if array == 1 else rows


def side_entries():
    pairs = [(0, d, (d, d + 1)) for d in range(1, REACH - 1, 2)] + [(0, REACH, (REACH,))]
    return pairs + [(1, d, (d,)) for d in range(1, REACH)] + [(2, d, (d,)) for d in range(1, REACH + 1)]


def x_plan(cells_y):
    first, second = {}, {}
    lengths = [0, 0]

    def put(message, plan, key, row, rows):
        plan.setdefault(key, []).append((row, rows, lengths[message]))
        lengths[message] += rows

    for array, distance, _ in side_entries():
        key = (array, distance)
        ends = y_rows(distance, array)
        put(0, first, key, 0, ends)
        put(0, first, key, cells_y - ends, ends)
        put(1, second, key, ends, cells_y - 2 * ends)
    return first, second, [-(-length // 8) * 8 for length in lengths]


def y_plan(cells_x):
    pieces = []
    start = 0
    inside = [(0, m) for m in range(cells_x // 2)] + [(a, x) for a in (1, 2) for x in range(cells_x)]
    chosen = [("inside", array, index, y_rows(0, array)) for array, index in inside]
    for side in ("low", "high"):
        chosen += [(side, array, distance, y_rows(distance, array)) for array, distance, _ in side_entries()]
    for side, array, index, rows in chosen:
        pieces.append((side, array, index, rows, start))
        start += rows
    return pieces, -(-start // 8) * 8


def shifts(axis, step):
    count = lax.axis_size(axis)
    return [(i, i + step) for i in range(count) if 0 <= i + step < count]


def swap_pairs():
    return [(i, i ^ 1) for i in range(lax.axis_size("gx"))]


def x_pairs():
    count = lax.axis_size("gx")
    pairs = [(i, i + 1) for i in range(1, count - 1, 2)]
    return pairs + [(j, i) for i, j in pairs]


def far_pairs():
    count = lax.axis_size("gx")
    return [(i, i - 2) for i in range(2, count, 2)] + [(i, i + 2) for i in range(1, count - 2, 2)]


def inside_rows(member, own, partner, array, index, first, rows):
    cells_x = own[0].shape[0]
    here = pl.ds(first, rows)

    def plane(x):
        if x // cells_x == member:
            return own[array][x % cells_x, here, :]
        value = partner[array][x % cells_x, here, :]
        return value + value if array == 1 else value

    if array != 0:
        return plane(index)
    depth = own[0].shape[2]
    row = lax.broadcasted_iota(jnp.int32, (rows, depth), 0) + first
    lane = lax.broadcasted_iota(jnp.int32, (rows, depth), 1)
    return jnp.where(((row + lane) & 1) == 1, plane(2 * index), plane(2 * index + 1))


def for_member(body):
    me = lax.axis_index("gx") & 1
    for member in range(2):
        pl.when(me == member)(functools.partial(body, member))


def split_kernel(block, pp, pf, pk, first, second, far):
    cells_x, cells_y, _ = pp.shape
    p, f, k = views(block, cells_x)
    plans = x_plan(cells_y)

    def body(member):
        for plan, target in zip(plans, (first, second)):
            for (array, distance), pieces in plan.items():
                plane = 2 * cells_x - distance if member == 1 else distance - 1
                index = plane // 2 if array == 0 else plane
                for row, rows, start in pieces:
                    value = inside_rows(member, (p, f, k), (pp, pf, pk), array, index, row, rows)
                    target[pl.ds(start, rows), :] = value
        outermost = (cells_x - 1) * member
        far[0] = p[outermost]
        far[1] = k[outermost]

    for_member(body)


def pack_kernel(block, pp, pf, pk, received, far, to_up, to_down):
    cells_x, cells_y, _ = pp.shape
    p, f, k = views(block, cells_x)
    plan = x_plan(cells_y)[0]

    def body(member):
        away = ("low", "high")[member]

        def piece(side, array, index, rows, row):
            if side == away:
                place = [s for r, _, s in plan[array, index] if r == row][0]
                return received[pl.ds(place, rows), :]
            if side != "inside" and index == REACH:
                return far[0 if array == 0 else 1, pl.ds(row, rows), :]
            if side == "inside":
                index += (cells_x // 2 if array == 0 else cells_x) * member
            else:
                plane = cells_x - index if member == 1 else cells_x - 1 + index
                index = plane // 2 if array == 0 else plane
            return inside_rows(member, (p, f, k), (pp, pf, pk), array, index, row, rows)

        for side, array, index, rows, start in y_plan(cells_x)[0]:
            to_up[pl.ds(start, rows), :] = piece(side, array, index, rows, cells_y - rows)
            to_down[pl.ds(start, rows), :] = piece(side, array, index, rows, 0)

    for_member(body)


def stacked(pressure, source, coefficient):
    block = jnp.concatenate([pressure, source, coefficient], 0)
    cells_x = pressure.shape[0]
    plane = lax.broadcasted_iota(jnp.int32, block.shape, 0)
    return block * jnp.where((plane >= cells_x) & (plane < 2 * cells_x), 2.0, 1.0)


def views(block, cells_x):
    return tuple(block.at[pl.ds(n * cells_x, cells_x)] for n in range(3))


def fine_halo(own, block):
    cells_x, cells_y, depth = own[0].shape
    params = pltpu.CompilerParams(vmem_limit_bytes=VMEM_LIMIT)

    def packed(length):
        return jax.ShapeDtypeStruct((length, depth), jnp.float32)

    partner = tuple(lax.ppermute(v, "gx", swap_pairs()) for v in own)
    lengths = x_plan(cells_y)[2]
    planes = jax.ShapeDtypeStruct((2, cells_y, depth), jnp.float32)
    first, second, outermost = pl.pallas_call(
        split_kernel, out_shape=[packed(n) for n in lengths] + [planes], compiler_params=params, name="split_block"
    )(block, *partner)
    far = lax.ppermute(outermost, "gx", far_pairs())
    received = lax.ppermute(first, "gx", x_pairs())
    length = y_plan(cells_x)[1]
    to_up, to_down = pl.pallas_call(
        pack_kernel, out_shape=[packed(length)] * 2, compiler_params=params, name="pack_halo"
    )(block, *partner, received, far)
    below = lax.ppermute(to_up, "gy", shifts("gy", 1))
    above = lax.ppermute(to_down, "gy", shifts("gy", -1))
    rest = lax.ppermute(second, "gx", x_pairs())
    return *partner, received, rest, far, below, above


def smooth_kernel(
    block, pp, pf, pk, received, rest, far, below, above,
    out, error_one, tiles,
    vp, vf, vk, wx, wy, zl, zh, dg, inv, va, vb,
    t0, t1, f1, k1, inv1, g1, h1, q2,
):
    cells_x, cells_y, depth = pp.shape
    planes = cells_x + 2 * REACH
    own_rows = pl.ds(ORIGIN, cells_y)
    top = ORIGIN - REACH + 1
    rows = cells_y + 2 * (REACH - 1)
    body = pl.ds(top, rows)

    windows = (vp, vf, vk)
    first_plan, second_plan, _ = x_plan(cells_y)

    def fill(array, x, first, value):
        if x < -REACH or x >= cells_x + REACH or (array == 1 and (x == -REACH or x == cells_x + REACH - 1)):
            return
        windows[array][REACH + x, pl.ds(ORIGIN + first, value.shape[0]), :] = value

    for x in range(cells_x):
        for array, ref in enumerate(views(block, cells_x)):
            fill(array, x, 0, ref[x])

    spans = {(array, distance): distances for array, distance, distances in side_entries()}

    def outside(side, distance):
        return -distance if side == "low" else cells_x - 1 + distance

    def fill_member(member):
        away, near = (("low", "high"), ("high", "low"))[member]
        for x in range(cells_x):
            for array, ref in enumerate((pp, pf, pk)):
                value = ref[x]
                fill(array, x + cells_x * (1 - 2 * member), 0, value + value if array == 1 else value)
        fill(0, outside(near, REACH), 0, far[0])
        fill(2, outside(near, REACH), 0, far[1])
        for plan, ref in ((first_plan, received), (second_plan, rest)):
            for (array, distance), pieces in plan.items():
                for row, count, start in pieces:
                    value = ref[pl.ds(start, count), :]
                    for each in spans[array, distance]:
                        fill(array, outside(away, each), row, value)

    for_member(fill_member)
    for side, array, index, count, start in y_plan(cells_x)[0]:
        before = below[pl.ds(start, count), :]
        after = above[pl.ds(start, count), :]
        if side == "inside":
            xs = (2 * index, 2 * index + 1) if array == 0 else (index,)
        else:
            xs = [outside(side, each) for each in spans[array, index]]
        for x in xs:
            fill(array, x, -count, before)
            fill(array, x, cells_y, after)

    def lanes(count):
        return lax.broadcasted_iota(jnp.int32, (count, depth), 1)

    def rows_of(first, count):
        return lax.broadcasted_iota(jnp.int32, (count, depth), 0) + (first - ORIGIN)

    lane = lanes(rows)

    def weigh(plane, _):
        centre = vk[plane, body, :]
        west = centre + vk[plane - 1, body, :]
        wx[plane, body, :] = west
        east = centre + vk[plane + 1, body, :]
        south = centre + vk[plane, pl.ds(top - 1, rows), :]
        north = centre + vk[plane, pl.ds(top + 1, rows), :]
        wy[plane, body, :] = south
        wy[plane, pl.ds(top + rows, 1), :] = north[rows - 1:, :]
        down = jnp.where(lane > 0, pltpu.roll(centre, 1, 1), 0.0)
        up = jnp.where(lane < depth - 1, pltpu.roll(centre, depth - 1, 1), 0.0)
        total = west + east + south + north + (centre + down) + (centre + up)
        zl[plane, body, :] = jnp.where(lane > 0, centre + down, 0.0)
        zh[plane, body, :] = jnp.where(lane < depth - 1, centre + up, 0.0)
        dg[plane, body, :] = total
        inside = centre > 0.0
        inv[plane, body, :] = jnp.where(inside, 1.0 / jnp.where(inside, total, 1.0), 0.0)
        return 0

    lax.fori_loop(1, planes - 1, weigh, 0, unroll=True)
    wx[planes - 1, body, :] = vk[planes - 1, body, :] + vk[planes - 2, body, :]

    def stencil(v, plane, first, count):
        here = pl.ds(first, count)
        centre = v[plane, here, :]
        total = wx[plane, here, :] * v[plane - 1, here, :] + wx[plane + 1, here, :] * v[plane + 1, here, :]
        total += wy[plane, here, :] * v[plane, pl.ds(first - 1, count), :]
        total += wy[plane, pl.ds(first + 1, count), :] * v[plane, pl.ds(first + 1, count), :]
        total += zl[plane, here, :] * pltpu.roll(centre, 1, 1)
        total += zh[plane, here, :] * pltpu.roll(centre, depth - 1, 1)
        return total

    def relax(source_ref, target, reach):
        def one(plane, _):
            total = stencil(source_ref, plane, top, rows)
            target[plane, body, :] = inv[plane, body, :] * (vf[plane, body, :] + total)
            return 0

        lax.fori_loop(REACH - reach, REACH + cells_x + reach, one, 0, unroll=True)

    relax(vp, va, REACH - 1)
    relax(va, vb, REACH - 2)
    relax(vb, va, REACH - 3)
    relax(va, vb, REACH - 4)

    own_lane = lanes(cells_y)
    own_row = rows_of(ORIGIN, cells_y)
    for x in range(cells_x):
        even = ((own_row + own_lane + x) & 1) == 0
        out[x] = jnp.where(even, va[REACH + x, own_rows, :], vb[REACH + x, own_rows, :])

    planes_one = cells_x // 2
    first = ORIGIN - 4
    count = cells_y + 8
    lane = lanes(count)
    row = rows_of(first, count)

    def pair_lane(value, stride, lane):
        up = pltpu.roll(value, depth - stride, 1)
        down = pltpu.roll(value, stride, 1)
        return value + jnp.where((lane & stride) == 0, up, down)

    def pair_row(ref, index, first, count, stride, row):
        centre = ref[index, pl.ds(first, count), :]
        up = ref[index, pl.ds(first + stride, count), :]
        down = ref[index, pl.ds(first - stride, count), :]
        return centre + jnp.where((row & stride) == 0, up, down)

    def residual(plane_one, _):
        total = jnp.zeros((count, depth), jnp.float32)
        for half in range(2):
            plane = 2 * plane_one + REACH - 4 + half
            here = pl.ds(first, count)
            twice = vf[plane, here, :] - dg[plane, here, :] * va[plane, here, :] + stencil(vb, plane, first, count)
            even = ((row + lane + half) & 1) == 0
            total += jnp.where(even, twice, 0.0)
        t0[plane_one, pl.ds(first, count), :] = pair_lane(total, 1, lane)
        return 0

    lax.fori_loop(0, planes_one + 4, residual, 0, unroll=True)
    for x in range(planes_one + 4):
        f1[x, pl.ds(first, count), :] = 0.5 * pair_row(t0, x, first, count, 1, row)

    first_k = ORIGIN - 6
    count_k = cells_y + 16
    lane_k = lanes(count_k)
    row_k = rows_of(first_k, count_k)
    for x in range(planes_one + 6):
        plane = 2 * x + REACH - 6
        here = pl.ds(first_k, count_k)
        t1[x, here, :] = pair_lane(vk[plane, here, :] + vk[plane + 1, here, :], 1, lane_k)
    for x in range(planes_one + 6):
        k1[x, pl.ds(first_k, count_k), :] = 0.125 * pair_row(t1, x, first_k, count_k, 1, row_k)

    def down2(value, lane):
        return jnp.where(lane >= 2, pltpu.roll(value, 2, 1), 0.0)

    def up2(value, lane):
        return jnp.where(lane < depth - 2, pltpu.roll(value, depth - 2, 1), 0.0)

    here = pl.ds(first, count)
    for x in range(planes_one + 4):
        centre = k1[x + 1, here, :]
        total = 6.0 * centre + (k1[x, here, :] + k1[x + 2, here, :])
        total += k1[x + 1, pl.ds(first - 2, count), :] + k1[x + 1, pl.ds(first + 2, count), :]
        total += down2(centre, lane) + up2(centre, lane)
        inside = centre > 0.0
        inverse = jnp.where(inside, 1.0 / jnp.where(inside, total, 1.0), 0.0)
        inv1[x, here, :] = inverse
        g1[x, here, :] = inverse * f1[x, here, :]

    def stencil_one(v, x, v_x, first, count, lane):
        here = pl.ds(first, count)
        south = pl.ds(first - 2, count)
        north = pl.ds(first + 2, count)
        kc = k1[x, here, :]
        vc = v[v_x, here, :]
        total = (kc + k1[x - 1, here, :]) * v[v_x - 1, here, :] + (kc + k1[x + 1, here, :]) * v[v_x + 1, here, :]
        total += (kc + k1[x, south, :]) * v[v_x, south, :] + (kc + k1[x, north, :]) * v[v_x, north, :]
        total += (kc + down2(kc, lane)) * down2(vc, lane) + (kc + up2(kc, lane)) * up2(vc, lane)
        return total

    first_h = ORIGIN - 2
    count_h = cells_y + 8
    lane_h = lanes(count_h)
    row_h = rows_of(first_h, count_h)
    for x in range(planes_one + 2):
        here = pl.ds(first_h, count_h)
        total = stencil_one(g1, x + 2, x + 1, first_h, count_h, lane_h)
        odd = inv1[x + 1, here, :] * (f1[x + 1, here, :] + total)
        h1[x, here, :] = odd
        even_cell = ((x - 1 + (row_h >> 1) + (lane_h >> 1)) & 1) == 0
        error_one[x, pl.ds(first_h - 8, count_h), :] = jnp.where(even_cell, g1[x + 1, here, :], odd)

    own2 = own_lane
    row2 = own_row
    for x in range(planes_one // 2):
        sum_r = jnp.zeros((cells_y, depth), jnp.float32)
        for half in range(2):
            x1 = 2 * x + half
            total = stencil_one(h1, x1 + 3, x1 + 1, ORIGIN, cells_y, own2)
            even_cell = ((x1 + (row2 >> 1) + (own2 >> 1)) & 1) == 0
            sum_r += jnp.where(even_cell, total, 0.0)
        sum_k = k1[2 * x + 3, own_rows, :] + k1[2 * x + 4, own_rows, :]
        t0[x, own_rows, :] = pair_lane(sum_r, 2, own2)
        t1[x, own_rows, :] = pair_lane(sum_k, 2, own2)
    lane8 = lanes(cells_y // 4)
    tile = jnp.zeros((cells_y // 4, depth), jnp.float32)
    for x in range(planes_one // 2):
        q2[0] = (1.0 / 64.0) * pair_row(t0, x, ORIGIN, cells_y, 2, row2)
        q2[1] = 0.125 * pair_row(t1, x, ORIGIN, cells_y, 2, row2)
        for field in range(2):
            kept = q2[field, pl.ds(0, cells_y // 4, stride=4), :]
            tile = jnp.where((lane8 & 3) == 2 * field + x, kept, tile)
    tiles[...] = jnp.broadcast_to(tile[None], tiles.shape)


def smooth(copies, block, halo):
    cells_x, cells_y, depth = halo[0].shape
    planes = cells_x + 2 * REACH
    tall = cells_y + 2 * ORIGIN
    planes_one = cells_x // 2
    window = pltpu.VMEM((planes, tall, depth), jnp.float32)

    def level_one(count):
        return pltpu.VMEM((count, tall, depth), jnp.float32)

    return pl.pallas_call(
        smooth_kernel,
        out_shape=(
            jax.ShapeDtypeStruct((cells_x, cells_y, depth), jnp.float32),
            jax.ShapeDtypeStruct((planes_one + 2, cells_y + 16, depth), jnp.float32),
            jax.ShapeDtypeStruct((copies, cells_y // 4, depth), jnp.float32),
        ),
        scratch_shapes=[window] * 11
        + [
            level_one(planes_one + 4),
            level_one(planes_one + 6),
            level_one(planes_one + 4),
            level_one(planes_one + 6),
            level_one(planes_one + 4),
            level_one(planes_one + 4),
            level_one(planes_one + 2),
            pltpu.VMEM((2, cells_y, depth), jnp.float32),
        ],
        compiler_params=pltpu.CompilerParams(vmem_limit_bytes=VMEM_LIMIT),
        name="smooth",
    )(block, *halo)


def ring(value, shift, axis):
    return pltpu.roll(value, shift % value.shape[axis], axis)


def before_x(v):
    return jnp.concatenate([jnp.zeros_like(v[:1]), v[:-1]], 0)


def after_x(v):
    return jnp.concatenate([v[1:], jnp.zeros_like(v[:1])], 0)


class Places:
    def __init__(self, shape):
        self.row = lax.broadcasted_iota(jnp.int32, shape, 1)
        self.lane = lax.broadcasted_iota(jnp.int32, shape, 2)
        self.part = self.lane & 3
        self.depth = shape[2]

    def before_y(self, v, stride):
        turned = ring(v, stride, 1)
        return jnp.where(self.row >= stride, turned, ring(turned, 1, 2))

    def after_y(self, v, stride):
        turned = ring(v, -stride, 1)
        return jnp.where(self.row < 8 - stride, turned, ring(turned, -1, 2))

    def has_before_y(self, stride):
        return (self.row >= stride) | (self.part > 0)

    def has_after_y(self, stride):
        return (self.row < 8 - stride) | (self.part < 3)

    def has_before_z(self, stride):
        return self.lane >= 4 * stride

    def has_after_z(self, stride):
        return self.lane < self.depth - 4 * stride


def whole_weights(k, places, stride):
    west = k + before_x(k)
    east = k + after_x(k)
    masks = (
        places.has_before_y(stride),
        places.has_after_y(stride),
        places.has_before_z(stride),
        places.has_after_z(stride),
    )
    near = (
        places.before_y(k, stride),
        places.after_y(k, stride),
        ring(k, 4 * stride, 2),
        ring(k, -4 * stride, 2),
    )
    diagonal = west + east
    weights = [west, east]
    for mask, value in zip(masks, near):
        diagonal += k + jnp.where(mask, value, 0.0)
        weights.append(jnp.where(mask, k + value, 0.0))
    return weights, diagonal


def whole_sum(v, weights, places, stride):
    total = weights[0] * before_x(v) + weights[1] * after_x(v)
    total += weights[2] * places.before_y(v, stride) + weights[3] * places.after_y(v, stride)
    total += weights[4] * ring(v, 4 * stride, 2) + weights[5] * ring(v, -4 * stride, 2)
    return total


def whole_solve(k2, rhs2):
    planes = k2.shape[0]
    places = Places(k2.shape)
    weights, diagonal = whole_weights(k2, places, 1)
    parity = lax.broadcasted_iota(jnp.int32, k2.shape, 0) + places.row + (places.lane >> 2)
    even = (parity & 1) == 0
    inverse = 1.0 / diagonal
    scaled = 32.0 * rhs2
    even_values = inverse * scaled
    odd_values = inverse * (scaled + whole_sum(even_values, weights, places, 1))
    error_two = jnp.where(even, even_values, odd_values)
    left = jnp.where(even, whole_sum(odd_values, weights, places, 1), 0.0)

    half = places.row[: planes // 2] , places.lane[: planes // 2]
    first_row = (half[0] & 1) == 0
    first_lane = (half[1] & 4) == 0

    def coarse(v):
        v = v.reshape(planes // 2, 2, *v.shape[1:])
        v = v[:, 0] + v[:, 1]
        v = v + jnp.where(first_row, ring(v, -1, 1), ring(v, 1, 1))
        return v + jnp.where(first_lane, ring(v, -4, 2), ring(v, 4, 2))

    remain = (1.0 / 256.0) * coarse(left)
    k3 = 0.125 * coarse(k2)
    places3 = Places(k3.shape)
    weights3, diagonal3 = whole_weights(k3, places3, 2)

    def total(v):
        return jnp.sum(jnp.sum(v, axis=0, keepdims=True), axis=(1, 2), keepdims=True)

    error = jnp.zeros_like(remain)
    direction = remain
    norm_now = total(remain * remain)
    for repeat in range(CSWEEPS):
        image = (diagonal3 * direction - whole_sum(direction, weights3, places3, 2)) * (1.0 / 128.0)
        alpha = norm_now / total(direction * image)
        error = error + alpha * direction
        if repeat == CSWEEPS - 1:
            break
        remain = remain - alpha * image
        norm_next = total(remain * remain)
        direction = remain + norm_next / norm_now * direction
        norm_now = norm_next

    lower = 0.75 * error + 0.25 * before_x(error)
    upper = 0.75 * error + 0.25 * after_x(error)
    fine = jnp.stack([lower, upper], 1).reshape(k2.shape)
    near = jnp.where(
        (places.row & 1) == 0,
        jnp.where(places.has_before_y(1), places.before_y(fine, 1), 0.0),
        jnp.where(places.has_after_y(1), places.after_y(fine, 1), 0.0),
    )
    fine = 0.75 * fine + 0.25 * near
    near = jnp.where(
        (places.lane & 4) == 0,
        jnp.where(places.has_before_z(1), ring(fine, 4, 2), 0.0),
        jnp.where(places.has_after_z(1), ring(fine, -4, 2), 0.0),
    )
    return error_two + (0.75 * fine + 0.25 * near)


def finish(grid, wide, smoothed, error_one, out, e1, e0):
    cells_x, cells_y, depth = smoothed.shape
    i, j = lax.axis_index("gx"), lax.axis_index("gy")
    first = 8 - 2
    count = cells_y + 8
    lane = lax.broadcasted_iota(jnp.int32, (count, depth), 1)
    row = lax.broadcasted_iota(jnp.int32, (count, depth), 0) - 2

    def widen_z(value, stride, lane):
        down = jnp.where(lane >= stride, pltpu.roll(value, stride, 1), 0.0)
        up = jnp.where(lane < depth - stride, pltpu.roll(value, depth - stride, 1), 0.0)
        return 0.75 * value + 0.25 * jnp.where((lane & stride) == 0, down, up)

    def widen_y(ref, index, first, count, stride, row):
        centre = ref[index, pl.ds(first, count), :]
        down = ref[index, pl.ds(first - stride, count), :]
        up = ref[index, pl.ds(first + stride, count), :]
        return 0.75 * centre + 0.25 * jnp.where((row & stride) == 0, down, up)

    low_row = jnp.where(j > 0, -cells_y, 0)
    high_row = jnp.where(j < grid[1] - 1, 2 * cells_y, cells_y)
    inside = (row >= low_row) & (row < high_row)
    planes_two = cells_x // 4 + 2
    mid = [widen_z(widen_y(wide, x, first, count, 2, row), 2, lane) for x in range(planes_two)]
    for x in range(cells_x // 2 + 2):
        centre = (x + 1) // 2
        near = centre + (1 if x % 2 == 0 else -1)
        value = jnp.where(inside, 0.75 * mid[centre] + 0.25 * mid[near], 0.0)
        if x == 0:
            value = jnp.where(i > 0, value, 0.0)
        if x == cells_x // 2 + 1:
            value = jnp.where(i < grid[0] - 1, value, 0.0)
        here = pl.ds(first, count)
        e1[x, here, :] = error_one[x, here, :] + value

    lane = lax.broadcasted_iota(jnp.int32, (cells_y, depth), 1)
    row = lax.broadcasted_iota(jnp.int32, (cells_y, depth), 0)
    for x in range(cells_x // 2 + 2):
        e0[x] = widen_z(widen_y(e1, x, 8, cells_y, 1, row), 1, lane)
    for x in range(cells_x):
        centre = x // 2 + 1
        near = centre + (-1 if x % 2 == 0 else 1)
        out[x] = smoothed[x] + (0.75 * e0[centre] + 0.25 * e0[near])


def correct_kernel(grid, gathered, smoothed, error_one, out, whole, strip, wide, e1, e0):
    cells_y = smoothed.shape[1]
    nx, ny = grid
    i, j = lax.axis_index("gx"), lax.axis_index("gy")
    lane = lax.broadcasted_iota(jnp.int32, (8, 128), 1) & 3
    fields = [[], []]
    for column in range(nx):
        parts = [gathered[column * ny + part] for part in range(ny)]
        for field in range(2):
            for x in range(2):
                place = 2 * field + x
                plane = None
                for part in range(ny):
                    turned = parts[part] if part == place else ring(parts[part], part - place, 1)
                    plane = turned if plane is None else jnp.where(lane == part, turned, plane)
                fields[field].append(plane)
    rhs2 = jnp.stack(fields[0], 0)
    k2 = jnp.stack(fields[1], 0)
    planes = 2 * nx
    whole[0] = jnp.zeros((8, 128), jnp.float32)
    whole[planes + 1] = jnp.zeros((8, 128), jnp.float32)
    whole[pl.ds(1, planes)] = whole_solve(k2, rhs2)

    for x in range(4):
        centre = pltpu.roll(whole[2 * i + x], lax.rem(128 - j, 128), 1)
        below = jnp.where(j > 0, ring(centre, 1, 1), 0.0)
        above = jnp.where(j < ny - 1, ring(centre, -1, 1), 0.0)
        for index, value in enumerate((below, centre, above)):
            value = jnp.where(lane == 0, value, 0.0)
            value = value + ring(value, 1, 1)
            strip[x, pl.ds(8 * index, 8), :] = value + ring(value, 2, 1)
        for place in range(4):
            wide[x, pl.ds(4 + place, 8, stride=4), :] = strip[x, pl.ds(7, 8), :]
            wide[x, pl.ds(36 + place, 2, stride=4), :] = strip[x, pl.ds(15, 2), :]
    finish(grid, wide, smoothed, error_one, out, e1, e0)


def finish_kernel(grid, wide, smoothed, error_one, out, e1, e0):
    finish(grid, wide, smoothed, error_one, out, e1, e0)


def last_scratch(cells_x, cells_y, depth):
    count = cells_x // 2 + 2
    return [
        pltpu.VMEM((count, cells_y + 16, depth), jnp.float32),
        pltpu.VMEM((count, cells_y, depth), jnp.float32),
    ]


def correct_whole(grid, tiles, smoothed, error_one):
    gathered = lax.all_to_all(tiles, ("gx", "gy"), 0, 0, tiled=False)
    cells_x, cells_y, depth = smoothed.shape
    return pl.pallas_call(
        functools.partial(correct_kernel, grid),
        out_shape=jax.ShapeDtypeStruct(smoothed.shape, jnp.float32),
        scratch_shapes=[
            pltpu.VMEM((2 * grid[0] + 2, 8, depth), jnp.float32),
            pltpu.VMEM((4, 24, depth), jnp.float32),
            pltpu.VMEM((4, cells_y + 16, depth), jnp.float32),
        ]
        + last_scratch(cells_x, cells_y, depth),
        compiler_params=pltpu.CompilerParams(vmem_limit_bytes=VMEM_LIMIT),
        name="correct",
    )(gathered, smoothed, error_one)


def with_faces(shard):
    for axis, dim in (("gx", 0), ("gy", 1)):
        length = shard.shape[dim]
        last = lax.slice_in_dim(shard, length - 1, length, axis=dim)
        initial = lax.slice_in_dim(shard, 0, 1, axis=dim)
        before = lax.ppermute(last, axis, shifts(axis, 1))
        after = lax.ppermute(initial, axis, shifts(axis, -1))
        shard = jnp.concatenate([before, shard, after], axis=dim)
    return shard


def with_zeros(field):
    return jnp.pad(field, ((1, 1), (1, 1), (0, 0)))


def pad_depth(field):
    return jnp.pad(field, ((0, 0), (0, 0), (1, 1)))


def restrict(field):
    size_x, size_y, size_z = field.shape
    return field.reshape(size_x // 2, 2, size_y // 2, 2, size_z // 2, 2).mean(axis=(1, 3, 5))


def level_weights(coef_pad):
    c = pad_depth(coef_pad)
    wx = (c[1:, 1:-1, 1:-1] + c[:-1, 1:-1, 1:-1]) * 0.5
    wy = (c[1:-1, 1:, 1:-1] + c[1:-1, :-1, 1:-1]) * 0.5
    wz = (c[1:-1, 1:-1, 1:] + c[1:-1, 1:-1, :-1]) * 0.5
    diagonal = wx[1:] + wx[:-1] + wy[:, 1:] + wy[:, :-1] + wz[:, :, 1:] + wz[:, :, :-1]
    return (wx, wy, wz), diagonal


def neighbour_sum(field_pad, weights):
    wx, wy, wz = weights
    v = pad_depth(field_pad)
    total = wx[:-1] * v[:-2, 1:-1, 1:-1] + wx[1:] * v[2:, 1:-1, 1:-1]
    total = total + wy[:, :-1] * v[1:-1, :-2, 1:-1] + wy[:, 1:] * v[1:-1, 2:, 1:-1]
    return total + wz[:, :, :-1] * v[1:-1, 1:-1, :-2] + wz[:, :, 1:] * v[1:-1, 1:-1, 2:]


def prolong_axis(padded, axis):
    length = padded.shape[axis]
    middle = lax.slice_in_dim(padded, 1, length - 1, axis=axis)
    before = lax.slice_in_dim(padded, 0, length - 2, axis=axis)
    after = lax.slice_in_dim(padded, 2, length, axis=axis)
    joined = jnp.stack([0.75 * middle + 0.25 * before, 0.75 * middle + 0.25 * after], axis=axis + 1)
    shape = list(middle.shape)
    shape[axis] = 2 * shape[axis]
    return joined.reshape(shape)


def coarse_solve(rhs, weights, diagonal):
    error = jnp.zeros_like(rhs)
    remain = rhs
    direction = rhs
    norm_now = jnp.sum(remain * remain)
    for _ in range(CSWEEPS):
        image = (diagonal * direction - neighbour_sum(with_zeros(direction), weights)) * 4.0**-3
        alpha = norm_now / jnp.sum(direction * image)
        error = error + alpha * direction
        remain = remain - alpha * image
        norm_next = jnp.sum(remain * remain)
        direction = remain + norm_next / norm_now * direction
        norm_now = norm_next
    return error


def correct_spread(grid, tiles, smoothed, error_one):
    cells_x, cells_y, depth = smoothed.shape
    shape2 = (cells_x // 4, cells_y // 4, depth // 4)
    own = tiles[0].reshape(shape2[1], shape2[2], 2, shape2[0]).transpose(2, 3, 0, 1)
    rhs2, k2 = own[0], own[1]
    weights, diagonal = level_weights(with_faces(k2))
    parity = sum(lax.broadcasted_iota(jnp.int32, shape2, d) for d in range(3)) % 2
    error_two = jnp.where(parity == 0, rhs2 * 16.0 / diagonal, 0.0)
    total = neighbour_sum(with_faces(error_two), weights)
    error_two = jnp.where(parity == 1, (rhs2 * 16.0 + total) / diagonal, error_two)
    total = neighbour_sum(with_faces(error_two), weights)
    rhs3 = restrict(rhs2 - (diagonal * error_two - total) * 4.0**-2)
    merged = jnp.stack([rhs3, restrict(k2)])
    merged = lax.all_gather(merged, "gx", axis=1, tiled=True)
    merged = lax.all_gather(merged, "gy", axis=2, tiled=True)
    weights3, diagonal3 = level_weights(with_zeros(merged[1]))
    error_three = coarse_solve(merged[0], weights3, diagonal3)
    start_x = lax.axis_index("gx") * rhs3.shape[0]
    start_y = lax.axis_index("gy") * rhs3.shape[1]
    window = lax.dynamic_slice(
        with_zeros(error_three),
        (start_x, start_y, jnp.int32(0)),
        (rhs3.shape[0] + 2, rhs3.shape[1] + 2, rhs3.shape[2]),
    )
    finer = pad_depth(window)
    for axis in range(3):
        finer = prolong_axis(finer, axis)
    wide = with_faces(error_two + finer)
    wide = jnp.repeat(jnp.repeat(wide, 4, axis=1), 4, axis=2)
    wide = jnp.pad(wide, ((0, 0), (4, 4), (0, 0)))
    return pl.pallas_call(
        functools.partial(finish_kernel, grid),
        out_shape=jax.ShapeDtypeStruct(smoothed.shape, jnp.float32),
        scratch_shapes=last_scratch(cells_x, cells_y, depth),
        compiler_params=pltpu.CompilerParams(vmem_limit_bytes=VMEM_LIMIT),
        name="finish",
    )(wide, smoothed, error_one)


def on_device(pressure, source, coefficient):
    grid = (lax.axis_size("gx"), lax.axis_size("gy"))
    _, cells_y, depth = pressure.shape
    fits = grid[1] == 4 and cells_y == 32 and depth == 128
    own = (pressure, source, coefficient)
    block = stacked(*own)
    halo = fine_halo(own, block)
    copies = grid[0] * grid[1] if fits else 1
    smoothed, error_one, tiles = smooth(copies, block, halo)
    correct = correct_whole if fits else correct_spread
    return correct(grid, tiles, smoothed, error_one)


def solution(mesh):
    spec = P("gx", "gy", None)
    return jax.shard_map(on_device, mesh=mesh, in_specs=(spec, spec, spec), out_specs=spec, check_vma=False)
```

```python
import functools
import jax
import jax.numpy as jnp
from jax import lax
from jax.experimental import pallas as pl
from jax.experimental.pallas import tpu as pltpu
from jax.sharding import PartitionSpec as P

CSWEEPS = 4
REACH = 9
ORIGIN = 16
VMEM_LIMIT = 48 * 1024 * 1024


def y_rows(distance, array):
    rows = REACH if distance <= 2 else REACH + 2 - distance
    return rows - 1 if array == 1 else rows


def side_entries():
    pairs = [(0, d, (d, d + 1)) for d in range(1, REACH - 1, 2)] + [(0, REACH, (REACH,))]
    return pairs + [(1, d, (d,)) for d in range(1, REACH)] + [(2, d, (d,)) for d in range(1, REACH + 1)]


def x_plan(cells_y):
    first, second = {}, {}
    lengths = [0, 0]

    def put(message, plan, key, row, rows):
        plan.setdefault(key, []).append((row, rows, lengths[message]))
        lengths[message] += rows

    for array, distance, _ in side_entries():
        key = (array, distance)
        ends = y_rows(distance, array)
        if array != 1 and distance == 1:
            put(0, first, key, 0, cells_y)
        else:
            put(0, first, key, 0, ends)
            put(0, first, key, cells_y - ends, ends)
            put(1, second, key, ends, cells_y - 2 * ends)
    return first, second, [-(-length // 8) * 8 for length in lengths]


def y_plan(cells_x):
    pieces = []
    start = 0
    inside = [(0, m) for m in range(cells_x // 2)] + [(a, x) for a in (1, 2) for x in range(cells_x)]
    chosen = [("inside", array, index, y_rows(0, array)) for array, index in inside]
    chosen += [("away", array, distance, y_rows(distance, array)) for array, distance, _ in side_entries()]
    for side, array, index, rows in chosen:
        pieces.append((side, array, index, rows, start))
        start += rows
    return pieces, -(-start // 8) * 8


def shifts(axis, step):
    count = lax.axis_size(axis)
    return [(i, i + step) for i in range(count) if 0 <= i + step < count]


def swap_pairs():
    return [(i, i ^ 1) for i in range(lax.axis_size("gx"))]


def x_pairs():
    count = lax.axis_size("gx")
    pairs = [(i, i + 1) for i in range(1, count - 1, 2)]
    return pairs + [(j, i) for i, j in pairs]


def inside_rows(member, own, partner, array, index, first, rows):
    cells_x = own[0].shape[0]
    here = pl.ds(first, rows)

    def plane(x):
        if x // cells_x == member:
            return own[array][x % cells_x, here, :]
        value = partner[array][x % cells_x, here, :]
        return value + value if array == 1 else value

    if array != 0:
        return plane(index)
    depth = own[0].shape[2]
    row = lax.broadcasted_iota(jnp.int32, (rows, depth), 0) + first
    lane = lax.broadcasted_iota(jnp.int32, (rows, depth), 1)
    return jnp.where(((row + lane) & 1) == 1, plane(2 * index), plane(2 * index + 1))


def for_member(body):
    me = lax.axis_index("gx") & 1
    for member in range(2):
        pl.when(me == member)(functools.partial(body, member))


def split_kernel(block, pp, pf, pk, first, second):
    cells_x, cells_y, _ = pp.shape
    p, f, k = views(block, cells_x)
    plans = x_plan(cells_y)

    def body(member):
        for plan, target in zip(plans, (first, second)):
            for (array, distance), pieces in plan.items():
                plane = 2 * cells_x - distance if member == 1 else distance - 1
                index = plane // 2 if array == 0 else plane
                for row, rows, start in pieces:
                    value = inside_rows(member, (p, f, k), (pp, pf, pk), array, index, row, rows)
                    target[pl.ds(start, rows), :] = value

    for_member(body)


def pack_kernel(block, received, to_up, to_down, far):
    cells_x, cells_y = block.shape[0] // 3, block.shape[1]
    own = views(block, cells_x)
    plan = x_plan(cells_y)[0]

    def piece(side, array, index, rows, row):
        if side == "inside":
            return inside_rows(0, own, None, array, index, row, rows)
        place = [s + row - r for r, count, s in plan[array, index] if r <= row and row + rows <= r + count][0]
        return received[pl.ds(place, rows), :]

    for side, array, index, rows, start in y_plan(cells_x)[0]:
        to_up[pl.ds(start, rows), :] = piece(side, array, index, rows, cells_y - rows)
        to_down[pl.ds(start, rows), :] = piece(side, array, index, rows, 0)
    far[0] = piece("away", 0, 1, cells_y, 0)
    far[1] = piece("away", 2, 1, cells_y, 0)


def stacked(pressure, source, coefficient):
    block = jnp.concatenate([pressure, source, coefficient], 0)
    cells_x = pressure.shape[0]
    plane = lax.broadcasted_iota(jnp.int32, block.shape, 0)
    return block * jnp.where((plane >= cells_x) & (plane < 2 * cells_x), 2.0, 1.0)


def views(block, cells_x):
    return tuple(block.at[pl.ds(n * cells_x, cells_x)] for n in range(3))


def fine_halo(own, block):
    cells_x, cells_y, depth = own[0].shape
    params = pltpu.CompilerParams(vmem_limit_bytes=VMEM_LIMIT)

    def packed(length):
        return jax.ShapeDtypeStruct((length, depth), jnp.float32)

    partner = tuple(lax.ppermute(v, "gx", swap_pairs()) for v in own)
    lengths = x_plan(cells_y)[2]
    first, second = pl.pallas_call(
        split_kernel, out_shape=[packed(n) for n in lengths], compiler_params=params, name="split_block"
    )(block, *partner)
    received = lax.ppermute(first, "gx", x_pairs())
    length = y_plan(cells_x)[1]
    planes = jax.ShapeDtypeStruct((2, cells_y, depth), jnp.float32)
    to_up, to_down, outermost = pl.pallas_call(
        pack_kernel, out_shape=[packed(length), packed(length), planes], compiler_params=params, name="pack_halo"
    )(block, received)
    below = lax.ppermute(to_up, "gy", shifts("gy", 1))
    above = lax.ppermute(to_down, "gy", shifts("gy", -1))
    far = lax.ppermute(outermost, "gx", swap_pairs())
    rest = lax.ppermute(second, "gx", x_pairs())
    below, above, far, rest = lax.optimization_barrier((below, above, far, rest))
    p_below = lax.ppermute(below, "gx", swap_pairs())
    p_above = lax.ppermute(above, "gx", swap_pairs())
    return *partner, received, rest, far, below, above, p_below, p_above


def smooth_kernel(
    block, pp, pf, pk, received, rest, far, below, above, p_below, p_above,
    out, error_one, tiles,
    vp, vf, vk, wx, wy, zl, zh, dg, inv, va, vb,
    t0, t1, f1, k1, inv1, g1, h1, q2,
):
    cells_x, cells_y, depth = pp.shape
    planes = cells_x + 2 * REACH
    own_rows = pl.ds(ORIGIN, cells_y)
    top = ORIGIN - REACH + 1
    rows = cells_y + 2 * (REACH - 1)
    body = pl.ds(top, rows)

    windows = (vp, vf, vk)
    first_plan, second_plan, _ = x_plan(cells_y)

    def fill(array, x, first, value):
        if x < -REACH or x >= cells_x + REACH or (array == 1 and (x == -REACH or x == cells_x + REACH - 1)):
            return
        windows[array][REACH + x, pl.ds(ORIGIN + first, value.shape[0]), :] = value

    for x in range(cells_x):
        for array, ref in enumerate(views(block, cells_x)):
            fill(array, x, 0, ref[x])

    spans = {(array, distance): distances for array, distance, distances in side_entries()}

    def outside(side, distance):
        return -distance if side == "low" else cells_x - 1 + distance

    def fill_member(member):
        away, near = (("low", "high"), ("high", "low"))[member]
        for x in range(cells_x):
            for array, ref in enumerate((pp, pf, pk)):
                value = ref[x]
                fill(array, x + cells_x * (1 - 2 * member), 0, value + value if array == 1 else value)
        fill(0, outside(near, REACH), 0, far[0])
        fill(2, outside(near, REACH), 0, far[1])
        for plan, ref in ((first_plan, received), (second_plan, rest)):
            for (array, distance), pieces in plan.items():
                for row, count, start in pieces:
                    value = ref[pl.ds(start, count), :]
                    for each in spans[array, distance]:
                        fill(array, outside(away, each), row, value)

        towards_partner = cells_x * (1 - 2 * member)
        for before, after, is_partner in ((below, above, False), (p_below, p_above, True)):
            for side, array, index, count, start in y_plan(cells_x)[0]:
                if side == "inside":
                    xs = (2 * index, 2 * index + 1) if array == 0 else (index,)
                    xs = [x + towards_partner * is_partner for x in xs]
                elif is_partner:
                    xs = [outside(near, cells_x + each) for each in spans[array, index]]
                else:
                    xs = [outside(away, each) for each in spans[array, index]]
                for x in xs:
                    fill(array, x, -count, before[pl.ds(start, count), :])
                    fill(array, x, cells_y, after[pl.ds(start, count), :])

    for_member(fill_member)

    def lanes(count):
        return lax.broadcasted_iota(jnp.int32, (count, depth), 1)

    def rows_of(first, count):
        return lax.broadcasted_iota(jnp.int32, (count, depth), 0) + (first - ORIGIN)

    lane = lanes(rows)

    def weigh(plane, _):
        centre = vk[plane, body, :]
        west = centre + vk[plane - 1, body, :]
        wx[plane, body, :] = west
        east = centre + vk[plane + 1, body, :]
        south = centre + vk[plane, pl.ds(top - 1, rows), :]
        north = centre + vk[plane, pl.ds(top + 1, rows), :]
        wy[plane, body, :] = south
        wy[plane, pl.ds(top + rows, 1), :] = north[rows - 1:, :]
        down = jnp.where(lane > 0, pltpu.roll(centre, 1, 1), 0.0)
        up = jnp.where(lane < depth - 1, pltpu.roll(centre, depth - 1, 1), 0.0)
        total = west + east + south + north + (centre + down) + (centre + up)
        zl[plane, body, :] = jnp.where(lane > 0, centre + down, 0.0)
        zh[plane, body, :] = jnp.where(lane < depth - 1, centre + up, 0.0)
        dg[plane, body, :] = total
        inside = centre > 0.0
        inv[plane, body, :] = jnp.where(inside, 1.0 / jnp.where(inside, total, 1.0), 0.0)
        return 0

    lax.fori_loop(1, planes - 1, weigh, 0, unroll=True)
    wx[planes - 1, body, :] = vk[planes - 1, body, :] + vk[planes - 2, body, :]

    def stencil(v, plane, first, count):
        here = pl.ds(first, count)
        centre = v[plane, here, :]
        total = wx[plane, here, :] * v[plane - 1, here, :] + wx[plane + 1, here, :] * v[plane + 1, here, :]
        total += wy[plane, here, :] * v[plane, pl.ds(first - 1, count), :]
        total += wy[plane, pl.ds(first + 1, count), :] * v[plane, pl.ds(first + 1, count), :]
        total += zl[plane, here, :] * pltpu.roll(centre, 1, 1)
        total += zh[plane, here, :] * pltpu.roll(centre, depth - 1, 1)
        return total

    def relax(source_ref, target, reach):
        def one(plane, _):
            total = stencil(source_ref, plane, top, rows)
            target[plane, body, :] = inv[plane, body, :] * (vf[plane, body, :] + total)
            return 0

        lax.fori_loop(REACH - reach, REACH + cells_x + reach, one, 0, unroll=True)

    relax(vp, va, REACH - 1)
    relax(va, vb, REACH - 2)
    relax(vb, va, REACH - 3)
    relax(va, vb, REACH - 4)

    own_lane = lanes(cells_y)
    own_row = rows_of(ORIGIN, cells_y)
    for x in range(cells_x):
        even = ((own_row + own_lane + x) & 1) == 0
        out[x] = jnp.where(even, va[REACH + x, own_rows, :], vb[REACH + x, own_rows, :])

    planes_one = cells_x // 2
    first = ORIGIN - 4
    count = cells_y + 8
    lane = lanes(count)
    row = rows_of(first, count)

    def pair_lane(value, stride, lane):
        up = pltpu.roll(value, depth - stride, 1)
        down = pltpu.roll(value, stride, 1)
        return value + jnp.where((lane & stride) == 0, up, down)

    def pair_row(ref, index, first, count, stride, row):
        centre = ref[index, pl.ds(first, count), :]
        up = ref[index, pl.ds(first + stride, count), :]
        down = ref[index, pl.ds(first - stride, count), :]
        return centre + jnp.where((row & stride) == 0, up, down)

    def residual(plane_one, _):
        total = jnp.zeros((count, depth), jnp.float32)
        for half in range(2):
            plane = 2 * plane_one + REACH - 4 + half
            here = pl.ds(first, count)
            twice = vf[plane, here, :] - dg[plane, here, :] * va[plane, here, :] + stencil(vb, plane, first, count)
            even = ((row + lane + half) & 1) == 0
            total += jnp.where(even, twice, 0.0)
        t0[plane_one, pl.ds(first, count), :] = pair_lane(total, 1, lane)
        return 0

    lax.fori_loop(0, planes_one + 4, residual, 0, unroll=True)
    for x in range(planes_one + 4):
        f1[x, pl.ds(first, count), :] = 0.5 * pair_row(t0, x, first, count, 1, row)

    first_k = ORIGIN - 6
    count_k = cells_y + 16
    lane_k = lanes(count_k)
    row_k = rows_of(first_k, count_k)
    for x in range(planes_one + 6):
        plane = 2 * x + REACH - 6
        here = pl.ds(first_k, count_k)
        t1[x, here, :] = pair_lane(vk[plane, here, :] + vk[plane + 1, here, :], 1, lane_k)
    for x in range(planes_one + 6):
        k1[x, pl.ds(first_k, count_k), :] = 0.125 * pair_row(t1, x, first_k, count_k, 1, row_k)

    def down2(value, lane):
        return jnp.where(lane >= 2, pltpu.roll(value, 2, 1), 0.0)

    def up2(value, lane):
        return jnp.where(lane < depth - 2, pltpu.roll(value, depth - 2, 1), 0.0)

    here = pl.ds(first, count)
    for x in range(planes_one + 4):
        centre = k1[x + 1, here, :]
        total = 6.0 * centre + (k1[x, here, :] + k1[x + 2, here, :])
        total += k1[x + 1, pl.ds(first - 2, count), :] + k1[x + 1, pl.ds(first + 2, count), :]
        total += down2(centre, lane) + up2(centre, lane)
        inside = centre > 0.0
        inverse = jnp.where(inside, 1.0 / jnp.where(inside, total, 1.0), 0.0)
        inv1[x, here, :] = inverse
        g1[x, here, :] = inverse * f1[x, here, :]

    def stencil_one(v, x, v_x, first, count, lane):
        here = pl.ds(first, count)
        south = pl.ds(first - 2, count)
        north = pl.ds(first + 2, count)
        kc = k1[x, here, :]
        vc = v[v_x, here, :]
        total = (kc + k1[x - 1, here, :]) * v[v_x - 1, here, :] + (kc + k1[x + 1, here, :]) * v[v_x + 1, here, :]
        total += (kc + k1[x, south, :]) * v[v_x, south, :] + (kc + k1[x, north, :]) * v[v_x, north, :]
        total += (kc + down2(kc, lane)) * down2(vc, lane) + (kc + up2(kc, lane)) * up2(vc, lane)
        return total

    first_h = ORIGIN - 2
    count_h = cells_y + 8
    lane_h = lanes(count_h)
    row_h = rows_of(first_h, count_h)
    for x in range(planes_one + 2):
        here = pl.ds(first_h, count_h)
        total = stencil_one(g1, x + 2, x + 1, first_h, count_h, lane_h)
        odd = inv1[x + 1, here, :] * (f1[x + 1, here, :] + total)
        h1[x, here, :] = odd
        even_cell = ((x - 1 + (row_h >> 1) + (lane_h >> 1)) & 1) == 0
        error_one[x, pl.ds(first_h - 8, count_h), :] = jnp.where(even_cell, g1[x + 1, here, :], odd)

    own2 = own_lane
    row2 = own_row
    for x in range(planes_one // 2):
        sum_r = jnp.zeros((cells_y, depth), jnp.float32)
        for half in range(2):
            x1 = 2 * x + half
            total = stencil_one(h1, x1 + 3, x1 + 1, ORIGIN, cells_y, own2)
            even_cell = ((x1 + (row2 >> 1) + (own2 >> 1)) & 1) == 0
            sum_r += jnp.where(even_cell, total, 0.0)
        sum_k = k1[2 * x + 3, own_rows, :] + k1[2 * x + 4, own_rows, :]
        t0[x, own_rows, :] = pair_lane(sum_r, 2, own2)
        t1[x, own_rows, :] = pair_lane(sum_k, 2, own2)
    lane8 = lanes(cells_y // 4)
    tile = jnp.zeros((cells_y // 4, depth), jnp.float32)
    for x in range(planes_one // 2):
        q2[0] = (1.0 / 64.0) * pair_row(t0, x, ORIGIN, cells_y, 2, row2)
        q2[1] = 0.125 * pair_row(t1, x, ORIGIN, cells_y, 2, row2)
        for field in range(2):
            kept = q2[field, pl.ds(0, cells_y // 4, stride=4), :]
            tile = jnp.where((lane8 & 3) == 2 * field + x, kept, tile)
    tiles[...] = jnp.broadcast_to(tile[None], tiles.shape)


def smooth(copies, block, halo):
    cells_x, cells_y, depth = halo[0].shape
    planes = cells_x + 2 * REACH
    tall = cells_y + 2 * ORIGIN
    planes_one = cells_x // 2
    window = pltpu.VMEM((planes, tall, depth), jnp.float32)

    def level_one(count):
        return pltpu.VMEM((count, tall, depth), jnp.float32)

    return pl.pallas_call(
        smooth_kernel,
        out_shape=(
            jax.ShapeDtypeStruct((cells_x, cells_y, depth), jnp.float32),
            jax.ShapeDtypeStruct((planes_one + 2, cells_y + 16, depth), jnp.float32),
            jax.ShapeDtypeStruct((copies, cells_y // 4, depth), jnp.float32),
        ),
        scratch_shapes=[window] * 11
        + [
            level_one(planes_one + 4),
            level_one(planes_one + 6),
            level_one(planes_one + 4),
            level_one(planes_one + 6),
            level_one(planes_one + 4),
            level_one(planes_one + 4),
            level_one(planes_one + 2),
            pltpu.VMEM((2, cells_y, depth), jnp.float32),
        ],
        compiler_params=pltpu.CompilerParams(vmem_limit_bytes=VMEM_LIMIT),
        name="smooth",
    )(block, *halo)


def ring(value, shift, axis):
    return pltpu.roll(value, shift % value.shape[axis], axis)


def before_x(v):
    return jnp.concatenate([jnp.zeros_like(v[:1]), v[:-1]], 0)


def after_x(v):
    return jnp.concatenate([v[1:], jnp.zeros_like(v[:1])], 0)


class Places:
    def __init__(self, shape):
        self.row = lax.broadcasted_iota(jnp.int32, shape, 1)
        self.lane = lax.broadcasted_iota(jnp.int32, shape, 2)
        self.part = self.lane & 3
        self.depth = shape[2]

    def before_y(self, v, stride):
        turned = ring(v, stride, 1)
        return jnp.where(self.row >= stride, turned, ring(turned, 1, 2))

    def after_y(self, v, stride):
        turned = ring(v, -stride, 1)
        return jnp.where(self.row < 8 - stride, turned, ring(turned, -1, 2))

    def has_before_y(self, stride):
        return (self.row >= stride) | (self.part > 0)

    def has_after_y(self, stride):
        return (self.row < 8 - stride) | (self.part < 3)

    def has_before_z(self, stride):
        return self.lane >= 4 * stride

    def has_after_z(self, stride):
        return self.lane < self.depth - 4 * stride


def whole_weights(k, places, stride):
    west = k + before_x(k)
    east = k + after_x(k)
    masks = (
        places.has_before_y(stride),
        places.has_after_y(stride),
        places.has_before_z(stride),
        places.has_after_z(stride),
    )
    near = (
        places.before_y(k, stride),
        places.after_y(k, stride),
        ring(k, 4 * stride, 2),
        ring(k, -4 * stride, 2),
    )
    diagonal = west + east
    weights = [west, east]
    for mask, value in zip(masks, near):
        diagonal += k + jnp.where(mask, value, 0.0)
        weights.append(jnp.where(mask, k + value, 0.0))
    return weights, diagonal


def whole_sum(v, weights, places, stride):
    total = weights[0] * before_x(v) + weights[1] * after_x(v)
    total += weights[2] * places.before_y(v, stride) + weights[3] * places.after_y(v, stride)
    total += weights[4] * ring(v, 4 * stride, 2) + weights[5] * ring(v, -4 * stride, 2)
    return total


def whole_solve(k2, rhs2):
    planes = k2.shape[0]
    places = Places(k2.shape)
    weights, diagonal = whole_weights(k2, places, 1)
    parity = lax.broadcasted_iota(jnp.int32, k2.shape, 0) + places.row + (places.lane >> 2)
    even = (parity & 1) == 0
    inverse = 1.0 / diagonal
    scaled = 32.0 * rhs2
    even_values = inverse * scaled
    odd_values = inverse * (scaled + whole_sum(even_values, weights, places, 1))
    error_two = jnp.where(even, even_values, odd_values)
    left = jnp.where(even, whole_sum(odd_values, weights, places, 1), 0.0)

    half = places.row[: planes // 2] , places.lane[: planes // 2]
    first_row = (half[0] & 1) == 0
    first_lane = (half[1] & 4) == 0

    def coarse(v):
        v = v.reshape(planes // 2, 2, *v.shape[1:])
        v = v[:, 0] + v[:, 1]
        v = v + jnp.where(first_row, ring(v, -1, 1), ring(v, 1, 1))
        return v + jnp.where(first_lane, ring(v, -4, 2), ring(v, 4, 2))

    remain = (1.0 / 256.0) * coarse(left)
    k3 = 0.125 * coarse(k2)
    places3 = Places(k3.shape)
    weights3, diagonal3 = whole_weights(k3, places3, 2)

    def total(v):
        return jnp.sum(jnp.sum(v, axis=0, keepdims=True), axis=(1, 2), keepdims=True)

    error = jnp.zeros_like(remain)
    direction = remain
    norm_now = total(remain * remain)
    for repeat in range(CSWEEPS):
        image = (diagonal3 * direction - whole_sum(direction, weights3, places3, 2)) * (1.0 / 128.0)
        alpha = norm_now / total(direction * image)
        error = error + alpha * direction
        if repeat == CSWEEPS - 1:
            break
        remain = remain - alpha * image
        norm_next = total(remain * remain)
        direction = remain + norm_next / norm_now * direction
        norm_now = norm_next

    lower = 0.75 * error + 0.25 * before_x(error)
    upper = 0.75 * error + 0.25 * after_x(error)
    fine = jnp.stack([lower, upper], 1).reshape(k2.shape)
    near = jnp.where(
        (places.row & 1) == 0,
        jnp.where(places.has_before_y(1), places.before_y(fine, 1), 0.0),
        jnp.where(places.has_after_y(1), places.after_y(fine, 1), 0.0),
    )
    fine = 0.75 * fine + 0.25 * near
    near = jnp.where(
        (places.lane & 4) == 0,
        jnp.where(places.has_before_z(1), ring(fine, 4, 2), 0.0),
        jnp.where(places.has_after_z(1), ring(fine, -4, 2), 0.0),
    )
    return error_two + (0.75 * fine + 0.25 * near)


def finish(grid, wide, smoothed, error_one, out, e1, e0):
    cells_x, cells_y, depth = smoothed.shape
    i, j = lax.axis_index("gx"), lax.axis_index("gy")
    first = 8 - 2
    count = cells_y + 8
    lane = lax.broadcasted_iota(jnp.int32, (count, depth), 1)
    row = lax.broadcasted_iota(jnp.int32, (count, depth), 0) - 2

    def widen_z(value, stride, lane):
        down = jnp.where(lane >= stride, pltpu.roll(value, stride, 1), 0.0)
        up = jnp.where(lane < depth - stride, pltpu.roll(value, depth - stride, 1), 0.0)
        return 0.75 * value + 0.25 * jnp.where((lane & stride) == 0, down, up)

    def widen_y(ref, index, first, count, stride, row):
        centre = ref[index, pl.ds(first, count), :]
        down = ref[index, pl.ds(first - stride, count), :]
        up = ref[index, pl.ds(first + stride, count), :]
        return 0.75 * centre + 0.25 * jnp.where((row & stride) == 0, down, up)

    low_row = jnp.where(j > 0, -cells_y, 0)
    high_row = jnp.where(j < grid[1] - 1, 2 * cells_y, cells_y)
    inside = (row >= low_row) & (row < high_row)
    planes_two = cells_x // 4 + 2
    mid = [widen_z(widen_y(wide, x, first, count, 2, row), 2, lane) for x in range(planes_two)]
    for x in range(cells_x // 2 + 2):
        centre = (x + 1) // 2
        near = centre + (1 if x % 2 == 0 else -1)
        value = jnp.where(inside, 0.75 * mid[centre] + 0.25 * mid[near], 0.0)
        if x == 0:
            value = jnp.where(i > 0, value, 0.0)
        if x == cells_x // 2 + 1:
            value = jnp.where(i < grid[0] - 1, value, 0.0)
        here = pl.ds(first, count)
        e1[x, here, :] = error_one[x, here, :] + value

    lane = lax.broadcasted_iota(jnp.int32, (cells_y, depth), 1)
    row = lax.broadcasted_iota(jnp.int32, (cells_y, depth), 0)
    for x in range(cells_x // 2 + 2):
        e0[x] = widen_z(widen_y(e1, x, 8, cells_y, 1, row), 1, lane)
    for x in range(cells_x):
        centre = x // 2 + 1
        near = centre + (-1 if x % 2 == 0 else 1)
        out[x] = smoothed[x] + (0.75 * e0[centre] + 0.25 * e0[near])


def correct_kernel(grid, gathered, smoothed, error_one, out, whole, strip, wide, e1, e0):
    cells_y = smoothed.shape[1]
    nx, ny = grid
    i, j = lax.axis_index("gx"), lax.axis_index("gy")
    lane = lax.broadcasted_iota(jnp.int32, (8, 128), 1) & 3
    fields = [[], []]
    for column in range(nx):
        parts = [gathered[column * ny + part] for part in range(ny)]
        for field in range(2):
            for x in range(2):
                place = 2 * field + x
                plane = None
                for part in range(ny):
                    turned = parts[part] if part == place else ring(parts[part], part - place, 1)
                    plane = turned if plane is None else jnp.where(lane == part, turned, plane)
                fields[field].append(plane)
    rhs2 = jnp.stack(fields[0], 0)
    k2 = jnp.stack(fields[1], 0)
    planes = 2 * nx
    whole[0] = jnp.zeros((8, 128), jnp.float32)
    whole[planes + 1] = jnp.zeros((8, 128), jnp.float32)
    whole[pl.ds(1, planes)] = whole_solve(k2, rhs2)

    for x in range(4):
        centre = pltpu.roll(whole[2 * i + x], lax.rem(128 - j, 128), 1)
        below = jnp.where(j > 0, ring(centre, 1, 1), 0.0)
        above = jnp.where(j < ny - 1, ring(centre, -1, 1), 0.0)
        for index, value in enumerate((below, centre, above)):
            value = jnp.where(lane == 0, value, 0.0)
            value = value + ring(value, 1, 1)
            strip[x, pl.ds(8 * index, 8), :] = value + ring(value, 2, 1)
        for place in range(4):
            wide[x, pl.ds(4 + place, 8, stride=4), :] = strip[x, pl.ds(7, 8), :]
            wide[x, pl.ds(36 + place, 2, stride=4), :] = strip[x, pl.ds(15, 2), :]
    finish(grid, wide, smoothed, error_one, out, e1, e0)


def finish_kernel(grid, wide, smoothed, error_one, out, e1, e0):
    finish(grid, wide, smoothed, error_one, out, e1, e0)


def last_scratch(cells_x, cells_y, depth):
    count = cells_x // 2 + 2
    return [
        pltpu.VMEM((count, cells_y + 16, depth), jnp.float32),
        pltpu.VMEM((count, cells_y, depth), jnp.float32),
    ]


def correct_whole(grid, tiles, smoothed, error_one):
    gathered = lax.all_to_all(tiles, ("gx", "gy"), 0, 0, tiled=False)
    cells_x, cells_y, depth = smoothed.shape
    return pl.pallas_call(
        functools.partial(correct_kernel, grid),
        out_shape=jax.ShapeDtypeStruct(smoothed.shape, jnp.float32),
        scratch_shapes=[
            pltpu.VMEM((2 * grid[0] + 2, 8, depth), jnp.float32),
            pltpu.VMEM((4, 24, depth), jnp.float32),
            pltpu.VMEM((4, cells_y + 16, depth), jnp.float32),
        ]
        + last_scratch(cells_x, cells_y, depth),
        compiler_params=pltpu.CompilerParams(vmem_limit_bytes=VMEM_LIMIT),
        name="correct",
    )(gathered, smoothed, error_one)


def with_faces(shard):
    for axis, dim in (("gx", 0), ("gy", 1)):
        length = shard.shape[dim]
        last = lax.slice_in_dim(shard, length - 1, length, axis=dim)
        initial = lax.slice_in_dim(shard, 0, 1, axis=dim)
        before = lax.ppermute(last, axis, shifts(axis, 1))
        after = lax.ppermute(initial, axis, shifts(axis, -1))
        shard = jnp.concatenate([before, shard, after], axis=dim)
    return shard


def with_zeros(field):
    return jnp.pad(field, ((1, 1), (1, 1), (0, 0)))


def pad_depth(field):
    return jnp.pad(field, ((0, 0), (0, 0), (1, 1)))


def restrict(field):
    size_x, size_y, size_z = field.shape
    return field.reshape(size_x // 2, 2, size_y // 2, 2, size_z // 2, 2).mean(axis=(1, 3, 5))


def level_weights(coef_pad):
    c = pad_depth(coef_pad)
    wx = (c[1:, 1:-1, 1:-1] + c[:-1, 1:-1, 1:-1]) * 0.5
    wy = (c[1:-1, 1:, 1:-1] + c[1:-1, :-1, 1:-1]) * 0.5
    wz = (c[1:-1, 1:-1, 1:] + c[1:-1, 1:-1, :-1]) * 0.5
    diagonal = wx[1:] + wx[:-1] + wy[:, 1:] + wy[:, :-1] + wz[:, :, 1:] + wz[:, :, :-1]
    return (wx, wy, wz), diagonal


def neighbour_sum(field_pad, weights):
    wx, wy, wz = weights
    v = pad_depth(field_pad)
    total = wx[:-1] * v[:-2, 1:-1, 1:-1] + wx[1:] * v[2:, 1:-1, 1:-1]
    total = total + wy[:, :-1] * v[1:-1, :-2, 1:-1] + wy[:, 1:] * v[1:-1, 2:, 1:-1]
    return total + wz[:, :, :-1] * v[1:-1, 1:-1, :-2] + wz[:, :, 1:] * v[1:-1, 1:-1, 2:]


def prolong_axis(padded, axis):
    length = padded.shape[axis]
    middle = lax.slice_in_dim(padded, 1, length - 1, axis=axis)
    before = lax.slice_in_dim(padded, 0, length - 2, axis=axis)
    after = lax.slice_in_dim(padded, 2, length, axis=axis)
    joined = jnp.stack([0.75 * middle + 0.25 * before, 0.75 * middle + 0.25 * after], axis=axis + 1)
    shape = list(middle.shape)
    shape[axis] = 2 * shape[axis]
    return joined.reshape(shape)


def coarse_solve(rhs, weights, diagonal):
    error = jnp.zeros_like(rhs)
    remain = rhs
    direction = rhs
    norm_now = jnp.sum(remain * remain)
    for _ in range(CSWEEPS):
        image = (diagonal * direction - neighbour_sum(with_zeros(direction), weights)) * 4.0**-3
        alpha = norm_now / jnp.sum(direction * image)
        error = error + alpha * direction
        remain = remain - alpha * image
        norm_next = jnp.sum(remain * remain)
        direction = remain + norm_next / norm_now * direction
        norm_now = norm_next
    return error


def correct_spread(grid, tiles, smoothed, error_one):
    cells_x, cells_y, depth = smoothed.shape
    shape2 = (cells_x // 4, cells_y // 4, depth // 4)
    own = tiles[0].reshape(shape2[1], shape2[2], 2, shape2[0]).transpose(2, 3, 0, 1)
    rhs2, k2 = own[0], own[1]
    weights, diagonal = level_weights(with_faces(k2))
    parity = sum(lax.broadcasted_iota(jnp.int32, shape2, d) for d in range(3)) % 2
    error_two = jnp.where(parity == 0, rhs2 * 16.0 / diagonal, 0.0)
    total = neighbour_sum(with_faces(error_two), weights)
    error_two = jnp.where(parity == 1, (rhs2 * 16.0 + total) / diagonal, error_two)
    total = neighbour_sum(with_faces(error_two), weights)
    rhs3 = restrict(rhs2 - (diagonal * error_two - total) * 4.0**-2)
    merged = jnp.stack([rhs3, restrict(k2)])
    merged = lax.all_gather(merged, "gx", axis=1, tiled=True)
    merged = lax.all_gather(merged, "gy", axis=2, tiled=True)
    weights3, diagonal3 = level_weights(with_zeros(merged[1]))
    error_three = coarse_solve(merged[0], weights3, diagonal3)
    start_x = lax.axis_index("gx") * rhs3.shape[0]
    start_y = lax.axis_index("gy") * rhs3.shape[1]
    window = lax.dynamic_slice(
        with_zeros(error_three),
        (start_x, start_y, jnp.int32(0)),
        (rhs3.shape[0] + 2, rhs3.shape[1] + 2, rhs3.shape[2]),
    )
    finer = pad_depth(window)
    for axis in range(3):
        finer = prolong_axis(finer, axis)
    wide = with_faces(error_two + finer)
    wide = jnp.repeat(jnp.repeat(wide, 4, axis=1), 4, axis=2)
    wide = jnp.pad(wide, ((0, 0), (4, 4), (0, 0)))
    return pl.pallas_call(
        functools.partial(finish_kernel, grid),
        out_shape=jax.ShapeDtypeStruct(smoothed.shape, jnp.float32),
        scratch_shapes=last_scratch(cells_x, cells_y, depth),
        compiler_params=pltpu.CompilerParams(vmem_limit_bytes=VMEM_LIMIT),
        name="finish",
    )(wide, smoothed, error_one)


def on_device(pressure, source, coefficient):
    grid = (lax.axis_size("gx"), lax.axis_size("gy"))
    _, cells_y, depth = pressure.shape
    fits = grid[1] == 4 and cells_y == 32 and depth == 128
    own = (pressure, source, coefficient)
    block = stacked(*own)
    halo = fine_halo(own, block)
    copies = grid[0] * grid[1] if fits else 1
    smoothed, error_one, tiles = smooth(copies, block, halo)
    correct = correct_whole if fits else correct_spread
    return correct(grid, tiles, smoothed, error_one)


def solution(mesh):
    spec = P("gx", "gy", None)
    return jax.shard_map(on_device, mesh=mesh, in_specs=(spec, spec, spec), out_specs=spec, check_vma=False)
```

```python
import functools
import jax
import jax.numpy as jnp
from jax import lax
from jax.experimental import pallas as pl
from jax.experimental.pallas import tpu as pltpu
from jax.sharding import PartitionSpec as P

CSWEEPS = 4
REACH = 9
ORIGIN = 16
VMEM_LIMIT = 48 * 1024 * 1024


def y_rows(distance, array):
    rows = REACH if distance <= 2 else REACH + 2 - distance
    return rows - 1 if array == 1 else rows


def side_entries():
    pairs = [(0, d, (d, d + 1)) for d in range(1, REACH - 1, 2)] + [(0, REACH, (REACH,))]
    return pairs + [(1, d, (d,)) for d in range(1, REACH)] + [(2, d, (d,)) for d in range(1, REACH + 1)]


def x_plan(cells_y):
    first, second = {}, {}
    lengths = [0, 0]

    def put(message, plan, key, row, rows):
        plan.setdefault(key, []).append((row, rows, lengths[message]))
        lengths[message] += rows

    for array, distance, _ in side_entries():
        key = (array, distance)
        ends = y_rows(distance, array)
        if array != 1 and distance == 1:
            put(0, first, key, 0, cells_y)
        else:
            put(0, first, key, 0, ends)
            put(0, first, key, cells_y - ends, ends)
            put(1, second, key, ends, cells_y - 2 * ends)
    return first, second, [-(-length // 8) * 8 for length in lengths]


def y_plan(cells_x):
    pieces = []
    start = 0
    inside = [(0, m) for m in range(cells_x // 2)] + [(a, x) for a in (1, 2) for x in range(cells_x)]
    chosen = [("inside", array, index, y_rows(0, array)) for array, index in inside]
    chosen += [("away", array, distance, y_rows(distance, array)) for array, distance, _ in side_entries()]
    for side, array, index, rows in chosen:
        pieces.append((side, array, index, rows, start))
        start += rows
    return pieces, -(-start // 8) * 8


def shifts(axis, step):
    count = lax.axis_size(axis)
    return [(i, i + step) for i in range(count) if 0 <= i + step < count]


def swap_pairs():
    return [(i, i ^ 1) for i in range(lax.axis_size("gx"))]


def x_pairs():
    count = lax.axis_size("gx")
    pairs = [(i, i + 1) for i in range(1, count - 1, 2)]
    return pairs + [(j, i) for i, j in pairs]


def inside_rows(member, own, partner, array, index, first, rows):
    cells_x = own[0].shape[0]
    here = pl.ds(first, rows)

    def plane(x):
        if x // cells_x == member:
            return own[array][x % cells_x, here, :]
        value = partner[array][x % cells_x, here, :]
        return value + value if array == 1 else value

    if array != 0:
        return plane(index)
    depth = own[0].shape[2]
    row = lax.broadcasted_iota(jnp.int32, (rows, depth), 0) + first
    lane = lax.broadcasted_iota(jnp.int32, (rows, depth), 1)
    return jnp.where(((row + lane) & 1) == 1, plane(2 * index), plane(2 * index + 1))


def for_member(body):
    me = lax.axis_index("gx") & 1
    for member in range(2):
        pl.when(me == member)(functools.partial(body, member))


def split_kernel(block, pp, pf, pk, first, second):
    cells_x, cells_y, _ = pp.shape
    p, f, k = views(block, cells_x)
    plans = x_plan(cells_y)

    def body(member):
        for plan, target in zip(plans, (first, second)):
            for (array, distance), pieces in plan.items():
                plane = 2 * cells_x - distance if member == 1 else distance - 1
                index = plane // 2 if array == 0 else plane
                for row, rows, start in pieces:
                    value = inside_rows(member, (p, f, k), (pp, pf, pk), array, index, row, rows)
                    target[pl.ds(start, rows), :] = value

    for_member(body)


def pack_kernel(block, received, to_up, to_down, far):
    cells_x, cells_y = block.shape[0] // 3, block.shape[1]
    own = views(block, cells_x)
    plan = x_plan(cells_y)[0]

    def piece(side, array, index, rows, row):
        if side == "inside":
            return inside_rows(0, own, None, array, index, row, rows)
        place = [s + row - r for r, count, s in plan[array, index] if r <= row and row + rows <= r + count][0]
        return received[pl.ds(place, rows), :]

    for side, array, index, rows, start in y_plan(cells_x)[0]:
        to_up[pl.ds(start, rows), :] = piece(side, array, index, rows, cells_y - rows)
        to_down[pl.ds(start, rows), :] = piece(side, array, index, rows, 0)
    far[0] = piece("away", 0, 1, cells_y, 0)
    far[1] = piece("away", 2, 1, cells_y, 0)


def stacked(pressure, source, coefficient):
    block = jnp.concatenate([pressure, source, coefficient], 0)
    cells_x = pressure.shape[0]
    plane = lax.broadcasted_iota(jnp.int32, block.shape, 0)
    return block * jnp.where((plane >= cells_x) & (plane < 2 * cells_x), 2.0, 1.0)


def views(block, cells_x):
    return tuple(block.at[pl.ds(n * cells_x, cells_x)] for n in range(3))


def fine_halo(own, block):
    cells_x, cells_y, depth = own[0].shape
    params = pltpu.CompilerParams(vmem_limit_bytes=VMEM_LIMIT)

    def packed(length):
        return jax.ShapeDtypeStruct((length, depth), jnp.float32)

    partner = tuple(lax.ppermute(v, "gx", swap_pairs()) for v in own)
    lengths = x_plan(cells_y)[2]
    first, second = pl.pallas_call(
        split_kernel, out_shape=[packed(n) for n in lengths], compiler_params=params, name="split_block"
    )(block, *partner)
    received = lax.ppermute(first, "gx", x_pairs())
    length = y_plan(cells_x)[1]
    planes = jax.ShapeDtypeStruct((2, cells_y, depth), jnp.float32)
    to_up, to_down, outermost = pl.pallas_call(
        pack_kernel, out_shape=[packed(length), packed(length), planes], compiler_params=params, name="pack_halo"
    )(block, received)
    below = lax.ppermute(to_up, "gy", shifts("gy", 1))
    above = lax.ppermute(to_down, "gy", shifts("gy", -1))
    far = lax.ppermute(outermost, "gx", swap_pairs())
    rest = lax.ppermute(second, "gx", x_pairs())
    below, above, far, rest = lax.optimization_barrier((below, above, far, rest))
    p_below = lax.ppermute(below, "gx", swap_pairs())
    p_above = lax.ppermute(above, "gx", swap_pairs())
    return *partner, received, rest, far, below, above, p_below, p_above


def smooth_kernel(
    block, pp, pf, pk, received, rest, far, below, above, p_below, p_above,
    out, error_one, tiles,
    vp, vf, vk, wx, wy, zl, zh, dg, inv, va, vb,
    t0, t1, f1, k1, inv1, g1, h1, q2,
):
    cells_x, cells_y, depth = pp.shape
    planes = cells_x + 2 * REACH
    own_rows = pl.ds(ORIGIN, cells_y)
    top = ORIGIN - REACH + 1
    rows = cells_y + 2 * (REACH - 1)
    body = pl.ds(top, rows)

    windows = (vp, vf, vk)
    first_plan, second_plan, _ = x_plan(cells_y)

    def fill(array, x, first, value):
        if x < -REACH or x >= cells_x + REACH or (array == 1 and (x == -REACH or x == cells_x + REACH - 1)):
            return
        windows[array][REACH + x, pl.ds(ORIGIN + first, value.shape[0]), :] = value

    for x in range(cells_x):
        for array, ref in enumerate(views(block, cells_x)):
            fill(array, x, 0, ref[x])

    spans = {(array, distance): distances for array, distance, distances in side_entries()}

    def outside(side, distance):
        return -distance if side == "low" else cells_x - 1 + distance

    def fill_member(member):
        away, near = (("low", "high"), ("high", "low"))[member]
        for x in range(cells_x):
            for array, ref in enumerate((pp, pf, pk)):
                value = ref[x]
                fill(array, x + cells_x * (1 - 2 * member), 0, value + value if array == 1 else value)
        fill(0, outside(near, REACH), 0, far[0])
        fill(2, outside(near, REACH), 0, far[1])
        for plan, ref in ((first_plan, received), (second_plan, rest)):
            for (array, distance), pieces in plan.items():
                for row, count, start in pieces:
                    value = ref[pl.ds(start, count), :]
                    for each in spans[array, distance]:
                        fill(array, outside(away, each), row, value)

        towards_partner = cells_x * (1 - 2 * member)
        for before, after, is_partner in ((below, above, False), (p_below, p_above, True)):
            for side, array, index, count, start in y_plan(cells_x)[0]:
                if side == "inside":
                    xs = (2 * index, 2 * index + 1) if array == 0 else (index,)
                    xs = [x + towards_partner * is_partner for x in xs]
                elif is_partner:
                    xs = [outside(near, cells_x + each) for each in spans[array, index]]
                else:
                    xs = [outside(away, each) for each in spans[array, index]]
                for x in xs:
                    fill(array, x, -count, before[pl.ds(start, count), :])
                    fill(array, x, cells_y, after[pl.ds(start, count), :])

    for_member(fill_member)

    def lanes(count):
        return lax.broadcasted_iota(jnp.int32, (count, depth), 1)

    def rows_of(first, count):
        return lax.broadcasted_iota(jnp.int32, (count, depth), 0) + (first - ORIGIN)

    lane = lanes(rows)

    def weigh(plane, _):
        centre = vk[plane, body, :]
        west = centre + vk[plane - 1, body, :]
        wx[plane, body, :] = west
        east = centre + vk[plane + 1, body, :]
        south = centre + vk[plane, pl.ds(top - 1, rows), :]
        north = centre + vk[plane, pl.ds(top + 1, rows), :]
        wy[plane, body, :] = south
        wy[plane, pl.ds(top + rows, 1), :] = north[rows - 1:, :]
        down = jnp.where(lane > 0, pltpu.roll(centre, 1, 1), 0.0)
        up = jnp.where(lane < depth - 1, pltpu.roll(centre, depth - 1, 1), 0.0)
        total = west + east + south + north + (centre + down) + (centre + up)
        zl[plane, body, :] = jnp.where(lane > 0, centre + down, 0.0)
        zh[plane, body, :] = jnp.where(lane < depth - 1, centre + up, 0.0)
        dg[plane, body, :] = total
        inside = centre > 0.0
        inv[plane, body, :] = jnp.where(inside, 1.0 / jnp.where(inside, total, 1.0), 0.0)
        return 0

    lax.fori_loop(1, planes - 1, weigh, 0, unroll=True)
    wx[planes - 1, body, :] = vk[planes - 1, body, :] + vk[planes - 2, body, :]

    def stencil(v, plane, first, count):
        here = pl.ds(first, count)
        centre = v[plane, here, :]
        total = wx[plane, here, :] * v[plane - 1, here, :] + wx[plane + 1, here, :] * v[plane + 1, here, :]
        total += wy[plane, here, :] * v[plane, pl.ds(first - 1, count), :]
        total += wy[plane, pl.ds(first + 1, count), :] * v[plane, pl.ds(first + 1, count), :]
        total += zl[plane, here, :] * pltpu.roll(centre, 1, 1)
        total += zh[plane, here, :] * pltpu.roll(centre, depth - 1, 1)
        return total

    def relax(source_ref, target, reach):
        def one(plane, _):
            total = stencil(source_ref, plane, top, rows)
            target[plane, body, :] = inv[plane, body, :] * (vf[plane, body, :] + total)
            return 0

        lax.fori_loop(REACH - reach, REACH + cells_x + reach, one, 0, unroll=True)

    relax(vp, va, REACH - 1)
    relax(va, vb, REACH - 2)
    relax(vb, va, REACH - 3)
    relax(va, vb, REACH - 4)

    own_lane = lanes(cells_y)
    own_row = rows_of(ORIGIN, cells_y)
    for x in range(cells_x):
        even = ((own_row + own_lane + x) & 1) == 0
        out[x] = jnp.where(even, va[REACH + x, own_rows, :], vb[REACH + x, own_rows, :])

    planes_one = cells_x // 2
    first = ORIGIN - 4
    count = cells_y + 8
    lane = lanes(count)
    row = rows_of(first, count)

    def pair_lane(value, stride, lane):
        up = pltpu.roll(value, depth - stride, 1)
        down = pltpu.roll(value, stride, 1)
        return value + jnp.where((lane & stride) == 0, up, down)

    def pair_row(ref, index, first, count, stride, row):
        centre = ref[index, pl.ds(first, count), :]
        up = ref[index, pl.ds(first + stride, count), :]
        down = ref[index, pl.ds(first - stride, count), :]
        return centre + jnp.where((row & stride) == 0, up, down)

    def residual(plane_one, _):
        total = jnp.zeros((count, depth), jnp.float32)
        for half in range(2):
            plane = 2 * plane_one + REACH - 4 + half
            here = pl.ds(first, count)
            twice = vf[plane, here, :] - dg[plane, here, :] * va[plane, here, :] + stencil(vb, plane, first, count)
            even = ((row + lane + half) & 1) == 0
            total += jnp.where(even, twice, 0.0)
        t0[plane_one, pl.ds(first, count), :] = pair_lane(total, 1, lane)
        return 0

    lax.fori_loop(0, planes_one + 4, residual, 0, unroll=True)
    for x in range(planes_one + 4):
        f1[x, pl.ds(first, count), :] = 0.5 * pair_row(t0, x, first, count, 1, row)

    first_k = ORIGIN - 6
    count_k = cells_y + 16
    lane_k = lanes(count_k)
    row_k = rows_of(first_k, count_k)
    for x in range(planes_one + 6):
        plane = 2 * x + REACH - 6
        here = pl.ds(first_k, count_k)
        t1[x, here, :] = pair_lane(vk[plane, here, :] + vk[plane + 1, here, :], 1, lane_k)
    for x in range(planes_one + 6):
        k1[x, pl.ds(first_k, count_k), :] = 0.125 * pair_row(t1, x, first_k, count_k, 1, row_k)

    def down2(value, lane):
        return jnp.where(lane >= 2, pltpu.roll(value, 2, 1), 0.0)

    def up2(value, lane):
        return jnp.where(lane < depth - 2, pltpu.roll(value, depth - 2, 1), 0.0)

    here = pl.ds(first, count)
    for x in range(planes_one + 4):
        centre = k1[x + 1, here, :]
        total = 6.0 * centre + (k1[x, here, :] + k1[x + 2, here, :])
        total += k1[x + 1, pl.ds(first - 2, count), :] + k1[x + 1, pl.ds(first + 2, count), :]
        total += down2(centre, lane) + up2(centre, lane)
        inside = centre > 0.0
        inverse = jnp.where(inside, 1.0 / jnp.where(inside, total, 1.0), 0.0)
        inv1[x, here, :] = inverse
        g1[x, here, :] = inverse * f1[x, here, :]

    def stencil_one(v, x, v_x, first, count, lane):
        here = pl.ds(first, count)
        south = pl.ds(first - 2, count)
        north = pl.ds(first + 2, count)
        kc = k1[x, here, :]
        vc = v[v_x, here, :]
        total = (kc + k1[x - 1, here, :]) * v[v_x - 1, here, :] + (kc + k1[x + 1, here, :]) * v[v_x + 1, here, :]
        total += (kc + k1[x, south, :]) * v[v_x, south, :] + (kc + k1[x, north, :]) * v[v_x, north, :]
        total += (kc + down2(kc, lane)) * down2(vc, lane) + (kc + up2(kc, lane)) * up2(vc, lane)
        return total

    first_h = ORIGIN - 2
    count_h = cells_y + 8
    lane_h = lanes(count_h)
    row_h = rows_of(first_h, count_h)
    for x in range(planes_one + 2):
        here = pl.ds(first_h, count_h)
        total = stencil_one(g1, x + 2, x + 1, first_h, count_h, lane_h)
        odd = inv1[x + 1, here, :] * (f1[x + 1, here, :] + total)
        h1[x, here, :] = odd
        even_cell = ((x - 1 + (row_h >> 1) + (lane_h >> 1)) & 1) == 0
        error_one[x, pl.ds(first_h - 8, count_h), :] = jnp.where(even_cell, g1[x + 1, here, :], odd)

    own2 = own_lane
    row2 = own_row
    for x in range(planes_one // 2):
        sum_r = jnp.zeros((cells_y, depth), jnp.float32)
        for half in range(2):
            x1 = 2 * x + half
            total = stencil_one(h1, x1 + 3, x1 + 1, ORIGIN, cells_y, own2)
            even_cell = ((x1 + (row2 >> 1) + (own2 >> 1)) & 1) == 0
            sum_r += jnp.where(even_cell, total, 0.0)
        sum_k = k1[2 * x + 3, own_rows, :] + k1[2 * x + 4, own_rows, :]
        t0[x, own_rows, :] = pair_lane(sum_r, 2, own2)
        t1[x, own_rows, :] = pair_lane(sum_k, 2, own2)
    lane8 = lanes(cells_y // 4)
    tile = jnp.zeros((cells_y // 4, depth), jnp.float32)
    for x in range(planes_one // 2):
        q2[0] = (1.0 / 64.0) * pair_row(t0, x, ORIGIN, cells_y, 2, row2)
        q2[1] = 0.125 * pair_row(t1, x, ORIGIN, cells_y, 2, row2)
        for field in range(2):
            kept = q2[field, pl.ds(0, cells_y // 4, stride=4), :]
            tile = jnp.where((lane8 & 3) == 2 * field + x, kept, tile)
    tiles[...] = jnp.broadcast_to(tile[None], tiles.shape)


def smooth(copies, block, halo):
    cells_x, cells_y, depth = halo[0].shape
    planes = cells_x + 2 * REACH
    tall = cells_y + 2 * ORIGIN
    planes_one = cells_x // 2
    window = pltpu.VMEM((planes, tall, depth), jnp.float32)

    def level_one(count):
        return pltpu.VMEM((count, tall, depth), jnp.float32)

    return pl.pallas_call(
        smooth_kernel,
        out_shape=(
            jax.ShapeDtypeStruct((cells_x, cells_y, depth), jnp.float32),
            jax.ShapeDtypeStruct((planes_one + 2, cells_y + 16, depth), jnp.float32),
            jax.ShapeDtypeStruct((copies, cells_y // 4, depth), jnp.float32),
        ),
        scratch_shapes=[window] * 11
        + [
            level_one(planes_one + 4),
            level_one(planes_one + 6),
            level_one(planes_one + 4),
            level_one(planes_one + 6),
            level_one(planes_one + 4),
            level_one(planes_one + 4),
            level_one(planes_one + 2),
            pltpu.VMEM((2, cells_y, depth), jnp.float32),
        ],
        compiler_params=pltpu.CompilerParams(vmem_limit_bytes=VMEM_LIMIT),
        name="smooth",
    )(block, *halo)


def ring(value, shift, axis):
    return pltpu.roll(value, shift % value.shape[axis], axis)


def before_x(v):
    return jnp.concatenate([jnp.zeros_like(v[:1]), v[:-1]], 0)


def after_x(v):
    return jnp.concatenate([v[1:], jnp.zeros_like(v[:1])], 0)


class Places:
    def __init__(self, shape):
        self.row = lax.broadcasted_iota(jnp.int32, shape, 1)
        self.lane = lax.broadcasted_iota(jnp.int32, shape, 2)
        self.part = self.lane & 3
        self.depth = shape[2]

    def before_y(self, v, stride):
        turned = ring(v, stride, 1)
        return jnp.where(self.row >= stride, turned, ring(turned, 1, 2))

    def after_y(self, v, stride):
        turned = ring(v, -stride, 1)
        return jnp.where(self.row < 8 - stride, turned, ring(turned, -1, 2))

    def has_before_y(self, stride):
        return (self.row >= stride) | (self.part > 0)

    def has_after_y(self, stride):
        return (self.row < 8 - stride) | (self.part < 3)

    def has_before_z(self, stride):
        return self.lane >= 4 * stride

    def has_after_z(self, stride):
        return self.lane < self.depth - 4 * stride


def whole_weights(k, places, stride):
    west = k + before_x(k)
    east = k + after_x(k)
    masks = (
        places.has_before_y(stride),
        places.has_after_y(stride),
        places.has_before_z(stride),
        places.has_after_z(stride),
    )
    near = (
        places.before_y(k, stride),
        places.after_y(k, stride),
        ring(k, 4 * stride, 2),
        ring(k, -4 * stride, 2),
    )
    diagonal = west + east
    weights = [west, east]
    for mask, value in zip(masks, near):
        diagonal += k + jnp.where(mask, value, 0.0)
        weights.append(jnp.where(mask, k + value, 0.0))
    return weights, diagonal


def whole_sum(v, weights, places, stride):
    total = weights[0] * before_x(v) + weights[1] * after_x(v)
    total += weights[2] * places.before_y(v, stride) + weights[3] * places.after_y(v, stride)
    total += weights[4] * ring(v, 4 * stride, 2) + weights[5] * ring(v, -4 * stride, 2)
    return total


def whole_solve(k2, rhs2):
    planes = k2.shape[0]
    places = Places(k2.shape)
    weights, diagonal = whole_weights(k2, places, 1)
    parity = lax.broadcasted_iota(jnp.int32, k2.shape, 0) + places.row + (places.lane >> 2)
    even = (parity & 1) == 0
    inverse = 1.0 / diagonal
    scaled = 32.0 * rhs2
    even_values = inverse * scaled
    odd_values = inverse * (scaled + whole_sum(even_values, weights, places, 1))
    error_two = jnp.where(even, even_values, odd_values)
    left = jnp.where(even, whole_sum(odd_values, weights, places, 1), 0.0)

    half = places.row[: planes // 2] , places.lane[: planes // 2]
    first_row = (half[0] & 1) == 0
    first_lane = (half[1] & 4) == 0

    def coarse(v):
        v = v.reshape(planes // 2, 2, *v.shape[1:])
        v = v[:, 0] + v[:, 1]
        v = v + jnp.where(first_row, ring(v, -1, 1), ring(v, 1, 1))
        return v + jnp.where(first_lane, ring(v, -4, 2), ring(v, 4, 2))

    remain = (1.0 / 256.0) * coarse(left)
    k3 = 0.125 * coarse(k2)
    places3 = Places(k3.shape)
    weights3, diagonal3 = whole_weights(k3, places3, 2)

    def total(v):
        return jnp.sum(jnp.sum(v, axis=0, keepdims=True), axis=(1, 2), keepdims=True)

    def around(v):
        return (
            places3.before_y(v, 2), places3.after_y(v, 2), ring(v, 8, 2), ring(v, -8, 2),
        )

    direction, sides = remain, around(remain)
    remain_sides = sides
    norm_now = total(remain * remain)
    error = error_before = error_after = jnp.zeros_like(remain)
    for repeat in range(CSWEEPS):
        coupled = weights3[0] * before_x(direction) + weights3[1] * after_x(direction)
        coupled += weights3[2] * sides[0] + weights3[3] * sides[1]
        coupled += weights3[4] * sides[2] + weights3[5] * sides[3]
        image = (diagonal3 * direction - coupled) * (1.0 / 128.0)
        alpha = norm_now / total(direction * image)
        error = error + alpha * direction
        error_before = error_before + alpha * sides[0]
        error_after = error_after + alpha * sides[1]
        if repeat == CSWEEPS - 1:
            break
        image_sides = around(image)
        remain = remain - alpha * image
        remain_sides = [r - alpha * q for r, q in zip(remain_sides, image_sides)]
        norm_next = total(remain * remain)
        beta = norm_next / norm_now
        direction = remain + beta * direction
        sides = [r + beta * p for r, p in zip(remain_sides, sides)]
        norm_now = norm_next

    near = jnp.where(
        first_row,
        jnp.where(places3.has_before_y(2), error_before, 0.0),
        jnp.where(places3.has_after_y(2), error_after, 0.0),
    )
    error = 0.75 * error + 0.25 * near
    lower = 0.75 * error + 0.25 * before_x(error)
    upper = 0.75 * error + 0.25 * after_x(error)
    fine = jnp.stack([lower, upper], 1).reshape(k2.shape)
    near = jnp.where(
        (places.lane & 4) == 0,
        jnp.where(places.has_before_z(1), ring(fine, 4, 2), 0.0),
        jnp.where(places.has_after_z(1), ring(fine, -4, 2), 0.0),
    )
    return error_two + (0.75 * fine + 0.25 * near)


def finish(grid, wide, smoothed, error_one, out, e1, e0):
    cells_x, cells_y, depth = smoothed.shape
    i, j = lax.axis_index("gx"), lax.axis_index("gy")
    first = 8 - 2
    count = cells_y + 8
    lane = lax.broadcasted_iota(jnp.int32, (count, depth), 1)
    row = lax.broadcasted_iota(jnp.int32, (count, depth), 0) - 2

    def widen_z(value, stride, lane):
        down = jnp.where(lane >= stride, pltpu.roll(value, stride, 1), 0.0)
        up = jnp.where(lane < depth - stride, pltpu.roll(value, depth - stride, 1), 0.0)
        return 0.75 * value + 0.25 * jnp.where((lane & stride) == 0, down, up)

    def widen_y(ref, index, first, count, stride, row):
        centre = ref[index, pl.ds(first, count), :]
        down = ref[index, pl.ds(first - stride, count), :]
        up = ref[index, pl.ds(first + stride, count), :]
        return 0.75 * centre + 0.25 * jnp.where((row & stride) == 0, down, up)

    low_row = jnp.where(j > 0, -cells_y, 0)
    high_row = jnp.where(j < grid[1] - 1, 2 * cells_y, cells_y)
    inside = (row >= low_row) & (row < high_row)
    planes_two = cells_x // 4 + 2
    mid = [widen_z(widen_y(wide, x, first, count, 2, row), 2, lane) for x in range(planes_two)]
    for x in range(cells_x // 2 + 2):
        centre = (x + 1) // 2
        near = centre + (1 if x % 2 == 0 else -1)
        value = jnp.where(inside, 0.75 * mid[centre] + 0.25 * mid[near], 0.0)
        if x == 0:
            value = jnp.where(i > 0, value, 0.0)
        if x == cells_x // 2 + 1:
            value = jnp.where(i < grid[0] - 1, value, 0.0)
        here = pl.ds(first, count)
        e1[x, here, :] = error_one[x, here, :] + value

    lane = lax.broadcasted_iota(jnp.int32, (cells_y, depth), 1)
    row = lax.broadcasted_iota(jnp.int32, (cells_y, depth), 0)
    for x in range(cells_x // 2 + 2):
        e0[x] = widen_z(widen_y(e1, x, 8, cells_y, 1, row), 1, lane)
    for x in range(cells_x):
        centre = x // 2 + 1
        near = centre + (-1 if x % 2 == 0 else 1)
        out[x] = smoothed[x] + (0.75 * e0[centre] + 0.25 * e0[near])


def correct_kernel(grid, gathered, smoothed, error_one, out, whole, strip, wide, e1, e0):
    cells_y = smoothed.shape[1]
    nx, ny = grid
    i, j = lax.axis_index("gx"), lax.axis_index("gy")
    lane = lax.broadcasted_iota(jnp.int32, (8, 128), 1) & 3
    fields = [[], []]
    for column in range(nx):
        parts = [gathered[column * ny + part] for part in range(ny)]
        for field in range(2):
            for x in range(2):
                place = 2 * field + x
                plane = None
                for part in range(ny):
                    turned = parts[part] if part == place else ring(parts[part], part - place, 1)
                    plane = turned if plane is None else jnp.where(lane == part, turned, plane)
                fields[field].append(plane)
    rhs2 = jnp.stack(fields[0], 0)
    k2 = jnp.stack(fields[1], 0)
    planes = 2 * nx
    whole[0] = jnp.zeros((8, 128), jnp.float32)
    whole[planes + 1] = jnp.zeros((8, 128), jnp.float32)
    whole[pl.ds(1, planes)] = whole_solve(k2, rhs2)

    masks = [[(j + side - lane) == shift for shift in range(-4, 5)] for side in (-1, 0, 1)]
    inside = (j > 0, True, j < ny - 1)
    for x in range(4):
        plane = whole[2 * i + x]
        turned = [plane if shift == 0 else ring(plane, -shift, 1) for shift in range(-4, 5)]
        for index in range(3):
            value = jnp.zeros_like(plane)
            for mask, each in zip(masks[index], turned):
                value = jnp.where(mask, each, value)
            strip[x, pl.ds(8 * index, 8), :] = value if index == 1 else jnp.where(inside[index], value, 0.0)
        for place in range(4):
            wide[x, pl.ds(4 + place, 8, stride=4), :] = strip[x, pl.ds(7, 8), :]
            wide[x, pl.ds(36 + place, 2, stride=4), :] = strip[x, pl.ds(15, 2), :]
    finish(grid, wide, smoothed, error_one, out, e1, e0)


def finish_kernel(grid, wide, smoothed, error_one, out, e1, e0):
    finish(grid, wide, smoothed, error_one, out, e1, e0)


def last_scratch(cells_x, cells_y, depth):
    count = cells_x // 2 + 2
    return [
        pltpu.VMEM((count, cells_y + 16, depth), jnp.float32),
        pltpu.VMEM((count, cells_y, depth), jnp.float32),
    ]


def correct_whole(grid, tiles, smoothed, error_one):
    gathered = lax.all_to_all(tiles, ("gx", "gy"), 0, 0, tiled=False)
    cells_x, cells_y, depth = smoothed.shape
    return pl.pallas_call(
        functools.partial(correct_kernel, grid),
        out_shape=jax.ShapeDtypeStruct(smoothed.shape, jnp.float32),
        scratch_shapes=[
            pltpu.VMEM((2 * grid[0] + 2, 8, depth), jnp.float32),
            pltpu.VMEM((4, 24, depth), jnp.float32),
            pltpu.VMEM((4, cells_y + 16, depth), jnp.float32),
        ]
        + last_scratch(cells_x, cells_y, depth),
        compiler_params=pltpu.CompilerParams(vmem_limit_bytes=VMEM_LIMIT),
        name="correct",
    )(gathered, smoothed, error_one)


def with_faces(shard):
    for axis, dim in (("gx", 0), ("gy", 1)):
        length = shard.shape[dim]
        last = lax.slice_in_dim(shard, length - 1, length, axis=dim)
        initial = lax.slice_in_dim(shard, 0, 1, axis=dim)
        before = lax.ppermute(last, axis, shifts(axis, 1))
        after = lax.ppermute(initial, axis, shifts(axis, -1))
        shard = jnp.concatenate([before, shard, after], axis=dim)
    return shard


def with_zeros(field):
    return jnp.pad(field, ((1, 1), (1, 1), (0, 0)))


def pad_depth(field):
    return jnp.pad(field, ((0, 0), (0, 0), (1, 1)))


def restrict(field):
    size_x, size_y, size_z = field.shape
    return field.reshape(size_x // 2, 2, size_y // 2, 2, size_z // 2, 2).mean(axis=(1, 3, 5))


def level_weights(coef_pad):
    c = pad_depth(coef_pad)
    wx = (c[1:, 1:-1, 1:-1] + c[:-1, 1:-1, 1:-1]) * 0.5
    wy = (c[1:-1, 1:, 1:-1] + c[1:-1, :-1, 1:-1]) * 0.5
    wz = (c[1:-1, 1:-1, 1:] + c[1:-1, 1:-1, :-1]) * 0.5
    diagonal = wx[1:] + wx[:-1] + wy[:, 1:] + wy[:, :-1] + wz[:, :, 1:] + wz[:, :, :-1]
    return (wx, wy, wz), diagonal


def neighbour_sum(field_pad, weights):
    wx, wy, wz = weights
    v = pad_depth(field_pad)
    total = wx[:-1] * v[:-2, 1:-1, 1:-1] + wx[1:] * v[2:, 1:-1, 1:-1]
    total = total + wy[:, :-1] * v[1:-1, :-2, 1:-1] + wy[:, 1:] * v[1:-1, 2:, 1:-1]
    return total + wz[:, :, :-1] * v[1:-1, 1:-1, :-2] + wz[:, :, 1:] * v[1:-1, 1:-1, 2:]


def prolong_axis(padded, axis):
    length = padded.shape[axis]
    middle = lax.slice_in_dim(padded, 1, length - 1, axis=axis)
    before = lax.slice_in_dim(padded, 0, length - 2, axis=axis)
    after = lax.slice_in_dim(padded, 2, length, axis=axis)
    joined = jnp.stack([0.75 * middle + 0.25 * before, 0.75 * middle + 0.25 * after], axis=axis + 1)
    shape = list(middle.shape)
    shape[axis] = 2 * shape[axis]
    return joined.reshape(shape)


def coarse_solve(rhs, weights, diagonal):
    error = jnp.zeros_like(rhs)
    remain = rhs
    direction = rhs
    norm_now = jnp.sum(remain * remain)
    for _ in range(CSWEEPS):
        image = (diagonal * direction - neighbour_sum(with_zeros(direction), weights)) * 4.0**-3
        alpha = norm_now / jnp.sum(direction * image)
        error = error + alpha * direction
        remain = remain - alpha * image
        norm_next = jnp.sum(remain * remain)
        direction = remain + norm_next / norm_now * direction
        norm_now = norm_next
    return error


def correct_spread(grid, tiles, smoothed, error_one):
    cells_x, cells_y, depth = smoothed.shape
    shape2 = (cells_x // 4, cells_y // 4, depth // 4)
    own = tiles[0].reshape(shape2[1], shape2[2], 2, shape2[0]).transpose(2, 3, 0, 1)
    rhs2, k2 = own[0], own[1]
    weights, diagonal = level_weights(with_faces(k2))
    parity = sum(lax.broadcasted_iota(jnp.int32, shape2, d) for d in range(3)) % 2
    error_two = jnp.where(parity == 0, rhs2 * 16.0 / diagonal, 0.0)
    total = neighbour_sum(with_faces(error_two), weights)
    error_two = jnp.where(parity == 1, (rhs2 * 16.0 + total) / diagonal, error_two)
    total = neighbour_sum(with_faces(error_two), weights)
    rhs3 = restrict(rhs2 - (diagonal * error_two - total) * 4.0**-2)
    merged = jnp.stack([rhs3, restrict(k2)])
    merged = lax.all_gather(merged, "gx", axis=1, tiled=True)
    merged = lax.all_gather(merged, "gy", axis=2, tiled=True)
    weights3, diagonal3 = level_weights(with_zeros(merged[1]))
    error_three = coarse_solve(merged[0], weights3, diagonal3)
    start_x = lax.axis_index("gx") * rhs3.shape[0]
    start_y = lax.axis_index("gy") * rhs3.shape[1]
    window = lax.dynamic_slice(
        with_zeros(error_three),
        (start_x, start_y, jnp.int32(0)),
        (rhs3.shape[0] + 2, rhs3.shape[1] + 2, rhs3.shape[2]),
    )
    finer = pad_depth(window)
    for axis in range(3):
        finer = prolong_axis(finer, axis)
    wide = with_faces(error_two + finer)
    wide = jnp.repeat(jnp.repeat(wide, 4, axis=1), 4, axis=2)
    wide = jnp.pad(wide, ((0, 0), (4, 4), (0, 0)))
    return pl.pallas_call(
        functools.partial(finish_kernel, grid),
        out_shape=jax.ShapeDtypeStruct(smoothed.shape, jnp.float32),
        scratch_shapes=last_scratch(cells_x, cells_y, depth),
        compiler_params=pltpu.CompilerParams(vmem_limit_bytes=VMEM_LIMIT),
        name="finish",
    )(wide, smoothed, error_one)


def on_device(pressure, source, coefficient):
    grid = (lax.axis_size("gx"), lax.axis_size("gy"))
    _, cells_y, depth = pressure.shape
    fits = grid[1] == 4 and cells_y == 32 and depth == 128
    own = (pressure, source, coefficient)
    block = stacked(*own)
    halo = fine_halo(own, block)
    copies = grid[0] * grid[1] if fits else 1
    smoothed, error_one, tiles = smooth(copies, block, halo)
    correct = correct_whole if fits else correct_spread
    return correct(grid, tiles, smoothed, error_one)


def solution(mesh):
    spec = P("gx", "gy", None)
    return jax.shard_map(on_device, mesh=mesh, in_specs=(spec, spec, spec), out_specs=spec, check_vma=False)
```

```python
import functools
import jax
import jax.numpy as jnp
from jax import lax
from jax.experimental import pallas as pl
from jax.experimental.pallas import tpu as pltpu
from jax.sharding import PartitionSpec as P

CSWEEPS = 4
REACH = 9
ORIGIN = 16
VMEM_LIMIT = 48 * 1024 * 1024


def y_rows(distance, array):
    rows = REACH if distance <= 2 else REACH + 2 - distance
    return rows - 1 if array == 1 else rows


def side_entries():
    pairs = [(0, d, (d, d + 1)) for d in range(1, REACH - 1, 2)] + [(0, REACH, (REACH,))]
    return pairs + [(1, d, (d,)) for d in range(1, REACH)] + [(2, d, (d,)) for d in range(1, REACH + 1)]


def x_plan(cells_y):
    first, second = {}, {}
    lengths = [0, 0]

    def put(message, plan, key, row, rows):
        plan.setdefault(key, []).append((row, rows, lengths[message]))
        lengths[message] += rows

    for array, distance, _ in side_entries():
        key = (array, distance)
        ends = y_rows(distance, array)
        if array != 1 and distance == 1:
            put(0, first, key, 0, cells_y)
        else:
            put(0, first, key, 0, ends)
            put(0, first, key, cells_y - ends, ends)
            put(1, second, key, ends, cells_y - 2 * ends)
    return first, second, [-(-length // 8) * 8 for length in lengths]


def y_plan(cells_x):
    pieces = []
    start = 0
    inside = [(0, m) for m in range(cells_x // 2)] + [(a, x) for a in (1, 2) for x in range(cells_x)]
    chosen = [("inside", array, index, y_rows(0, array)) for array, index in inside]
    chosen += [("away", array, distance, y_rows(distance, array)) for array, distance, _ in side_entries()]
    for side, array, index, rows in chosen:
        pieces.append((side, array, index, rows, start))
        start += rows
    return pieces, -(-start // 8) * 8


def shifts(axis, step):
    count = lax.axis_size(axis)
    return [(i, i + step) for i in range(count) if 0 <= i + step < count]


def swap_pairs():
    return [(i, i ^ 1) for i in range(lax.axis_size("gx"))]


def x_pairs():
    count = lax.axis_size("gx")
    pairs = [(i, i + 1) for i in range(1, count - 1, 2)]
    return pairs + [(j, i) for i, j in pairs]


def inside_rows(member, own, partner, array, index, first, rows):
    cells_x = own[0].shape[0]
    here = pl.ds(first, rows)

    def plane(x):
        if x // cells_x == member:
            return own[array][x % cells_x, here, :]
        value = partner[array][x % cells_x, here, :]
        return value + value if array == 1 else value

    if array != 0:
        return plane(index)
    depth = own[0].shape[2]
    row = lax.broadcasted_iota(jnp.int32, (rows, depth), 0) + first
    lane = lax.broadcasted_iota(jnp.int32, (rows, depth), 1)
    return jnp.where(((row + lane) & 1) == 1, plane(2 * index), plane(2 * index + 1))


def for_member(body):
    me = lax.axis_index("gx") & 1
    for member in range(2):
        pl.when(me == member)(functools.partial(body, member))


def split_kernel(block, pp, pf, pk, first, second):
    cells_x, cells_y, _ = pp.shape
    p, f, k = views(block, cells_x)
    plans = x_plan(cells_y)

    def body(member):
        for plan, target in zip(plans, (first, second)):
            for (array, distance), pieces in plan.items():
                plane = 2 * cells_x - distance if member == 1 else distance - 1
                index = plane // 2 if array == 0 else plane
                for row, rows, start in pieces:
                    value = inside_rows(member, (p, f, k), (pp, pf, pk), array, index, row, rows)
                    target[pl.ds(start, rows), :] = value

    for_member(body)


def pack_kernel(block, received, to_up, to_down, far):
    cells_x, cells_y = block.shape[0] // 3, block.shape[1]
    own = views(block, cells_x)
    plan = x_plan(cells_y)[0]

    def piece(side, array, index, rows, row):
        if side == "inside":
            return inside_rows(0, own, None, array, index, row, rows)
        place = [s + row - r for r, count, s in plan[array, index] if r <= row and row + rows <= r + count][0]
        return received[pl.ds(place, rows), :]

    for side, array, index, rows, start in y_plan(cells_x)[0]:
        to_up[pl.ds(start, rows), :] = piece(side, array, index, rows, cells_y - rows)
        to_down[pl.ds(start, rows), :] = piece(side, array, index, rows, 0)
    far[0] = piece("away", 0, 1, cells_y, 0)
    far[1] = piece("away", 2, 1, cells_y, 0)


def stacked(pressure, source, coefficient):
    block = jnp.concatenate([pressure, source, coefficient], 0)
    cells_x = pressure.shape[0]
    plane = lax.broadcasted_iota(jnp.int32, block.shape, 0)
    return block * jnp.where((plane >= cells_x) & (plane < 2 * cells_x), 2.0, 1.0)


def views(block, cells_x):
    return tuple(block.at[pl.ds(n * cells_x, cells_x)] for n in range(3))


def fine_halo(own, block):
    cells_x, cells_y, depth = own[0].shape
    params = pltpu.CompilerParams(vmem_limit_bytes=VMEM_LIMIT)

    def packed(length):
        return jax.ShapeDtypeStruct((length, depth), jnp.float32)

    partner = tuple(lax.ppermute(v, "gx", swap_pairs()) for v in own)
    lengths = x_plan(cells_y)[2]
    first, second = pl.pallas_call(
        split_kernel, out_shape=[packed(n) for n in lengths], compiler_params=params, name="split_block"
    )(block, *partner)
    received = lax.ppermute(first, "gx", x_pairs())
    length = y_plan(cells_x)[1]
    planes = jax.ShapeDtypeStruct((2, cells_y, depth), jnp.float32)
    to_up, to_down, outermost = pl.pallas_call(
        pack_kernel, out_shape=[packed(length), packed(length), planes], compiler_params=params, name="pack_halo"
    )(block, received)
    below = lax.ppermute(to_up, "gy", shifts("gy", 1))
    above = lax.ppermute(to_down, "gy", shifts("gy", -1))
    far = lax.ppermute(outermost, "gx", swap_pairs())
    rest = lax.ppermute(second, "gx", x_pairs())
    above, far, rest = lax.optimization_barrier((above, far, rest))
    p_below = lax.ppermute(below, "gx", swap_pairs())
    p_above = lax.ppermute(above, "gx", swap_pairs())
    return *partner, received, rest, far, below, above, p_below, p_above


def smooth_kernel(
    block, pp, pf, pk, received, rest, far, below, above, p_below, p_above,
    out, error_one, tiles,
    vp, vf, vk, wx, wy, zl, zh, dg, inv, va, vb,
    t0, t1, f1, k1, inv1, g1, h1, q2,
):
    cells_x, cells_y, depth = pp.shape
    planes = cells_x + 2 * REACH
    own_rows = pl.ds(ORIGIN, cells_y)
    top = ORIGIN - REACH + 1
    rows = cells_y + 2 * (REACH - 1)
    body = pl.ds(top, rows)

    windows = (vp, vf, vk)
    first_plan, second_plan, _ = x_plan(cells_y)

    def fill(array, x, first, value):
        if x < -REACH or x >= cells_x + REACH or (array == 1 and (x == -REACH or x == cells_x + REACH - 1)):
            return
        windows[array][REACH + x, pl.ds(ORIGIN + first, value.shape[0]), :] = value

    for x in range(cells_x):
        for array, ref in enumerate(views(block, cells_x)):
            fill(array, x, 0, ref[x])

    spans = {(array, distance): distances for array, distance, distances in side_entries()}

    def outside(side, distance):
        return -distance if side == "low" else cells_x - 1 + distance

    def fill_member(member):
        away, near = (("low", "high"), ("high", "low"))[member]
        for x in range(cells_x):
            for array, ref in enumerate((pp, pf, pk)):
                value = ref[x]
                fill(array, x + cells_x * (1 - 2 * member), 0, value + value if array == 1 else value)
        fill(0, outside(near, REACH), 0, far[0])
        fill(2, outside(near, REACH), 0, far[1])
        for plan, ref in ((first_plan, received), (second_plan, rest)):
            for (array, distance), pieces in plan.items():
                for row, count, start in pieces:
                    value = ref[pl.ds(start, count), :]
                    for each in spans[array, distance]:
                        fill(array, outside(away, each), row, value)

        towards_partner = cells_x * (1 - 2 * member)
        for before, after, is_partner in ((below, above, False), (p_below, p_above, True)):
            for side, array, index, count, start in y_plan(cells_x)[0]:
                if side == "inside":
                    xs = (2 * index, 2 * index + 1) if array == 0 else (index,)
                    xs = [x + towards_partner * is_partner for x in xs]
                elif is_partner:
                    xs = [outside(near, cells_x + each) for each in spans[array, index]]
                else:
                    xs = [outside(away, each) for each in spans[array, index]]
                for x in xs:
                    fill(array, x, -count, before[pl.ds(start, count), :])
                    fill(array, x, cells_y, after[pl.ds(start, count), :])

    for_member(fill_member)

    def lanes(count):
        return lax.broadcasted_iota(jnp.int32, (count, depth), 1)

    def rows_of(first, count):
        return lax.broadcasted_iota(jnp.int32, (count, depth), 0) + (first - ORIGIN)

    lane = lanes(rows)

    def weigh(plane, _):
        centre = vk[plane, body, :]
        west = centre + vk[plane - 1, body, :]
        wx[plane, body, :] = west
        east = centre + vk[plane + 1, body, :]
        south = centre + vk[plane, pl.ds(top - 1, rows), :]
        north = centre + vk[plane, pl.ds(top + 1, rows), :]
        wy[plane, body, :] = south
        wy[plane, pl.ds(top + rows, 1), :] = north[rows - 1:, :]
        down = jnp.where(lane > 0, pltpu.roll(centre, 1, 1), 0.0)
        up = jnp.where(lane < depth - 1, pltpu.roll(centre, depth - 1, 1), 0.0)
        total = west + east + south + north + (centre + down) + (centre + up)
        zl[plane, body, :] = jnp.where(lane > 0, centre + down, 0.0)
        zh[plane, body, :] = jnp.where(lane < depth - 1, centre + up, 0.0)
        dg[plane, body, :] = total
        inside = centre > 0.0
        inv[plane, body, :] = jnp.where(inside, 1.0 / jnp.where(inside, total, 1.0), 0.0)
        return 0

    lax.fori_loop(1, planes - 1, weigh, 0, unroll=True)
    wx[planes - 1, body, :] = vk[planes - 1, body, :] + vk[planes - 2, body, :]

    def stencil(v, plane, first, count):
        here = pl.ds(first, count)
        centre = v[plane, here, :]
        total = wx[plane, here, :] * v[plane - 1, here, :] + wx[plane + 1, here, :] * v[plane + 1, here, :]
        total += wy[plane, here, :] * v[plane, pl.ds(first - 1, count), :]
        total += wy[plane, pl.ds(first + 1, count), :] * v[plane, pl.ds(first + 1, count), :]
        total += zl[plane, here, :] * pltpu.roll(centre, 1, 1)
        total += zh[plane, here, :] * pltpu.roll(centre, depth - 1, 1)
        return total

    def relax(source_ref, target, reach):
        def one(plane, _):
            total = stencil(source_ref, plane, top, rows)
            target[plane, body, :] = inv[plane, body, :] * (vf[plane, body, :] + total)
            return 0

        lax.fori_loop(REACH - reach, REACH + cells_x + reach, one, 0, unroll=True)

    relax(vp, va, REACH - 1)
    relax(va, vb, REACH - 2)
    relax(vb, va, REACH - 3)
    relax(va, vb, REACH - 4)

    own_lane = lanes(cells_y)
    own_row = rows_of(ORIGIN, cells_y)
    for x in range(cells_x):
        even = ((own_row + own_lane + x) & 1) == 0
        out[x] = jnp.where(even, va[REACH + x, own_rows, :], vb[REACH + x, own_rows, :])

    planes_one = cells_x // 2
    first = ORIGIN - 4
    count = cells_y + 8
    lane = lanes(count)
    row = rows_of(first, count)

    def pair_lane(value, stride, lane):
        up = pltpu.roll(value, depth - stride, 1)
        down = pltpu.roll(value, stride, 1)
        return value + jnp.where((lane & stride) == 0, up, down)

    def pair_row(ref, index, first, count, stride, row):
        centre = ref[index, pl.ds(first, count), :]
        up = ref[index, pl.ds(first + stride, count), :]
        down = ref[index, pl.ds(first - stride, count), :]
        return centre + jnp.where((row & stride) == 0, up, down)

    def residual(plane_one, _):
        total = jnp.zeros((count, depth), jnp.float32)
        for half in range(2):
            plane = 2 * plane_one + REACH - 4 + half
            here = pl.ds(first, count)
            twice = vf[plane, here, :] - dg[plane, here, :] * va[plane, here, :] + stencil(vb, plane, first, count)
            even = ((row + lane + half) & 1) == 0
            total += jnp.where(even, twice, 0.0)
        t0[plane_one, pl.ds(first, count), :] = pair_lane(total, 1, lane)
        return 0

    lax.fori_loop(0, planes_one + 4, residual, 0, unroll=True)
    for x in range(planes_one + 4):
        f1[x, pl.ds(first, count), :] = 0.5 * pair_row(t0, x, first, count, 1, row)

    first_k = ORIGIN - 6
    count_k = cells_y + 16
    lane_k = lanes(count_k)
    row_k = rows_of(first_k, count_k)
    for x in range(planes_one + 6):
        plane = 2 * x + REACH - 6
        here = pl.ds(first_k, count_k)
        t1[x, here, :] = pair_lane(vk[plane, here, :] + vk[plane + 1, here, :], 1, lane_k)
    for x in range(planes_one + 6):
        k1[x, pl.ds(first_k, count_k), :] = 0.125 * pair_row(t1, x, first_k, count_k, 1, row_k)

    def down2(value, lane):
        return jnp.where(lane >= 2, pltpu.roll(value, 2, 1), 0.0)

    def up2(value, lane):
        return jnp.where(lane < depth - 2, pltpu.roll(value, depth - 2, 1), 0.0)

    here = pl.ds(first, count)
    for x in range(planes_one + 4):
        centre = k1[x + 1, here, :]
        total = 6.0 * centre + (k1[x, here, :] + k1[x + 2, here, :])
        total += k1[x + 1, pl.ds(first - 2, count), :] + k1[x + 1, pl.ds(first + 2, count), :]
        total += down2(centre, lane) + up2(centre, lane)
        inside = centre > 0.0
        inverse = jnp.where(inside, 1.0 / jnp.where(inside, total, 1.0), 0.0)
        inv1[x, here, :] = inverse
        g1[x, here, :] = inverse * f1[x, here, :]

    def stencil_one(v, x, v_x, first, count, lane):
        here = pl.ds(first, count)
        south = pl.ds(first - 2, count)
        north = pl.ds(first + 2, count)
        kc = k1[x, here, :]
        vc = v[v_x, here, :]
        total = (kc + k1[x - 1, here, :]) * v[v_x - 1, here, :] + (kc + k1[x + 1, here, :]) * v[v_x + 1, here, :]
        total += (kc + k1[x, south, :]) * v[v_x, south, :] + (kc + k1[x, north, :]) * v[v_x, north, :]
        total += (kc + down2(kc, lane)) * down2(vc, lane) + (kc + up2(kc, lane)) * up2(vc, lane)
        return total

    first_h = ORIGIN - 2
    count_h = cells_y + 8
    lane_h = lanes(count_h)
    row_h = rows_of(first_h, count_h)
    for x in range(planes_one + 2):
        here = pl.ds(first_h, count_h)
        total = stencil_one(g1, x + 2, x + 1, first_h, count_h, lane_h)
        odd = inv1[x + 1, here, :] * (f1[x + 1, here, :] + total)
        h1[x, here, :] = odd
        even_cell = ((x - 1 + (row_h >> 1) + (lane_h >> 1)) & 1) == 0
        error_one[x, pl.ds(first_h - 8, count_h), :] = jnp.where(even_cell, g1[x + 1, here, :], odd)

    own2 = own_lane
    row2 = own_row
    for x in range(planes_one // 2):
        sum_r = jnp.zeros((cells_y, depth), jnp.float32)
        for half in range(2):
            x1 = 2 * x + half
            total = stencil_one(h1, x1 + 3, x1 + 1, ORIGIN, cells_y, own2)
            even_cell = ((x1 + (row2 >> 1) + (own2 >> 1)) & 1) == 0
            sum_r += jnp.where(even_cell, total, 0.0)
        sum_k = k1[2 * x + 3, own_rows, :] + k1[2 * x + 4, own_rows, :]
        t0[x, own_rows, :] = pair_lane(sum_r, 2, own2)
        t1[x, own_rows, :] = pair_lane(sum_k, 2, own2)
    lane8 = lanes(cells_y // 4)
    tile = jnp.zeros((cells_y // 4, depth), jnp.float32)
    for x in range(planes_one // 2):
        q2[0] = (1.0 / 64.0) * pair_row(t0, x, ORIGIN, cells_y, 2, row2)
        q2[1] = 0.125 * pair_row(t1, x, ORIGIN, cells_y, 2, row2)
        for field in range(2):
            kept = q2[field, pl.ds(0, cells_y // 4, stride=4), :]
            tile = jnp.where((lane8 & 3) == 2 * field + x, kept, tile)
    tiles[...] = jnp.broadcast_to(tile[None], tiles.shape)


def smooth(copies, block, halo):
    cells_x, cells_y, depth = halo[0].shape
    planes = cells_x + 2 * REACH
    tall = cells_y + 2 * ORIGIN
    planes_one = cells_x // 2
    window = pltpu.VMEM((planes, tall, depth), jnp.float32)

    def level_one(count):
        return pltpu.VMEM((count, tall, depth), jnp.float32)

    return pl.pallas_call(
        smooth_kernel,
        out_shape=(
            jax.ShapeDtypeStruct((cells_x, cells_y, depth), jnp.float32),
            jax.ShapeDtypeStruct((planes_one + 2, cells_y + 16, depth), jnp.float32),
            jax.ShapeDtypeStruct((copies, cells_y // 4, depth), jnp.float32),
        ),
        scratch_shapes=[window] * 11
        + [
            level_one(planes_one + 4),
            level_one(planes_one + 6),
            level_one(planes_one + 4),
            level_one(planes_one + 6),
            level_one(planes_one + 4),
            level_one(planes_one + 4),
            level_one(planes_one + 2),
            pltpu.VMEM((2, cells_y, depth), jnp.float32),
        ],
        compiler_params=pltpu.CompilerParams(vmem_limit_bytes=VMEM_LIMIT),
        name="smooth",
    )(block, *halo)


def ring(value, shift, axis):
    return pltpu.roll(value, shift % value.shape[axis], axis)


def before_x(v):
    return jnp.concatenate([jnp.zeros_like(v[:1]), v[:-1]], 0)


def after_x(v):
    return jnp.concatenate([v[1:], jnp.zeros_like(v[:1])], 0)


class Places:
    def __init__(self, shape):
        self.row = lax.broadcasted_iota(jnp.int32, shape, 1)
        self.lane = lax.broadcasted_iota(jnp.int32, shape, 2)
        self.part = self.lane & 3
        self.depth = shape[2]

    def before_y(self, v, stride):
        turned = ring(v, stride, 1)
        return jnp.where(self.row >= stride, turned, ring(turned, 1, 2))

    def after_y(self, v, stride):
        turned = ring(v, -stride, 1)
        return jnp.where(self.row < 8 - stride, turned, ring(turned, -1, 2))

    def has_before_y(self, stride):
        return (self.row >= stride) | (self.part > 0)

    def has_after_y(self, stride):
        return (self.row < 8 - stride) | (self.part < 3)

    def has_before_z(self, stride):
        return self.lane >= 4 * stride

    def has_after_z(self, stride):
        return self.lane < self.depth - 4 * stride


def whole_weights(k, places, stride):
    west = k + before_x(k)
    east = k + after_x(k)
    masks = (
        places.has_before_y(stride),
        places.has_after_y(stride),
        places.has_before_z(stride),
        places.has_after_z(stride),
    )
    near = (
        places.before_y(k, stride),
        places.after_y(k, stride),
        ring(k, 4 * stride, 2),
        ring(k, -4 * stride, 2),
    )
    diagonal = west + east
    weights = [west, east]
    for mask, value in zip(masks, near):
        diagonal += k + jnp.where(mask, value, 0.0)
        weights.append(jnp.where(mask, k + value, 0.0))
    return weights, diagonal


def whole_sum(v, weights, places, stride):
    total = weights[0] * before_x(v) + weights[1] * after_x(v)
    total += weights[2] * places.before_y(v, stride) + weights[3] * places.after_y(v, stride)
    total += weights[4] * ring(v, 4 * stride, 2) + weights[5] * ring(v, -4 * stride, 2)
    return total


def whole_solve(k2, rhs2):
    planes = k2.shape[0]
    places = Places(k2.shape)
    weights, diagonal = whole_weights(k2, places, 1)
    parity = lax.broadcasted_iota(jnp.int32, k2.shape, 0) + places.row + (places.lane >> 2)
    even = (parity & 1) == 0
    inverse = 1.0 / diagonal
    scaled = 32.0 * rhs2
    even_values = inverse * scaled
    odd_values = inverse * (scaled + whole_sum(even_values, weights, places, 1))
    error_two = jnp.where(even, even_values, odd_values)
    left = jnp.where(even, whole_sum(odd_values, weights, places, 1), 0.0)

    half = places.row[: planes // 2] , places.lane[: planes // 2]
    first_row = (half[0] & 1) == 0
    first_lane = (half[1] & 4) == 0

    def coarse(v):
        v = v.reshape(planes // 2, 2, *v.shape[1:])
        v = v[:, 0] + v[:, 1]
        v = v + jnp.where(first_row, ring(v, -1, 1), ring(v, 1, 1))
        return v + jnp.where(first_lane, ring(v, -4, 2), ring(v, 4, 2))

    remain = (1.0 / 256.0) * coarse(left)
    k3 = 0.125 * coarse(k2)
    places3 = Places(k3.shape)
    weights3, diagonal3 = whole_weights(k3, places3, 2)

    def total(v):
        return jnp.sum(jnp.sum(v, axis=0, keepdims=True), axis=(1, 2), keepdims=True)

    def around(v):
        return (
            places3.before_y(v, 2), places3.after_y(v, 2), ring(v, 8, 2), ring(v, -8, 2),
        )

    direction, sides = remain, around(remain)
    remain_sides = sides
    norm_now = total(remain * remain)
    error = error_before = error_after = jnp.zeros_like(remain)
    for repeat in range(CSWEEPS):
        coupled = weights3[0] * before_x(direction) + weights3[1] * after_x(direction)
        coupled += weights3[2] * sides[0] + weights3[3] * sides[1]
        coupled += weights3[4] * sides[2] + weights3[5] * sides[3]
        image = (diagonal3 * direction - coupled) * (1.0 / 128.0)
        alpha = norm_now / total(direction * image)
        error = error + alpha * direction
        error_before = error_before + alpha * sides[0]
        error_after = error_after + alpha * sides[1]
        if repeat == CSWEEPS - 1:
            break
        image_sides = around(image)
        remain = remain - alpha * image
        remain_sides = [r - alpha * q for r, q in zip(remain_sides, image_sides)]
        norm_next = total(remain * remain)
        beta = norm_next / norm_now
        direction = remain + beta * direction
        sides = [r + beta * p for r, p in zip(remain_sides, sides)]
        norm_now = norm_next

    near = jnp.where(
        first_row,
        jnp.where(places3.has_before_y(2), error_before, 0.0),
        jnp.where(places3.has_after_y(2), error_after, 0.0),
    )
    error = 0.75 * error + 0.25 * near
    lower = 0.75 * error + 0.25 * before_x(error)
    upper = 0.75 * error + 0.25 * after_x(error)
    fine = jnp.stack([lower, upper], 1).reshape(k2.shape)
    near = jnp.where(
        (places.lane & 4) == 0,
        jnp.where(places.has_before_z(1), ring(fine, 4, 2), 0.0),
        jnp.where(places.has_after_z(1), ring(fine, -4, 2), 0.0),
    )
    return error_two + (0.75 * fine + 0.25 * near)


def finish(grid, wide, smoothed, error_one, out, e1, e0):
    cells_x, cells_y, depth = smoothed.shape
    i, j = lax.axis_index("gx"), lax.axis_index("gy")
    first = 8 - 2
    count = cells_y + 8
    lane = lax.broadcasted_iota(jnp.int32, (count, depth), 1)
    row = lax.broadcasted_iota(jnp.int32, (count, depth), 0) - 2

    def widen_z(value, stride, lane):
        down = jnp.where(lane >= stride, pltpu.roll(value, stride, 1), 0.0)
        up = jnp.where(lane < depth - stride, pltpu.roll(value, depth - stride, 1), 0.0)
        return 0.75 * value + 0.25 * jnp.where((lane & stride) == 0, down, up)

    def widen_y(ref, index, first, count, stride, row):
        centre = ref[index, pl.ds(first, count), :]
        down = ref[index, pl.ds(first - stride, count), :]
        up = ref[index, pl.ds(first + stride, count), :]
        return 0.75 * centre + 0.25 * jnp.where((row & stride) == 0, down, up)

    low_row = jnp.where(j > 0, -cells_y, 0)
    high_row = jnp.where(j < grid[1] - 1, 2 * cells_y, cells_y)
    inside = (row >= low_row) & (row < high_row)
    planes_two = cells_x // 4 + 2
    mid = [widen_z(widen_y(wide, x, first, count, 2, row), 2, lane) for x in range(planes_two)]
    for x in range(cells_x // 2 + 2):
        centre = (x + 1) // 2
        near = centre + (1 if x % 2 == 0 else -1)
        value = jnp.where(inside, 0.75 * mid[centre] + 0.25 * mid[near], 0.0)
        if x == 0:
            value = jnp.where(i > 0, value, 0.0)
        if x == cells_x // 2 + 1:
            value = jnp.where(i < grid[0] - 1, value, 0.0)
        here = pl.ds(first, count)
        e1[x, here, :] = error_one[x, here, :] + value

    lane = lax.broadcasted_iota(jnp.int32, (cells_y, depth), 1)
    row = lax.broadcasted_iota(jnp.int32, (cells_y, depth), 0)
    for x in range(cells_x // 2 + 2):
        e0[x] = widen_z(widen_y(e1, x, 8, cells_y, 1, row), 1, lane)
    for x in range(cells_x):
        centre = x // 2 + 1
        near = centre + (-1 if x % 2 == 0 else 1)
        out[x] = smoothed[x] + (0.75 * e0[centre] + 0.25 * e0[near])


def correct_kernel(grid, gathered, smoothed, error_one, out, whole, strip, wide, e1, e0):
    cells_y = smoothed.shape[1]
    nx, ny = grid
    i, j = lax.axis_index("gx"), lax.axis_index("gy")
    lane = lax.broadcasted_iota(jnp.int32, (8, 128), 1) & 3
    fields = [[], []]
    for column in range(nx):
        parts = [gathered[column * ny + part] for part in range(ny)]
        for field in range(2):
            for x in range(2):
                place = 2 * field + x
                plane = None
                for part in range(ny):
                    turned = parts[part] if part == place else ring(parts[part], part - place, 1)
                    plane = turned if plane is None else jnp.where(lane == part, turned, plane)
                fields[field].append(plane)
    rhs2 = jnp.stack(fields[0], 0)
    k2 = jnp.stack(fields[1], 0)
    planes = 2 * nx
    whole[0] = jnp.zeros((8, 128), jnp.float32)
    whole[planes + 1] = jnp.zeros((8, 128), jnp.float32)
    whole[pl.ds(1, planes)] = whole_solve(k2, rhs2)

    masks = [[(j + side - lane) == shift for shift in range(-4, 5)] for side in (-1, 0, 1)]
    inside = (j > 0, True, j < ny - 1)
    for x in range(4):
        plane = whole[2 * i + x]
        turned = [plane if shift == 0 else ring(plane, -shift, 1) for shift in range(-4, 5)]
        for index in range(3):
            value = jnp.zeros_like(plane)
            for mask, each in zip(masks[index], turned):
                value = jnp.where(mask, each, value)
            strip[x, pl.ds(8 * index, 8), :] = value if index == 1 else jnp.where(inside[index], value, 0.0)
        for place in range(4):
            wide[x, pl.ds(4 + place, 8, stride=4), :] = strip[x, pl.ds(7, 8), :]
            wide[x, pl.ds(36 + place, 2, stride=4), :] = strip[x, pl.ds(15, 2), :]
    finish(grid, wide, smoothed, error_one, out, e1, e0)


def finish_kernel(grid, wide, smoothed, error_one, out, e1, e0):
    finish(grid, wide, smoothed, error_one, out, e1, e0)


def last_scratch(cells_x, cells_y, depth):
    count = cells_x // 2 + 2
    return [
        pltpu.VMEM((count, cells_y + 16, depth), jnp.float32),
        pltpu.VMEM((count, cells_y, depth), jnp.float32),
    ]


def correct_whole(grid, tiles, smoothed, error_one):
    gathered = lax.all_to_all(tiles, ("gx", "gy"), 0, 0, tiled=False)
    cells_x, cells_y, depth = smoothed.shape
    return pl.pallas_call(
        functools.partial(correct_kernel, grid),
        out_shape=jax.ShapeDtypeStruct(smoothed.shape, jnp.float32),
        scratch_shapes=[
            pltpu.VMEM((2 * grid[0] + 2, 8, depth), jnp.float32),
            pltpu.VMEM((4, 24, depth), jnp.float32),
            pltpu.VMEM((4, cells_y + 16, depth), jnp.float32),
        ]
        + last_scratch(cells_x, cells_y, depth),
        compiler_params=pltpu.CompilerParams(vmem_limit_bytes=VMEM_LIMIT),
        name="correct",
    )(gathered, smoothed, error_one)


def with_faces(shard):
    for axis, dim in (("gx", 0), ("gy", 1)):
        length = shard.shape[dim]
        last = lax.slice_in_dim(shard, length - 1, length, axis=dim)
        initial = lax.slice_in_dim(shard, 0, 1, axis=dim)
        before = lax.ppermute(last, axis, shifts(axis, 1))
        after = lax.ppermute(initial, axis, shifts(axis, -1))
        shard = jnp.concatenate([before, shard, after], axis=dim)
    return shard


def with_zeros(field):
    return jnp.pad(field, ((1, 1), (1, 1), (0, 0)))


def pad_depth(field):
    return jnp.pad(field, ((0, 0), (0, 0), (1, 1)))


def restrict(field):
    size_x, size_y, size_z = field.shape
    return field.reshape(size_x // 2, 2, size_y // 2, 2, size_z // 2, 2).mean(axis=(1, 3, 5))


def level_weights(coef_pad):
    c = pad_depth(coef_pad)
    wx = (c[1:, 1:-1, 1:-1] + c[:-1, 1:-1, 1:-1]) * 0.5
    wy = (c[1:-1, 1:, 1:-1] + c[1:-1, :-1, 1:-1]) * 0.5
    wz = (c[1:-1, 1:-1, 1:] + c[1:-1, 1:-1, :-1]) * 0.5
    diagonal = wx[1:] + wx[:-1] + wy[:, 1:] + wy[:, :-1] + wz[:, :, 1:] + wz[:, :, :-1]
    return (wx, wy, wz), diagonal


def neighbour_sum(field_pad, weights):
    wx, wy, wz = weights
    v = pad_depth(field_pad)
    total = wx[:-1] * v[:-2, 1:-1, 1:-1] + wx[1:] * v[2:, 1:-1, 1:-1]
    total = total + wy[:, :-1] * v[1:-1, :-2, 1:-1] + wy[:, 1:] * v[1:-1, 2:, 1:-1]
    return total + wz[:, :, :-1] * v[1:-1, 1:-1, :-2] + wz[:, :, 1:] * v[1:-1, 1:-1, 2:]


def prolong_axis(padded, axis):
    length = padded.shape[axis]
    middle = lax.slice_in_dim(padded, 1, length - 1, axis=axis)
    before = lax.slice_in_dim(padded, 0, length - 2, axis=axis)
    after = lax.slice_in_dim(padded, 2, length, axis=axis)
    joined = jnp.stack([0.75 * middle + 0.25 * before, 0.75 * middle + 0.25 * after], axis=axis + 1)
    shape = list(middle.shape)
    shape[axis] = 2 * shape[axis]
    return joined.reshape(shape)


def coarse_solve(rhs, weights, diagonal):
    error = jnp.zeros_like(rhs)
    remain = rhs
    direction = rhs
    norm_now = jnp.sum(remain * remain)
    for _ in range(CSWEEPS):
        image = (diagonal * direction - neighbour_sum(with_zeros(direction), weights)) * 4.0**-3
        alpha = norm_now / jnp.sum(direction * image)
        error = error + alpha * direction
        remain = remain - alpha * image
        norm_next = jnp.sum(remain * remain)
        direction = remain + norm_next / norm_now * direction
        norm_now = norm_next
    return error


def correct_spread(grid, tiles, smoothed, error_one):
    cells_x, cells_y, depth = smoothed.shape
    shape2 = (cells_x // 4, cells_y // 4, depth // 4)
    own = tiles[0].reshape(shape2[1], shape2[2], 2, shape2[0]).transpose(2, 3, 0, 1)
    rhs2, k2 = own[0], own[1]
    weights, diagonal = level_weights(with_faces(k2))
    parity = sum(lax.broadcasted_iota(jnp.int32, shape2, d) for d in range(3)) % 2
    error_two = jnp.where(parity == 0, rhs2 * 16.0 / diagonal, 0.0)
    total = neighbour_sum(with_faces(error_two), weights)
    error_two = jnp.where(parity == 1, (rhs2 * 16.0 + total) / diagonal, error_two)
    total = neighbour_sum(with_faces(error_two), weights)
    rhs3 = restrict(rhs2 - (diagonal * error_two - total) * 4.0**-2)
    merged = jnp.stack([rhs3, restrict(k2)])
    merged = lax.all_gather(merged, "gx", axis=1, tiled=True)
    merged = lax.all_gather(merged, "gy", axis=2, tiled=True)
    weights3, diagonal3 = level_weights(with_zeros(merged[1]))
    error_three = coarse_solve(merged[0], weights3, diagonal3)
    start_x = lax.axis_index("gx") * rhs3.shape[0]
    start_y = lax.axis_index("gy") * rhs3.shape[1]
    window = lax.dynamic_slice(
        with_zeros(error_three),
        (start_x, start_y, jnp.int32(0)),
        (rhs3.shape[0] + 2, rhs3.shape[1] + 2, rhs3.shape[2]),
    )
    finer = pad_depth(window)
    for axis in range(3):
        finer = prolong_axis(finer, axis)
    wide = with_faces(error_two + finer)
    wide = jnp.repeat(jnp.repeat(wide, 4, axis=1), 4, axis=2)
    wide = jnp.pad(wide, ((0, 0), (4, 4), (0, 0)))
    return pl.pallas_call(
        functools.partial(finish_kernel, grid),
        out_shape=jax.ShapeDtypeStruct(smoothed.shape, jnp.float32),
        scratch_shapes=last_scratch(cells_x, cells_y, depth),
        compiler_params=pltpu.CompilerParams(vmem_limit_bytes=VMEM_LIMIT),
        name="finish",
    )(wide, smoothed, error_one)


def on_device(pressure, source, coefficient):
    grid = (lax.axis_size("gx"), lax.axis_size("gy"))
    _, cells_y, depth = pressure.shape
    fits = grid[1] == 4 and cells_y == 32 and depth == 128
    own = (pressure, source, coefficient)
    block = stacked(*own)
    halo = fine_halo(own, block)
    copies = grid[0] * grid[1] if fits else 1
    smoothed, error_one, tiles = smooth(copies, block, halo)
    correct = correct_whole if fits else correct_spread
    return correct(grid, tiles, smoothed, error_one)


def solution(mesh):
    spec = P("gx", "gy", None)
    return jax.shard_map(on_device, mesh=mesh, in_specs=(spec, spec, spec), out_specs=spec, check_vma=False)
```

```python
import functools
import jax
import jax.numpy as jnp
from jax import lax
from jax.experimental import pallas as pl
from jax.experimental.pallas import tpu as pltpu
from jax.sharding import PartitionSpec as P

CSWEEPS = 4
REACH = 9
ORIGIN = 16
VMEM_LIMIT = 48 * 1024 * 1024


def y_rows(distance, array):
    rows = REACH if distance <= 2 else REACH + 2 - distance
    return rows - 1 if array == 1 else rows


def side_entries():
    pairs = [(0, d, (d, d + 1)) for d in range(1, REACH - 1, 2)] + [(0, REACH, (REACH,))]
    return pairs + [(1, d, (d,)) for d in range(1, REACH)] + [(2, d, (d,)) for d in range(1, REACH + 1)]


def x_plan(cells_y):
    first, second = {}, {}
    lengths = [0, 0]

    def put(message, plan, key, row, rows):
        plan.setdefault(key, []).append((row, rows, lengths[message]))
        lengths[message] += rows

    for array, distance, _ in side_entries():
        key = (array, distance)
        ends = y_rows(distance, array)
        put(0, first, key, 0, ends)
        put(0, first, key, cells_y - ends, ends)
        put(1, second, key, ends, cells_y - 2 * ends)
    return first, second, [-(-length // 8) * 8 for length in lengths]


def y_plan(cells_x):
    pieces = []
    start = 0
    inside = [(0, m) for m in range(cells_x // 2)] + [(a, x) for a in (1, 2) for x in range(cells_x)]
    chosen = [("inside", array, index, y_rows(0, array)) for array, index in inside]
    chosen += [("away", array, distance, y_rows(distance, array)) for array, distance, _ in side_entries()]
    for side, array, index, rows in chosen:
        pieces.append((side, array, index, rows, start))
        start += rows
    return pieces, -(-start // 8) * 8


def shifts(axis, step):
    count = lax.axis_size(axis)
    return [(i, i + step) for i in range(count) if 0 <= i + step < count]


def swap_pairs():
    return [(i, i ^ 1) for i in range(lax.axis_size("gx"))]


def x_pairs():
    count = lax.axis_size("gx")
    pairs = [(i, i + 1) for i in range(1, count - 1, 2)]
    return pairs + [(j, i) for i, j in pairs]


def inside_rows(member, own, partner, array, index, first, rows):
    cells_x = own[0].shape[0]
    here = pl.ds(first, rows)

    def plane(x):
        if x // cells_x == member:
            return own[array][x % cells_x, here, :]
        value = partner[array][x % cells_x, here, :]
        return value + value if array == 1 else value

    if array != 0:
        return plane(index)
    depth = own[0].shape[2]
    row = lax.broadcasted_iota(jnp.int32, (rows, depth), 0) + first
    lane = lax.broadcasted_iota(jnp.int32, (rows, depth), 1)
    return jnp.where(((row + lane) & 1) == 1, plane(2 * index), plane(2 * index + 1))


def for_member(body):
    me = lax.axis_index("gx") & 1
    for member in range(2):
        pl.when(me == member)(functools.partial(body, member))


def split_kernel(block, pp, pf, pk, first, second):
    cells_x, cells_y, _ = pp.shape
    p, f, k = views(block, cells_x)
    plans = x_plan(cells_y)

    def body(member):
        for plan, target in zip(plans, (first, second)):
            for (array, distance), pieces in plan.items():
                plane = 2 * cells_x - distance if member == 1 else distance - 1
                index = plane // 2 if array == 0 else plane
                for row, rows, start in pieces:
                    value = inside_rows(member, (p, f, k), (pp, pf, pk), array, index, row, rows)
                    target[pl.ds(start, rows), :] = value

    for_member(body)


def pack_kernel(block, received, to_up, to_down):
    cells_x, cells_y = block.shape[0] // 3, block.shape[1]
    own = views(block, cells_x)
    plan = x_plan(cells_y)[0]

    def piece(side, array, index, rows, row):
        if side == "inside":
            return inside_rows(0, own, None, array, index, row, rows)
        place = [s + row - r for r, count, s in plan[array, index] if r <= row and row + rows <= r + count][0]
        return received[pl.ds(place, rows), :]

    for side, array, index, rows, start in y_plan(cells_x)[0]:
        to_up[pl.ds(start, rows), :] = piece(side, array, index, rows, cells_y - rows)
        to_down[pl.ds(start, rows), :] = piece(side, array, index, rows, 0)


def far_kernel(received, rest, far):
    plans = x_plan(far.shape[1])
    for place, array in ((0, 0), (1, 2)):
        for plan, ref in zip(plans, (received, rest)):
            for row, rows, start in plan[array, 1]:
                far[place, pl.ds(row, rows), :] = ref[pl.ds(start, rows), :]


def stacked(pressure, source, coefficient):
    block = jnp.concatenate([pressure, source, coefficient], 0)
    cells_x = pressure.shape[0]
    plane = lax.broadcasted_iota(jnp.int32, block.shape, 0)
    return block * jnp.where((plane >= cells_x) & (plane < 2 * cells_x), 2.0, 1.0)


def views(block, cells_x):
    return tuple(block.at[pl.ds(n * cells_x, cells_x)] for n in range(3))


def fine_halo(own, block):
    cells_x, cells_y, depth = own[0].shape
    params = pltpu.CompilerParams(vmem_limit_bytes=VMEM_LIMIT)

    def packed(length):
        return jax.ShapeDtypeStruct((length, depth), jnp.float32)

    partner = tuple(lax.ppermute(v, "gx", swap_pairs()) for v in own)
    lengths = x_plan(cells_y)[2]
    first, second = pl.pallas_call(
        split_kernel, out_shape=[packed(n) for n in lengths], compiler_params=params, name="split_block"
    )(block, *partner)
    received = lax.ppermute(first, "gx", x_pairs())
    length = y_plan(cells_x)[1]
    planes = jax.ShapeDtypeStruct((2, cells_y, depth), jnp.float32)
    to_up, to_down = pl.pallas_call(
        pack_kernel, out_shape=[packed(length), packed(length)], compiler_params=params, name="pack_halo"
    )(block, received)
    below = lax.ppermute(to_up, "gy", shifts("gy", 1))
    above = lax.ppermute(to_down, "gy", shifts("gy", -1))
    rest = lax.ppermute(second, "gx", x_pairs())
    outermost = pl.pallas_call(far_kernel, out_shape=planes, compiler_params=params, name="far_planes")(received, rest)
    far = lax.ppermute(outermost, "gx", swap_pairs())
    above, far, rest = lax.optimization_barrier((above, far, rest))
    p_below = lax.ppermute(below, "gx", swap_pairs())
    p_above = lax.ppermute(above, "gx", swap_pairs())
    return *partner, received, rest, far, below, above, p_below, p_above


def smooth_kernel(
    block, pp, pf, pk, received, rest, far, below, above, p_below, p_above,
    out, error_one, tiles,
    vp, vf, vk, wx, wy, zl, zh, dg, inv, va, vb,
    t0, t1, f1, k1, inv1, g1, h1, q2,
):
    cells_x, cells_y, depth = pp.shape
    planes = cells_x + 2 * REACH
    own_rows = pl.ds(ORIGIN, cells_y)
    top = ORIGIN - REACH + 1
    rows = cells_y + 2 * (REACH - 1)
    body = pl.ds(top, rows)

    windows = (vp, vf, vk)
    first_plan, second_plan, _ = x_plan(cells_y)

    def fill(array, x, first, value):
        if x < -REACH or x >= cells_x + REACH or (array == 1 and (x == -REACH or x == cells_x + REACH - 1)):
            return
        windows[array][REACH + x, pl.ds(ORIGIN + first, value.shape[0]), :] = value

    for x in range(cells_x):
        for array, ref in enumerate(views(block, cells_x)):
            fill(array, x, 0, ref[x])

    spans = {(array, distance): distances for array, distance, distances in side_entries()}

    def outside(side, distance):
        return -distance if side == "low" else cells_x - 1 + distance

    def fill_member(member):
        away, near = (("low", "high"), ("high", "low"))[member]
        for x in range(cells_x):
            for array, ref in enumerate((pp, pf, pk)):
                value = ref[x]
                fill(array, x + cells_x * (1 - 2 * member), 0, value + value if array == 1 else value)
        fill(0, outside(near, REACH), 0, far[0])
        fill(2, outside(near, REACH), 0, far[1])
        for plan, ref in ((first_plan, received), (second_plan, rest)):
            for (array, distance), pieces in plan.items():
                for row, count, start in pieces:
                    value = ref[pl.ds(start, count), :]
                    for each in spans[array, distance]:
                        fill(array, outside(away, each), row, value)

        towards_partner = cells_x * (1 - 2 * member)
        for before, after, is_partner in ((below, above, False), (p_below, p_above, True)):
            for side, array, index, count, start in y_plan(cells_x)[0]:
                if side == "inside":
                    xs = (2 * index, 2 * index + 1) if array == 0 else (index,)
                    xs = [x + towards_partner * is_partner for x in xs]
                elif is_partner:
                    xs = [outside(near, cells_x + each) for each in spans[array, index]]
                else:
                    xs = [outside(away, each) for each in spans[array, index]]
                for x in xs:
                    fill(array, x, -count, before[pl.ds(start, count), :])
                    fill(array, x, cells_y, after[pl.ds(start, count), :])

    for_member(fill_member)

    def lanes(count):
        return lax.broadcasted_iota(jnp.int32, (count, depth), 1)

    def rows_of(first, count):
        return lax.broadcasted_iota(jnp.int32, (count, depth), 0) + (first - ORIGIN)

    lane = lanes(rows)

    def weigh(plane, _):
        centre = vk[plane, body, :]
        west = centre + vk[plane - 1, body, :]
        wx[plane, body, :] = west
        east = centre + vk[plane + 1, body, :]
        south = centre + vk[plane, pl.ds(top - 1, rows), :]
        north = centre + vk[plane, pl.ds(top + 1, rows), :]
        wy[plane, body, :] = south
        wy[plane, pl.ds(top + rows, 1), :] = north[rows - 1:, :]
        down = jnp.where(lane > 0, pltpu.roll(centre, 1, 1), 0.0)
        up = jnp.where(lane < depth - 1, pltpu.roll(centre, depth - 1, 1), 0.0)
        total = west + east + south + north + (centre + down) + (centre + up)
        zl[plane, body, :] = jnp.where(lane > 0, centre + down, 0.0)
        zh[plane, body, :] = jnp.where(lane < depth - 1, centre + up, 0.0)
        dg[plane, body, :] = total
        inside = centre > 0.0
        inv[plane, body, :] = jnp.where(inside, 1.0 / jnp.where(inside, total, 1.0), 0.0)
        return 0

    lax.fori_loop(1, planes - 1, weigh, 0, unroll=True)
    wx[planes - 1, body, :] = vk[planes - 1, body, :] + vk[planes - 2, body, :]

    def stencil(v, plane, first, count):
        here = pl.ds(first, count)
        centre = v[plane, here, :]
        total = wx[plane, here, :] * v[plane - 1, here, :] + wx[plane + 1, here, :] * v[plane + 1, here, :]
        total += wy[plane, here, :] * v[plane, pl.ds(first - 1, count), :]
        total += wy[plane, pl.ds(first + 1, count), :] * v[plane, pl.ds(first + 1, count), :]
        total += zl[plane, here, :] * pltpu.roll(centre, 1, 1)
        total += zh[plane, here, :] * pltpu.roll(centre, depth - 1, 1)
        return total

    def relax(source_ref, target, reach):
        def one(plane, _):
            total = stencil(source_ref, plane, top, rows)
            target[plane, body, :] = inv[plane, body, :] * (vf[plane, body, :] + total)
            return 0

        lax.fori_loop(REACH - reach, REACH + cells_x + reach, one, 0, unroll=True)

    relax(vp, va, REACH - 1)
    relax(va, vb, REACH - 2)
    relax(vb, va, REACH - 3)
    relax(va, vb, REACH - 4)

    own_lane = lanes(cells_y)
    own_row = rows_of(ORIGIN, cells_y)
    for x in range(cells_x):
        even = ((own_row + own_lane + x) & 1) == 0
        out[x] = jnp.where(even, va[REACH + x, own_rows, :], vb[REACH + x, own_rows, :])

    planes_one = cells_x // 2
    first = ORIGIN - 4
    count = cells_y + 8
    lane = lanes(count)
    row = rows_of(first, count)

    def pair_lane(value, stride, lane):
        up = pltpu.roll(value, depth - stride, 1)
        down = pltpu.roll(value, stride, 1)
        return value + jnp.where((lane & stride) == 0, up, down)

    def pair_row(ref, index, first, count, stride, row):
        centre = ref[index, pl.ds(first, count), :]
        up = ref[index, pl.ds(first + stride, count), :]
        down = ref[index, pl.ds(first - stride, count), :]
        return centre + jnp.where((row & stride) == 0, up, down)

    def residual(plane_one, _):
        total = jnp.zeros((count, depth), jnp.float32)
        for half in range(2):
            plane = 2 * plane_one + REACH - 4 + half
            here = pl.ds(first, count)
            twice = vf[plane, here, :] - dg[plane, here, :] * va[plane, here, :] + stencil(vb, plane, first, count)
            even = ((row + lane + half) & 1) == 0
            total += jnp.where(even, twice, 0.0)
        t0[plane_one, pl.ds(first, count), :] = pair_lane(total, 1, lane)
        return 0

    lax.fori_loop(0, planes_one + 4, residual, 0, unroll=True)
    for x in range(planes_one + 4):
        f1[x, pl.ds(first, count), :] = 0.5 * pair_row(t0, x, first, count, 1, row)

    first_k = ORIGIN - 6
    count_k = cells_y + 16
    lane_k = lanes(count_k)
    row_k = rows_of(first_k, count_k)
    for x in range(planes_one + 6):
        plane = 2 * x + REACH - 6
        here = pl.ds(first_k, count_k)
        t1[x, here, :] = pair_lane(vk[plane, here, :] + vk[plane + 1, here, :], 1, lane_k)
    for x in range(planes_one + 6):
        k1[x, pl.ds(first_k, count_k), :] = 0.125 * pair_row(t1, x, first_k, count_k, 1, row_k)

    def down2(value, lane):
        return jnp.where(lane >= 2, pltpu.roll(value, 2, 1), 0.0)

    def up2(value, lane):
        return jnp.where(lane < depth - 2, pltpu.roll(value, depth - 2, 1), 0.0)

    here = pl.ds(first, count)
    for x in range(planes_one + 4):
        centre = k1[x + 1, here, :]
        total = 6.0 * centre + (k1[x, here, :] + k1[x + 2, here, :])
        total += k1[x + 1, pl.ds(first - 2, count), :] + k1[x + 1, pl.ds(first + 2, count), :]
        total += down2(centre, lane) + up2(centre, lane)
        inside = centre > 0.0
        inverse = jnp.where(inside, 1.0 / jnp.where(inside, total, 1.0), 0.0)
        inv1[x, here, :] = inverse
        g1[x, here, :] = inverse * f1[x, here, :]

    def stencil_one(v, x, v_x, first, count, lane):
        here = pl.ds(first, count)
        south = pl.ds(first - 2, count)
        north = pl.ds(first + 2, count)
        kc = k1[x, here, :]
        vc = v[v_x, here, :]
        total = (kc + k1[x - 1, here, :]) * v[v_x - 1, here, :] + (kc + k1[x + 1, here, :]) * v[v_x + 1, here, :]
        total += (kc + k1[x, south, :]) * v[v_x, south, :] + (kc + k1[x, north, :]) * v[v_x, north, :]
        total += (kc + down2(kc, lane)) * down2(vc, lane) + (kc + up2(kc, lane)) * up2(vc, lane)
        return total

    first_h = ORIGIN - 2
    count_h = cells_y + 8
    lane_h = lanes(count_h)
    row_h = rows_of(first_h, count_h)
    for x in range(planes_one + 2):
        here = pl.ds(first_h, count_h)
        total = stencil_one(g1, x + 2, x + 1, first_h, count_h, lane_h)
        odd = inv1[x + 1, here, :] * (f1[x + 1, here, :] + total)
        h1[x, here, :] = odd
        even_cell = ((x - 1 + (row_h >> 1) + (lane_h >> 1)) & 1) == 0
        error_one[x, pl.ds(first_h - 8, count_h), :] = jnp.where(even_cell, g1[x + 1, here, :], odd)

    own2 = own_lane
    row2 = own_row
    for x in range(planes_one // 2):
        sum_r = jnp.zeros((cells_y, depth), jnp.float32)
        for half in range(2):
            x1 = 2 * x + half
            total = stencil_one(h1, x1 + 3, x1 + 1, ORIGIN, cells_y, own2)
            even_cell = ((x1 + (row2 >> 1) + (own2 >> 1)) & 1) == 0
            sum_r += jnp.where(even_cell, total, 0.0)
        sum_k = k1[2 * x + 3, own_rows, :] + k1[2 * x + 4, own_rows, :]
        t0[x, own_rows, :] = pair_lane(sum_r, 2, own2)
        t1[x, own_rows, :] = pair_lane(sum_k, 2, own2)
    lane8 = lanes(cells_y // 4)
    tile = jnp.zeros((cells_y // 4, depth), jnp.float32)
    for x in range(planes_one // 2):
        q2[0] = (1.0 / 64.0) * pair_row(t0, x, ORIGIN, cells_y, 2, row2)
        q2[1] = 0.125 * pair_row(t1, x, ORIGIN, cells_y, 2, row2)
        for field in range(2):
            kept = q2[field, pl.ds(0, cells_y // 4, stride=4), :]
            tile = jnp.where((lane8 & 3) == 2 * field + x, kept, tile)
    tiles[...] = jnp.broadcast_to(tile[None], tiles.shape)


def smooth(copies, block, halo):
    cells_x, cells_y, depth = halo[0].shape
    planes = cells_x + 2 * REACH
    tall = cells_y + 2 * ORIGIN
    planes_one = cells_x // 2
    window = pltpu.VMEM((planes, tall, depth), jnp.float32)

    def level_one(count):
        return pltpu.VMEM((count, tall, depth), jnp.float32)

    return pl.pallas_call(
        smooth_kernel,
        out_shape=(
            jax.ShapeDtypeStruct((cells_x, cells_y, depth), jnp.float32),
            jax.ShapeDtypeStruct((planes_one + 2, cells_y + 16, depth), jnp.float32),
            jax.ShapeDtypeStruct((copies, cells_y // 4, depth), jnp.float32),
        ),
        scratch_shapes=[window] * 11
        + [
            level_one(planes_one + 4),
            level_one(planes_one + 6),
            level_one(planes_one + 4),
            level_one(planes_one + 6),
            level_one(planes_one + 4),
            level_one(planes_one + 4),
            level_one(planes_one + 2),
            pltpu.VMEM((2, cells_y, depth), jnp.float32),
        ],
        compiler_params=pltpu.CompilerParams(vmem_limit_bytes=VMEM_LIMIT),
        name="smooth",
    )(block, *halo)


def ring(value, shift, axis):
    return pltpu.roll(value, shift % value.shape[axis], axis)


def before_x(v):
    return jnp.concatenate([jnp.zeros_like(v[:1]), v[:-1]], 0)


def after_x(v):
    return jnp.concatenate([v[1:], jnp.zeros_like(v[:1])], 0)


class Places:
    def __init__(self, shape):
        self.row = lax.broadcasted_iota(jnp.int32, shape, 1)
        self.lane = lax.broadcasted_iota(jnp.int32, shape, 2)
        self.part = self.lane & 3
        self.depth = shape[2]

    def before_y(self, v, stride):
        turned = ring(v, stride, 1)
        return jnp.where(self.row >= stride, turned, ring(turned, 1, 2))

    def after_y(self, v, stride):
        turned = ring(v, -stride, 1)
        return jnp.where(self.row < 8 - stride, turned, ring(turned, -1, 2))

    def has_before_y(self, stride):
        return (self.row >= stride) | (self.part > 0)

    def has_after_y(self, stride):
        return (self.row < 8 - stride) | (self.part < 3)

    def has_before_z(self, stride):
        return self.lane >= 4 * stride

    def has_after_z(self, stride):
        return self.lane < self.depth - 4 * stride


def whole_weights(k, places, stride):
    west = k + before_x(k)
    east = k + after_x(k)
    masks = (
        places.has_before_y(stride),
        places.has_after_y(stride),
        places.has_before_z(stride),
        places.has_after_z(stride),
    )
    near = (
        places.before_y(k, stride),
        places.after_y(k, stride),
        ring(k, 4 * stride, 2),
        ring(k, -4 * stride, 2),
    )
    diagonal = west + east
    weights = [west, east]
    for mask, value in zip(masks, near):
        diagonal += k + jnp.where(mask, value, 0.0)
        weights.append(jnp.where(mask, k + value, 0.0))
    return weights, diagonal


def whole_sum(v, weights, places, stride):
    total = weights[0] * before_x(v) + weights[1] * after_x(v)
    total += weights[2] * places.before_y(v, stride) + weights[3] * places.after_y(v, stride)
    total += weights[4] * ring(v, 4 * stride, 2) + weights[5] * ring(v, -4 * stride, 2)
    return total


def whole_solve(k2, rhs2):
    planes = k2.shape[0]
    places = Places(k2.shape)
    weights, diagonal = whole_weights(k2, places, 1)
    parity = lax.broadcasted_iota(jnp.int32, k2.shape, 0) + places.row + (places.lane >> 2)
    even = (parity & 1) == 0
    inverse = 1.0 / diagonal
    scaled = 32.0 * rhs2
    even_values = inverse * scaled
    odd_values = inverse * (scaled + whole_sum(even_values, weights, places, 1))
    error_two = jnp.where(even, even_values, odd_values)
    left = jnp.where(even, whole_sum(odd_values, weights, places, 1), 0.0)

    half = places.row[: planes // 2] , places.lane[: planes // 2]
    first_row = (half[0] & 1) == 0
    first_lane = (half[1] & 4) == 0

    def coarse(v):
        v = v.reshape(planes // 2, 2, *v.shape[1:])
        v = v[:, 0] + v[:, 1]
        v = v + jnp.where(first_row, ring(v, -1, 1), ring(v, 1, 1))
        return v + jnp.where(first_lane, ring(v, -4, 2), ring(v, 4, 2))

    remain = (1.0 / 256.0) * coarse(left)
    k3 = 0.125 * coarse(k2)
    places3 = Places(k3.shape)
    weights3, diagonal3 = whole_weights(k3, places3, 2)

    def total(v):
        return jnp.sum(jnp.sum(v, axis=0, keepdims=True), axis=(1, 2), keepdims=True)

    def around(v):
        return (
            places3.before_y(v, 2), places3.after_y(v, 2), ring(v, 8, 2), ring(v, -8, 2),
        )

    direction, sides = remain, around(remain)
    remain_sides = sides
    norm_now = total(remain * remain)
    error = error_before = error_after = jnp.zeros_like(remain)
    for repeat in range(CSWEEPS):
        coupled = weights3[0] * before_x(direction) + weights3[1] * after_x(direction)
        coupled += weights3[2] * sides[0] + weights3[3] * sides[1]
        coupled += weights3[4] * sides[2] + weights3[5] * sides[3]
        image = (diagonal3 * direction - coupled) * (1.0 / 128.0)
        alpha = norm_now / total(direction * image)
        error = error + alpha * direction
        error_before = error_before + alpha * sides[0]
        error_after = error_after + alpha * sides[1]
        if repeat == CSWEEPS - 1:
            break
        image_sides = around(image)
        remain = remain - alpha * image
        remain_sides = [r - alpha * q for r, q in zip(remain_sides, image_sides)]
        norm_next = total(remain * remain)
        beta = norm_next / norm_now
        direction = remain + beta * direction
        sides = [r + beta * p for r, p in zip(remain_sides, sides)]
        norm_now = norm_next

    near = jnp.where(
        first_row,
        jnp.where(places3.has_before_y(2), error_before, 0.0),
        jnp.where(places3.has_after_y(2), error_after, 0.0),
    )
    error = 0.75 * error + 0.25 * near
    lower = 0.75 * error + 0.25 * before_x(error)
    upper = 0.75 * error + 0.25 * after_x(error)
    fine = jnp.stack([lower, upper], 1).reshape(k2.shape)
    near = jnp.where(
        (places.lane & 4) == 0,
        jnp.where(places.has_before_z(1), ring(fine, 4, 2), 0.0),
        jnp.where(places.has_after_z(1), ring(fine, -4, 2), 0.0),
    )
    return error_two + (0.75 * fine + 0.25 * near)


def finish(grid, wide, smoothed, error_one, out, e1, e0):
    cells_x, cells_y, depth = smoothed.shape
    i, j = lax.axis_index("gx"), lax.axis_index("gy")
    first = 8 - 2
    count = cells_y + 8
    lane = lax.broadcasted_iota(jnp.int32, (count, depth), 1)
    row = lax.broadcasted_iota(jnp.int32, (count, depth), 0) - 2

    def widen_z(value, stride, lane):
        down = jnp.where(lane >= stride, pltpu.roll(value, stride, 1), 0.0)
        up = jnp.where(lane < depth - stride, pltpu.roll(value, depth - stride, 1), 0.0)
        return 0.75 * value + 0.25 * jnp.where((lane & stride) == 0, down, up)

    def widen_y(ref, index, first, count, stride, row):
        centre = ref[index, pl.ds(first, count), :]
        down = ref[index, pl.ds(first - stride, count), :]
        up = ref[index, pl.ds(first + stride, count), :]
        return 0.75 * centre + 0.25 * jnp.where((row & stride) == 0, down, up)

    low_row = jnp.where(j > 0, -cells_y, 0)
    high_row = jnp.where(j < grid[1] - 1, 2 * cells_y, cells_y)
    inside = (row >= low_row) & (row < high_row)
    planes_two = cells_x // 4 + 2
    mid = [widen_z(widen_y(wide, x, first, count, 2, row), 2, lane) for x in range(planes_two)]
    for x in range(cells_x // 2 + 2):
        centre = (x + 1) // 2
        near = centre + (1 if x % 2 == 0 else -1)
        value = jnp.where(inside, 0.75 * mid[centre] + 0.25 * mid[near], 0.0)
        if x == 0:
            value = jnp.where(i > 0, value, 0.0)
        if x == cells_x // 2 + 1:
            value = jnp.where(i < grid[0] - 1, value, 0.0)
        here = pl.ds(first, count)
        e1[x, here, :] = error_one[x, here, :] + value

    lane = lax.broadcasted_iota(jnp.int32, (cells_y, depth), 1)
    row = lax.broadcasted_iota(jnp.int32, (cells_y, depth), 0)
    for x in range(cells_x // 2 + 2):
        e0[x] = widen_z(widen_y(e1, x, 8, cells_y, 1, row), 1, lane)
    for x in range(cells_x):
        centre = x // 2 + 1
        near = centre + (-1 if x % 2 == 0 else 1)
        out[x] = smoothed[x] + (0.75 * e0[centre] + 0.25 * e0[near])


def correct_kernel(grid, gathered, smoothed, error_one, out, whole, strip, wide, e1, e0):
    cells_y = smoothed.shape[1]
    nx, ny = grid
    i, j = lax.axis_index("gx"), lax.axis_index("gy")
    lane = lax.broadcasted_iota(jnp.int32, (8, 128), 1) & 3
    fields = [[], []]
    for column in range(nx):
        parts = [gathered[column * ny + part] for part in range(ny)]
        for field in range(2):
            for x in range(2):
                place = 2 * field + x
                plane = None
                for part in range(ny):
                    turned = parts[part] if part == place else ring(parts[part], part - place, 1)
                    plane = turned if plane is None else jnp.where(lane == part, turned, plane)
                fields[field].append(plane)
    rhs2 = jnp.stack(fields[0], 0)
    k2 = jnp.stack(fields[1], 0)
    planes = 2 * nx
    whole[0] = jnp.zeros((8, 128), jnp.float32)
    whole[planes + 1] = jnp.zeros((8, 128), jnp.float32)
    whole[pl.ds(1, planes)] = whole_solve(k2, rhs2)

    masks = [[(j + side - lane) == shift for shift in range(-4, 5)] for side in (-1, 0, 1)]
    inside = (j > 0, True, j < ny - 1)
    for x in range(4):
        plane = whole[2 * i + x]
        turned = [plane if shift == 0 else ring(plane, -shift, 1) for shift in range(-4, 5)]
        for index in range(3):
            value = jnp.zeros_like(plane)
            for mask, each in zip(masks[index], turned):
                value = jnp.where(mask, each, value)
            strip[x, pl.ds(8 * index, 8), :] = value if index == 1 else jnp.where(inside[index], value, 0.0)
        for place in range(4):
            wide[x, pl.ds(4 + place, 8, stride=4), :] = strip[x, pl.ds(7, 8), :]
            wide[x, pl.ds(36 + place, 2, stride=4), :] = strip[x, pl.ds(15, 2), :]
    finish(grid, wide, smoothed, error_one, out, e1, e0)


def finish_kernel(grid, wide, smoothed, error_one, out, e1, e0):
    finish(grid, wide, smoothed, error_one, out, e1, e0)


def last_scratch(cells_x, cells_y, depth):
    count = cells_x // 2 + 2
    return [
        pltpu.VMEM((count, cells_y + 16, depth), jnp.float32),
        pltpu.VMEM((count, cells_y, depth), jnp.float32),
    ]


def correct_whole(grid, tiles, smoothed, error_one):
    gathered = lax.all_to_all(tiles, ("gx", "gy"), 0, 0, tiled=False)
    cells_x, cells_y, depth = smoothed.shape
    return pl.pallas_call(
        functools.partial(correct_kernel, grid),
        out_shape=jax.ShapeDtypeStruct(smoothed.shape, jnp.float32),
        scratch_shapes=[
            pltpu.VMEM((2 * grid[0] + 2, 8, depth), jnp.float32),
            pltpu.VMEM((4, 24, depth), jnp.float32),
            pltpu.VMEM((4, cells_y + 16, depth), jnp.float32),
        ]
        + last_scratch(cells_x, cells_y, depth),
        compiler_params=pltpu.CompilerParams(vmem_limit_bytes=VMEM_LIMIT),
        name="correct",
    )(gathered, smoothed, error_one)


def with_faces(shard):
    for axis, dim in (("gx", 0), ("gy", 1)):
        length = shard.shape[dim]
        last = lax.slice_in_dim(shard, length - 1, length, axis=dim)
        initial = lax.slice_in_dim(shard, 0, 1, axis=dim)
        before = lax.ppermute(last, axis, shifts(axis, 1))
        after = lax.ppermute(initial, axis, shifts(axis, -1))
        shard = jnp.concatenate([before, shard, after], axis=dim)
    return shard


def with_zeros(field):
    return jnp.pad(field, ((1, 1), (1, 1), (0, 0)))


def pad_depth(field):
    return jnp.pad(field, ((0, 0), (0, 0), (1, 1)))


def restrict(field):
    size_x, size_y, size_z = field.shape
    return field.reshape(size_x // 2, 2, size_y // 2, 2, size_z // 2, 2).mean(axis=(1, 3, 5))


def level_weights(coef_pad):
    c = pad_depth(coef_pad)
    wx = (c[1:, 1:-1, 1:-1] + c[:-1, 1:-1, 1:-1]) * 0.5
    wy = (c[1:-1, 1:, 1:-1] + c[1:-1, :-1, 1:-1]) * 0.5
    wz = (c[1:-1, 1:-1, 1:] + c[1:-1, 1:-1, :-1]) * 0.5
    diagonal = wx[1:] + wx[:-1] + wy[:, 1:] + wy[:, :-1] + wz[:, :, 1:] + wz[:, :, :-1]
    return (wx, wy, wz), diagonal


def neighbour_sum(field_pad, weights):
    wx, wy, wz = weights
    v = pad_depth(field_pad)
    total = wx[:-1] * v[:-2, 1:-1, 1:-1] + wx[1:] * v[2:, 1:-1, 1:-1]
    total = total + wy[:, :-1] * v[1:-1, :-2, 1:-1] + wy[:, 1:] * v[1:-1, 2:, 1:-1]
    return total + wz[:, :, :-1] * v[1:-1, 1:-1, :-2] + wz[:, :, 1:] * v[1:-1, 1:-1, 2:]


def prolong_axis(padded, axis):
    length = padded.shape[axis]
    middle = lax.slice_in_dim(padded, 1, length - 1, axis=axis)
    before = lax.slice_in_dim(padded, 0, length - 2, axis=axis)
    after = lax.slice_in_dim(padded, 2, length, axis=axis)
    joined = jnp.stack([0.75 * middle + 0.25 * before, 0.75 * middle + 0.25 * after], axis=axis + 1)
    shape = list(middle.shape)
    shape[axis] = 2 * shape[axis]
    return joined.reshape(shape)


def coarse_solve(rhs, weights, diagonal):
    error = jnp.zeros_like(rhs)
    remain = rhs
    direction = rhs
    norm_now = jnp.sum(remain * remain)
    for _ in range(CSWEEPS):
        image = (diagonal * direction - neighbour_sum(with_zeros(direction), weights)) * 4.0**-3
        alpha = norm_now / jnp.sum(direction * image)
        error = error + alpha * direction
        remain = remain - alpha * image
        norm_next = jnp.sum(remain * remain)
        direction = remain + norm_next / norm_now * direction
        norm_now = norm_next
    return error


def correct_spread(grid, tiles, smoothed, error_one):
    cells_x, cells_y, depth = smoothed.shape
    shape2 = (cells_x // 4, cells_y // 4, depth // 4)
    own = tiles[0].reshape(shape2[1], shape2[2], 2, shape2[0]).transpose(2, 3, 0, 1)
    rhs2, k2 = own[0], own[1]
    weights, diagonal = level_weights(with_faces(k2))
    parity = sum(lax.broadcasted_iota(jnp.int32, shape2, d) for d in range(3)) % 2
    error_two = jnp.where(parity == 0, rhs2 * 16.0 / diagonal, 0.0)
    total = neighbour_sum(with_faces(error_two), weights)
    error_two = jnp.where(parity == 1, (rhs2 * 16.0 + total) / diagonal, error_two)
    total = neighbour_sum(with_faces(error_two), weights)
    rhs3 = restrict(rhs2 - (diagonal * error_two - total) * 4.0**-2)
    merged = jnp.stack([rhs3, restrict(k2)])
    merged = lax.all_gather(merged, "gx", axis=1, tiled=True)
    merged = lax.all_gather(merged, "gy", axis=2, tiled=True)
    weights3, diagonal3 = level_weights(with_zeros(merged[1]))
    error_three = coarse_solve(merged[0], weights3, diagonal3)
    start_x = lax.axis_index("gx") * rhs3.shape[0]
    start_y = lax.axis_index("gy") * rhs3.shape[1]
    window = lax.dynamic_slice(
        with_zeros(error_three),
        (start_x, start_y, jnp.int32(0)),
        (rhs3.shape[0] + 2, rhs3.shape[1] + 2, rhs3.shape[2]),
    )
    finer = pad_depth(window)
    for axis in range(3):
        finer = prolong_axis(finer, axis)
    wide = with_faces(error_two + finer)
    wide = jnp.repeat(jnp.repeat(wide, 4, axis=1), 4, axis=2)
    wide = jnp.pad(wide, ((0, 0), (4, 4), (0, 0)))
    return pl.pallas_call(
        functools.partial(finish_kernel, grid),
        out_shape=jax.ShapeDtypeStruct(smoothed.shape, jnp.float32),
        scratch_shapes=last_scratch(cells_x, cells_y, depth),
        compiler_params=pltpu.CompilerParams(vmem_limit_bytes=VMEM_LIMIT),
        name="finish",
    )(wide, smoothed, error_one)


def on_device(pressure, source, coefficient):
    grid = (lax.axis_size("gx"), lax.axis_size("gy"))
    _, cells_y, depth = pressure.shape
    fits = grid[1] == 4 and cells_y == 32 and depth == 128
    own = (pressure, source, coefficient)
    block = stacked(*own)
    halo = fine_halo(own, block)
    copies = grid[0] * grid[1] if fits else 1
    smoothed, error_one, tiles = smooth(copies, block, halo)
    correct = correct_whole if fits else correct_spread
    return correct(grid, tiles, smoothed, error_one)


def solution(mesh):
    spec = P("gx", "gy", None)
    return jax.shard_map(on_device, mesh=mesh, in_specs=(spec, spec, spec), out_specs=spec, check_vma=False)
```

```python
import functools
import jax
import jax.numpy as jnp
from jax import lax
from jax.experimental import pallas as pl
from jax.experimental.pallas import tpu as pltpu
from jax.sharding import PartitionSpec as P

CSWEEPS = 4
REACH = 9
ORIGIN = 16
VMEM_LIMIT = 48 * 1024 * 1024


def y_rows(distance, array):
    rows = REACH if distance <= 2 else REACH + 2 - distance
    return rows - 1 if array == 1 else rows


def side_entries():
    pairs = [(0, d, (d, d + 1)) for d in range(1, REACH - 1, 2)] + [(0, REACH, (REACH,))]
    return pairs + [(1, d, (d,)) for d in range(1, REACH)] + [(2, d, (d,)) for d in range(1, REACH + 1)]


def x_plan(cells_y):
    first, second = {}, {}
    lengths = [0, 0]

    def put(message, plan, key, row, rows):
        plan.setdefault(key, []).append((row, rows, lengths[message]))
        lengths[message] += rows

    for array, distance, _ in side_entries():
        key = (array, distance)
        ends = y_rows(distance, array)
        put(0, first, key, 0, ends)
        put(0, first, key, cells_y - ends, ends)
        put(1, second, key, ends, cells_y - 2 * ends)
    return first, second, [-(-length // 8) * 8 for length in lengths]


def y_plan(cells_x):
    pieces = []
    start = 0
    inside = [(0, m) for m in range(cells_x // 2)] + [(a, x) for a in (1, 2) for x in range(cells_x)]
    chosen = [("inside", array, index, y_rows(0, array)) for array, index in inside]
    chosen += [("away", array, distance, y_rows(distance, array)) for array, distance, _ in side_entries()]
    for side, array, index, rows in chosen:
        pieces.append((side, array, index, rows, start))
        start += rows
    return pieces, -(-start // 8) * 8


def shifts(axis, step):
    count = lax.axis_size(axis)
    return [(i, i + step) for i in range(count) if 0 <= i + step < count]


def swap_pairs():
    return [(i, i ^ 1) for i in range(lax.axis_size("gx"))]


def x_pairs():
    count = lax.axis_size("gx")
    pairs = [(i, i + 1) for i in range(1, count - 1, 2)]
    return pairs + [(j, i) for i, j in pairs]


def inside_rows(member, own, partner, array, index, first, rows):
    cells_x = own[0].shape[0]
    here = pl.ds(first, rows)

    def plane(x):
        if x // cells_x == member:
            return own[array][x % cells_x, here, :]
        value = partner[array][x % cells_x, here, :]
        return value + value if array == 1 else value

    if array != 0:
        return plane(index)
    depth = own[0].shape[2]
    row = lax.broadcasted_iota(jnp.int32, (rows, depth), 0) + first
    lane = lax.broadcasted_iota(jnp.int32, (rows, depth), 1)
    return jnp.where(((row + lane) & 1) == 1, plane(2 * index), plane(2 * index + 1))


def for_member(body):
    me = lax.axis_index("gx") & 1
    for member in range(2):
        pl.when(me == member)(functools.partial(body, member))


def split_kernel(block, pp, pf, pk, first, second):
    cells_x, cells_y, _ = pp.shape
    p, f, k = views(block, cells_x)
    plans = x_plan(cells_y)

    def body(member):
        for plan, target in zip(plans, (first, second)):
            for (array, distance), pieces in plan.items():
                plane = 2 * cells_x - distance if member == 1 else distance - 1
                index = plane // 2 if array == 0 else plane
                for row, rows, start in pieces:
                    value = inside_rows(member, (p, f, k), (pp, pf, pk), array, index, row, rows)
                    target[pl.ds(start, rows), :] = value

    for_member(body)


def pack_kernel(block, received, to_up, to_down):
    cells_x, cells_y = block.shape[0] // 3, block.shape[1]
    own = views(block, cells_x)
    plan = x_plan(cells_y)[0]

    def piece(side, array, index, rows, row):
        if side == "inside":
            return inside_rows(0, own, None, array, index, row, rows)
        place = [s + row - r for r, count, s in plan[array, index] if r <= row and row + rows <= r + count][0]
        return received[pl.ds(place, rows), :]

    for side, array, index, rows, start in y_plan(cells_x)[0]:
        to_up[pl.ds(start, rows), :] = piece(side, array, index, rows, cells_y - rows)
        to_down[pl.ds(start, rows), :] = piece(side, array, index, rows, 0)


def far_kernel(received, rest, far):
    plans = x_plan(far.shape[1])
    for place, array in ((0, 0), (1, 2)):
        for plan, ref in zip(plans, (received, rest)):
            for row, rows, start in plan[array, 1]:
                far[place, pl.ds(row, rows), :] = ref[pl.ds(start, rows), :]


def stacked(pressure, source, coefficient):
    block = jnp.concatenate([pressure, source, coefficient], 0)
    cells_x = pressure.shape[0]
    plane = lax.broadcasted_iota(jnp.int32, block.shape, 0)
    return block * jnp.where((plane >= cells_x) & (plane < 2 * cells_x), 2.0, 1.0)


def views(block, cells_x):
    return tuple(block.at[pl.ds(n * cells_x, cells_x)] for n in range(3))


def fine_halo(own, block):
    cells_x, cells_y, depth = own[0].shape
    params = pltpu.CompilerParams(vmem_limit_bytes=VMEM_LIMIT)

    def packed(length):
        return jax.ShapeDtypeStruct((length, depth), jnp.float32)

    partner = tuple(lax.ppermute(v, "gx", swap_pairs()) for v in own)
    lengths = x_plan(cells_y)[2]
    first, second = pl.pallas_call(
        split_kernel, out_shape=[packed(n) for n in lengths], compiler_params=params, name="split_block"
    )(block, *partner)
    received = lax.ppermute(first, "gx", x_pairs())
    length = y_plan(cells_x)[1]
    planes = jax.ShapeDtypeStruct((2, cells_y, depth), jnp.float32)
    to_up, to_down = pl.pallas_call(
        pack_kernel, out_shape=[packed(length), packed(length)], compiler_params=params, name="pack_halo"
    )(block, received)
    below = lax.ppermute(to_up, "gy", shifts("gy", 1))
    above = lax.ppermute(to_down, "gy", shifts("gy", -1))
    rest = lax.ppermute(second, "gx", x_pairs())
    outermost = pl.pallas_call(far_kernel, out_shape=planes, compiler_params=params, name="far_planes")(received, rest)
    far = lax.ppermute(outermost, "gx", swap_pairs())
    above, far, rest = lax.optimization_barrier((above, far, rest))
    p_below = lax.ppermute(below, "gx", swap_pairs())
    p_above = lax.ppermute(above, "gx", swap_pairs())
    return *partner, received, rest, far, below, above, p_below, p_above


def smooth_kernel(
    block, pp, pf, pk, received, rest, far, below, above, p_below, p_above,
    out, error_one, tiles,
    vp, vf, vk, wx, wy, zl, zh, dg, inv, va, vb,
    t0, t1, f1, k1, inv1, g1, h1, q2,
):
    cells_x, cells_y, depth = pp.shape
    planes = cells_x + 2 * REACH
    own_rows = pl.ds(ORIGIN, cells_y)
    top = ORIGIN - REACH + 1
    rows = cells_y + 2 * (REACH - 1)
    body = pl.ds(top, rows)

    windows = (vp, vf, vk)
    first_plan, second_plan, _ = x_plan(cells_y)

    def fill(array, x, first, value):
        if x < -REACH or x >= cells_x + REACH or (array == 1 and (x == -REACH or x == cells_x + REACH - 1)):
            return
        windows[array][REACH + x, pl.ds(ORIGIN + first, value.shape[0]), :] = value

    for x in range(cells_x):
        for array, ref in enumerate(views(block, cells_x)):
            fill(array, x, 0, ref[x])

    spans = {(array, distance): distances for array, distance, distances in side_entries()}

    def outside(side, distance):
        return -distance if side == "low" else cells_x - 1 + distance

    def fill_member(member):
        away, near = (("low", "high"), ("high", "low"))[member]
        for x in range(cells_x):
            for array, ref in enumerate((pp, pf, pk)):
                value = ref[x]
                fill(array, x + cells_x * (1 - 2 * member), 0, value + value if array == 1 else value)
        fill(0, outside(near, REACH), 0, far[0])
        fill(2, outside(near, REACH), 0, far[1])
        for plan, ref in ((first_plan, received), (second_plan, rest)):
            for (array, distance), pieces in plan.items():
                for row, count, start in pieces:
                    value = ref[pl.ds(start, count), :]
                    for each in spans[array, distance]:
                        fill(array, outside(away, each), row, value)

        towards_partner = cells_x * (1 - 2 * member)
        for before, after, is_partner in ((below, above, False), (p_below, p_above, True)):
            for side, array, index, count, start in y_plan(cells_x)[0]:
                if side == "inside":
                    xs = (2 * index, 2 * index + 1) if array == 0 else (index,)
                    xs = [x + towards_partner * is_partner for x in xs]
                elif is_partner:
                    xs = [outside(near, cells_x + each) for each in spans[array, index]]
                else:
                    xs = [outside(away, each) for each in spans[array, index]]
                for x in xs:
                    fill(array, x, -count, before[pl.ds(start, count), :])
                    fill(array, x, cells_y, after[pl.ds(start, count), :])

    for_member(fill_member)

    def lanes(count):
        return lax.broadcasted_iota(jnp.int32, (count, depth), 1)

    def rows_of(first, count):
        return lax.broadcasted_iota(jnp.int32, (count, depth), 0) + (first - ORIGIN)

    lane = lanes(rows)

    def weigh(plane, _):
        centre = vk[plane, body, :]
        west = centre + vk[plane - 1, body, :]
        wx[plane, body, :] = west
        east = centre + vk[plane + 1, body, :]
        south = centre + vk[plane, pl.ds(top - 1, rows), :]
        north = centre + vk[plane, pl.ds(top + 1, rows), :]
        wy[plane, body, :] = south
        wy[plane, pl.ds(top + rows, 1), :] = north[rows - 1:, :]
        down = jnp.where(lane > 0, pltpu.roll(centre, 1, 1), 0.0)
        up = jnp.where(lane < depth - 1, pltpu.roll(centre, depth - 1, 1), 0.0)
        total = west + east + south + north + (centre + down) + (centre + up)
        zl[plane, body, :] = jnp.where(lane > 0, centre + down, 0.0)
        zh[plane, body, :] = jnp.where(lane < depth - 1, centre + up, 0.0)
        dg[plane, body, :] = total
        inside = centre > 0.0
        inv[plane, body, :] = jnp.where(inside, 1.0 / jnp.where(inside, total, 1.0), 0.0)
        return 0

    lax.fori_loop(1, planes - 1, weigh, 0, unroll=True)
    wx[planes - 1, body, :] = vk[planes - 1, body, :] + vk[planes - 2, body, :]

    def stencil(v, plane, first, count):
        here = pl.ds(first, count)
        centre = v[plane, here, :]
        total = wx[plane, here, :] * v[plane - 1, here, :] + wx[plane + 1, here, :] * v[plane + 1, here, :]
        total += wy[plane, here, :] * v[plane, pl.ds(first - 1, count), :]
        total += wy[plane, pl.ds(first + 1, count), :] * v[plane, pl.ds(first + 1, count), :]
        total += zl[plane, here, :] * pltpu.roll(centre, 1, 1)
        total += zh[plane, here, :] * pltpu.roll(centre, depth - 1, 1)
        return total

    def relax(source_ref, target, reach):
        def one(plane, _):
            total = stencil(source_ref, plane, top, rows)
            target[plane, body, :] = inv[plane, body, :] * (vf[plane, body, :] + total)
            return 0

        lax.fori_loop(REACH - reach, REACH + cells_x + reach, one, 0, unroll=True)

    relax(vp, va, REACH - 1)
    relax(va, vb, REACH - 2)
    relax(vb, va, REACH - 3)
    relax(va, vb, REACH - 4)

    own_lane = lanes(cells_y)
    own_row = rows_of(ORIGIN, cells_y)
    for x in range(cells_x):
        even = ((own_row + own_lane + x) & 1) == 0
        out[x] = jnp.where(even, va[REACH + x, own_rows, :], vb[REACH + x, own_rows, :])

    planes_one = cells_x // 2
    first = ORIGIN - 4
    count = cells_y + 8
    lane = lanes(count)
    row = rows_of(first, count)

    def pair_lane(value, stride, lane):
        up = pltpu.roll(value, depth - stride, 1)
        down = pltpu.roll(value, stride, 1)
        return value + jnp.where((lane & stride) == 0, up, down)

    def pair_row(ref, index, first, count, stride, row):
        centre = ref[index, pl.ds(first, count), :]
        up = ref[index, pl.ds(first + stride, count), :]
        down = ref[index, pl.ds(first - stride, count), :]
        return centre + jnp.where((row & stride) == 0, up, down)

    def residual(plane_one, _):
        total = jnp.zeros((count, depth), jnp.float32)
        for half in range(2):
            plane = 2 * plane_one + REACH - 4 + half
            here = pl.ds(first, count)
            twice = vf[plane, here, :] - dg[plane, here, :] * va[plane, here, :] + stencil(vb, plane, first, count)
            even = ((row + lane + half) & 1) == 0
            total += jnp.where(even, twice, 0.0)
        t0[plane_one, pl.ds(first, count), :] = pair_lane(total, 1, lane)
        return 0

    lax.fori_loop(0, planes_one + 4, residual, 0, unroll=True)
    for x in range(planes_one + 4):
        f1[x, pl.ds(first, count), :] = 0.5 * pair_row(t0, x, first, count, 1, row)

    first_k = ORIGIN - 6
    count_k = cells_y + 16
    lane_k = lanes(count_k)
    row_k = rows_of(first_k, count_k)
    for x in range(planes_one + 6):
        plane = 2 * x + REACH - 6
        here = pl.ds(first_k, count_k)
        t1[x, here, :] = pair_lane(vk[plane, here, :] + vk[plane + 1, here, :], 1, lane_k)
    for x in range(planes_one + 6):
        k1[x, pl.ds(first_k, count_k), :] = 0.125 * pair_row(t1, x, first_k, count_k, 1, row_k)

    def down2(value, lane):
        return jnp.where(lane >= 2, pltpu.roll(value, 2, 1), 0.0)

    def up2(value, lane):
        return jnp.where(lane < depth - 2, pltpu.roll(value, depth - 2, 1), 0.0)

    here = pl.ds(first, count)
    for x in range(planes_one + 4):
        centre = k1[x + 1, here, :]
        total = 6.0 * centre + (k1[x, here, :] + k1[x + 2, here, :])
        total += k1[x + 1, pl.ds(first - 2, count), :] + k1[x + 1, pl.ds(first + 2, count), :]
        total += down2(centre, lane) + up2(centre, lane)
        inside = centre > 0.0
        inverse = jnp.where(inside, 1.0 / jnp.where(inside, total, 1.0), 0.0)
        inv1[x, here, :] = inverse
        g1[x, here, :] = inverse * f1[x, here, :]

    def stencil_one(v, x, v_x, first, count, lane):
        here = pl.ds(first, count)
        south = pl.ds(first - 2, count)
        north = pl.ds(first + 2, count)
        kc = k1[x, here, :]
        vc = v[v_x, here, :]
        total = (kc + k1[x - 1, here, :]) * v[v_x - 1, here, :] + (kc + k1[x + 1, here, :]) * v[v_x + 1, here, :]
        total += (kc + k1[x, south, :]) * v[v_x, south, :] + (kc + k1[x, north, :]) * v[v_x, north, :]
        total += (kc + down2(kc, lane)) * down2(vc, lane) + (kc + up2(kc, lane)) * up2(vc, lane)
        return total

    first_h = ORIGIN - 2
    count_h = cells_y + 8
    lane_h = lanes(count_h)
    row_h = rows_of(first_h, count_h)
    for x in range(planes_one + 2):
        here = pl.ds(first_h, count_h)
        total = stencil_one(g1, x + 2, x + 1, first_h, count_h, lane_h)
        odd = inv1[x + 1, here, :] * (f1[x + 1, here, :] + total)
        h1[x, here, :] = odd
        even_cell = ((x - 1 + (row_h >> 1) + (lane_h >> 1)) & 1) == 0
        error_one[x, pl.ds(first_h - 8, count_h), :] = jnp.where(even_cell, g1[x + 1, here, :], odd)

    own2 = own_lane
    row2 = own_row
    for x in range(planes_one // 2):
        sum_r = jnp.zeros((cells_y, depth), jnp.float32)
        for half in range(2):
            x1 = 2 * x + half
            total = stencil_one(h1, x1 + 3, x1 + 1, ORIGIN, cells_y, own2)
            even_cell = ((x1 + (row2 >> 1) + (own2 >> 1)) & 1) == 0
            sum_r += jnp.where(even_cell, total, 0.0)
        sum_k = k1[2 * x + 3, own_rows, :] + k1[2 * x + 4, own_rows, :]
        t0[x, own_rows, :] = pair_lane(sum_r, 2, own2)
        t1[x, own_rows, :] = pair_lane(sum_k, 2, own2)
    lane8 = lanes(cells_y // 4)
    tile = jnp.zeros((cells_y // 4, depth), jnp.float32)
    for x in range(planes_one // 2):
        q2[0] = (1.0 / 64.0) * pair_row(t0, x, ORIGIN, cells_y, 2, row2)
        q2[1] = 0.125 * pair_row(t1, x, ORIGIN, cells_y, 2, row2)
        for field in range(2):
            kept = q2[field, pl.ds(0, cells_y // 4, stride=4), :]
            tile = jnp.where((lane8 & 3) == 2 * field + x, kept, tile)
    tiles[...] = jnp.broadcast_to(tile[None], tiles.shape)


def smooth(copies, block, halo):
    cells_x, cells_y, depth = halo[0].shape
    planes = cells_x + 2 * REACH
    tall = cells_y + 2 * ORIGIN
    planes_one = cells_x // 2
    window = pltpu.VMEM((planes, tall, depth), jnp.float32)

    def level_one(count):
        return pltpu.VMEM((count, tall, depth), jnp.float32)

    return pl.pallas_call(
        smooth_kernel,
        out_shape=(
            jax.ShapeDtypeStruct((cells_x, cells_y, depth), jnp.float32),
            jax.ShapeDtypeStruct((planes_one + 2, cells_y + 16, depth), jnp.float32),
            jax.ShapeDtypeStruct((copies, cells_y // 4, depth), jnp.float32),
        ),
        scratch_shapes=[window] * 11
        + [
            level_one(planes_one + 4),
            level_one(planes_one + 6),
            level_one(planes_one + 4),
            level_one(planes_one + 6),
            level_one(planes_one + 4),
            level_one(planes_one + 4),
            level_one(planes_one + 2),
            pltpu.VMEM((2, cells_y, depth), jnp.float32),
        ],
        compiler_params=pltpu.CompilerParams(vmem_limit_bytes=VMEM_LIMIT),
        name="smooth",
    )(block, *halo)


def ring(value, shift, axis):
    return pltpu.roll(value, shift % value.shape[axis], axis)


def before_x(v):
    return jnp.concatenate([jnp.zeros_like(v[:1]), v[:-1]], 0)


def after_x(v):
    return jnp.concatenate([v[1:], jnp.zeros_like(v[:1])], 0)


class Places:
    def __init__(self, shape):
        self.row = lax.broadcasted_iota(jnp.int32, shape, 1)
        self.lane = lax.broadcasted_iota(jnp.int32, shape, 2)
        self.part = self.lane & 3
        self.depth = shape[2]

    def before_y(self, v, stride):
        turned = ring(v, stride, 1)
        return jnp.where(self.row >= stride, turned, ring(turned, 1, 2))

    def after_y(self, v, stride):
        turned = ring(v, -stride, 1)
        return jnp.where(self.row < 8 - stride, turned, ring(turned, -1, 2))

    def has_before_y(self, stride):
        return (self.row >= stride) | (self.part > 0)

    def has_after_y(self, stride):
        return (self.row < 8 - stride) | (self.part < 3)

    def has_before_z(self, stride):
        return self.lane >= 4 * stride

    def has_after_z(self, stride):
        return self.lane < self.depth - 4 * stride


def whole_weights(k, places, stride):
    west = k + before_x(k)
    east = k + after_x(k)
    masks = (
        places.has_before_y(stride),
        places.has_after_y(stride),
        places.has_before_z(stride),
        places.has_after_z(stride),
    )
    near = (
        places.before_y(k, stride),
        places.after_y(k, stride),
        ring(k, 4 * stride, 2),
        ring(k, -4 * stride, 2),
    )
    diagonal = west + east
    weights = [west, east]
    for mask, value in zip(masks, near):
        diagonal += k + jnp.where(mask, value, 0.0)
        weights.append(jnp.where(mask, k + value, 0.0))
    return weights, diagonal


def whole_sum(v, weights, places, stride):
    total = weights[0] * before_x(v) + weights[1] * after_x(v)
    total += weights[2] * places.before_y(v, stride) + weights[3] * places.after_y(v, stride)
    total += weights[4] * ring(v, 4 * stride, 2) + weights[5] * ring(v, -4 * stride, 2)
    return total


def whole_solve(k2, rhs2):
    planes = k2.shape[0]
    places = Places(k2.shape)
    weights, diagonal = whole_weights(k2, places, 1)
    parity = lax.broadcasted_iota(jnp.int32, k2.shape, 0) + places.row + (places.lane >> 2)
    even = (parity & 1) == 0
    inverse = 1.0 / diagonal
    scaled = 32.0 * rhs2
    even_values = inverse * scaled
    odd_values = inverse * (scaled + whole_sum(even_values, weights, places, 1))
    error_two = jnp.where(even, even_values, odd_values)
    left = jnp.where(even, whole_sum(odd_values, weights, places, 1), 0.0)

    half = places.row[: planes // 2] , places.lane[: planes // 2]
    first_row = (half[0] & 1) == 0
    first_lane = (half[1] & 4) == 0

    def coarse(v):
        v = v.reshape(planes // 2, 2, *v.shape[1:])
        v = v[:, 0] + v[:, 1]
        v = v + jnp.where(first_row, ring(v, -1, 1), ring(v, 1, 1))
        return v + jnp.where(first_lane, ring(v, -4, 2), ring(v, 4, 2))

    remain = (1.0 / 256.0) * coarse(left)
    k3 = 0.125 * coarse(k2)
    places3 = Places(k3.shape)
    weights3, diagonal3 = whole_weights(k3, places3, 2)

    def total(v):
        return jnp.sum(jnp.sum(v, axis=0, keepdims=True), axis=(1, 2), keepdims=True)

    def around(v):
        return (
            places3.before_y(v, 2), places3.after_y(v, 2), ring(v, 8, 2), ring(v, -8, 2),
        )

    def apply(v, sides):
        coupled = weights3[0] * before_x(v) + weights3[1] * after_x(v)
        coupled += weights3[2] * sides[0] + weights3[3] * sides[1]
        coupled += weights3[4] * sides[2] + weights3[5] * sides[3]
        return (diagonal3 * v - coupled) * (1.0 / 128.0)

    remain_sides = around(remain)
    direction, sides = remain, remain_sides
    image = apply(remain, remain_sides)
    image_sides = around(image)
    norm_now = total(remain * remain)
    error = error_before = error_after = jnp.zeros_like(remain)
    for repeat in range(CSWEEPS):
        alpha = norm_now / total(direction * image)
        error = error + alpha * direction
        error_before = error_before + alpha * sides[0]
        error_after = error_after + alpha * sides[1]
        if repeat == CSWEEPS - 1:
            break
        remain = remain - alpha * image
        remain_sides = [r - alpha * q for r, q in zip(remain_sides, image_sides)]
        applied = apply(remain, remain_sides)
        applied_sides = around(applied)
        norm_next = total(remain * remain)
        beta = norm_next / norm_now
        direction = remain + beta * direction
        sides = [r + beta * p for r, p in zip(remain_sides, sides)]
        image = applied + beta * image
        image_sides = [w + beta * q for w, q in zip(applied_sides, image_sides)]
        norm_now = norm_next

    near = jnp.where(
        first_row,
        jnp.where(places3.has_before_y(2), error_before, 0.0),
        jnp.where(places3.has_after_y(2), error_after, 0.0),
    )
    error = 0.75 * error + 0.25 * near
    lower = 0.75 * error + 0.25 * before_x(error)
    upper = 0.75 * error + 0.25 * after_x(error)
    fine = jnp.stack([lower, upper], 1).reshape(k2.shape)
    near = jnp.where(
        (places.lane & 4) == 0,
        jnp.where(places.has_before_z(1), ring(fine, 4, 2), 0.0),
        jnp.where(places.has_after_z(1), ring(fine, -4, 2), 0.0),
    )
    return error_two + (0.75 * fine + 0.25 * near)


def finish(grid, wide, smoothed, error_one, out, e1, e0):
    cells_x, cells_y, depth = smoothed.shape
    i, j = lax.axis_index("gx"), lax.axis_index("gy")
    first = 8 - 2
    count = cells_y + 8
    lane = lax.broadcasted_iota(jnp.int32, (count, depth), 1)
    row = lax.broadcasted_iota(jnp.int32, (count, depth), 0) - 2

    def widen_z(value, stride, lane):
        down = jnp.where(lane >= stride, pltpu.roll(value, stride, 1), 0.0)
        up = jnp.where(lane < depth - stride, pltpu.roll(value, depth - stride, 1), 0.0)
        return 0.75 * value + 0.25 * jnp.where((lane & stride) == 0, down, up)

    def widen_y(ref, index, first, count, stride, row):
        centre = ref[index, pl.ds(first, count), :]
        down = ref[index, pl.ds(first - stride, count), :]
        up = ref[index, pl.ds(first + stride, count), :]
        return 0.75 * centre + 0.25 * jnp.where((row & stride) == 0, down, up)

    low_row = jnp.where(j > 0, -cells_y, 0)
    high_row = jnp.where(j < grid[1] - 1, 2 * cells_y, cells_y)
    inside = (row >= low_row) & (row < high_row)
    planes_two = cells_x // 4 + 2
    mid = [widen_z(widen_y(wide, x, first, count, 2, row), 2, lane) for x in range(planes_two)]
    for x in range(cells_x // 2 + 2):
        centre = (x + 1) // 2
        near = centre + (1 if x % 2 == 0 else -1)
        value = jnp.where(inside, 0.75 * mid[centre] + 0.25 * mid[near], 0.0)
        if x == 0:
            value = jnp.where(i > 0, value, 0.0)
        if x == cells_x // 2 + 1:
            value = jnp.where(i < grid[0] - 1, value, 0.0)
        here = pl.ds(first, count)
        e1[x, here, :] = error_one[x, here, :] + value

    lane = lax.broadcasted_iota(jnp.int32, (cells_y, depth), 1)
    row = lax.broadcasted_iota(jnp.int32, (cells_y, depth), 0)
    for x in range(cells_x // 2 + 2):
        e0[x] = widen_z(widen_y(e1, x, 8, cells_y, 1, row), 1, lane)
    for x in range(cells_x):
        centre = x // 2 + 1
        near = centre + (-1 if x % 2 == 0 else 1)
        out[x] = smoothed[x] + (0.75 * e0[centre] + 0.25 * e0[near])


def correct_kernel(grid, gathered, smoothed, error_one, out, whole, strip, wide, e1, e0):
    cells_y = smoothed.shape[1]
    nx, ny = grid
    i, j = lax.axis_index("gx"), lax.axis_index("gy")
    lane = lax.broadcasted_iota(jnp.int32, (8, 128), 1) & 3
    fields = [[], []]
    for column in range(nx):
        parts = [gathered[column * ny + part] for part in range(ny)]
        for field in range(2):
            for x in range(2):
                place = 2 * field + x
                plane = None
                for part in range(ny):
                    turned = parts[part] if part == place else ring(parts[part], part - place, 1)
                    plane = turned if plane is None else jnp.where(lane == part, turned, plane)
                fields[field].append(plane)
    rhs2 = jnp.stack(fields[0], 0)
    k2 = jnp.stack(fields[1], 0)
    planes = 2 * nx
    whole[0] = jnp.zeros((8, 128), jnp.float32)
    whole[planes + 1] = jnp.zeros((8, 128), jnp.float32)
    whole[pl.ds(1, planes)] = whole_solve(k2, rhs2)

    masks = [[(j + side - lane) == shift for shift in range(-4, 5)] for side in (-1, 0, 1)]
    inside = (j > 0, True, j < ny - 1)
    for x in range(4):
        plane = whole[2 * i + x]
        turned = [plane if shift == 0 else ring(plane, -shift, 1) for shift in range(-4, 5)]
        for index in range(3):
            value = jnp.zeros_like(plane)
            for mask, each in zip(masks[index], turned):
                value = jnp.where(mask, each, value)
            strip[x, pl.ds(8 * index, 8), :] = value if index == 1 else jnp.where(inside[index], value, 0.0)
        for place in range(4):
            wide[x, pl.ds(4 + place, 8, stride=4), :] = strip[x, pl.ds(7, 8), :]
            wide[x, pl.ds(36 + place, 2, stride=4), :] = strip[x, pl.ds(15, 2), :]
    finish(grid, wide, smoothed, error_one, out, e1, e0)


def finish_kernel(grid, wide, smoothed, error_one, out, e1, e0):
    finish(grid, wide, smoothed, error_one, out, e1, e0)


def last_scratch(cells_x, cells_y, depth):
    count = cells_x // 2 + 2
    return [
        pltpu.VMEM((count, cells_y + 16, depth), jnp.float32),
        pltpu.VMEM((count, cells_y, depth), jnp.float32),
    ]


def correct_whole(grid, tiles, smoothed, error_one):
    gathered = lax.all_to_all(tiles, ("gx", "gy"), 0, 0, tiled=False)
    cells_x, cells_y, depth = smoothed.shape
    return pl.pallas_call(
        functools.partial(correct_kernel, grid),
        out_shape=jax.ShapeDtypeStruct(smoothed.shape, jnp.float32),
        scratch_shapes=[
            pltpu.VMEM((2 * grid[0] + 2, 8, depth), jnp.float32),
            pltpu.VMEM((4, 24, depth), jnp.float32),
            pltpu.VMEM((4, cells_y + 16, depth), jnp.float32),
        ]
        + last_scratch(cells_x, cells_y, depth),
        compiler_params=pltpu.CompilerParams(vmem_limit_bytes=VMEM_LIMIT),
        name="correct",
    )(gathered, smoothed, error_one)


def with_faces(shard):
    for axis, dim in (("gx", 0), ("gy", 1)):
        length = shard.shape[dim]
        last = lax.slice_in_dim(shard, length - 1, length, axis=dim)
        initial = lax.slice_in_dim(shard, 0, 1, axis=dim)
        before = lax.ppermute(last, axis, shifts(axis, 1))
        after = lax.ppermute(initial, axis, shifts(axis, -1))
        shard = jnp.concatenate([before, shard, after], axis=dim)
    return shard


def with_zeros(field):
    return jnp.pad(field, ((1, 1), (1, 1), (0, 0)))


def pad_depth(field):
    return jnp.pad(field, ((0, 0), (0, 0), (1, 1)))


def restrict(field):
    size_x, size_y, size_z = field.shape
    return field.reshape(size_x // 2, 2, size_y // 2, 2, size_z // 2, 2).mean(axis=(1, 3, 5))


def level_weights(coef_pad):
    c = pad_depth(coef_pad)
    wx = (c[1:, 1:-1, 1:-1] + c[:-1, 1:-1, 1:-1]) * 0.5
    wy = (c[1:-1, 1:, 1:-1] + c[1:-1, :-1, 1:-1]) * 0.5
    wz = (c[1:-1, 1:-1, 1:] + c[1:-1, 1:-1, :-1]) * 0.5
    diagonal = wx[1:] + wx[:-1] + wy[:, 1:] + wy[:, :-1] + wz[:, :, 1:] + wz[:, :, :-1]
    return (wx, wy, wz), diagonal


def neighbour_sum(field_pad, weights):
    wx, wy, wz = weights
    v = pad_depth(field_pad)
    total = wx[:-1] * v[:-2, 1:-1, 1:-1] + wx[1:] * v[2:, 1:-1, 1:-1]
    total = total + wy[:, :-1] * v[1:-1, :-2, 1:-1] + wy[:, 1:] * v[1:-1, 2:, 1:-1]
    return total + wz[:, :, :-1] * v[1:-1, 1:-1, :-2] + wz[:, :, 1:] * v[1:-1, 1:-1, 2:]


def prolong_axis(padded, axis):
    length = padded.shape[axis]
    middle = lax.slice_in_dim(padded, 1, length - 1, axis=axis)
    before = lax.slice_in_dim(padded, 0, length - 2, axis=axis)
    after = lax.slice_in_dim(padded, 2, length, axis=axis)
    joined = jnp.stack([0.75 * middle + 0.25 * before, 0.75 * middle + 0.25 * after], axis=axis + 1)
    shape = list(middle.shape)
    shape[axis] = 2 * shape[axis]
    return joined.reshape(shape)


def coarse_solve(rhs, weights, diagonal):
    error = jnp.zeros_like(rhs)
    remain = rhs
    direction = rhs
    norm_now = jnp.sum(remain * remain)
    for _ in range(CSWEEPS):
        image = (diagonal * direction - neighbour_sum(with_zeros(direction), weights)) * 4.0**-3
        alpha = norm_now / jnp.sum(direction * image)
        error = error + alpha * direction
        remain = remain - alpha * image
        norm_next = jnp.sum(remain * remain)
        direction = remain + norm_next / norm_now * direction
        norm_now = norm_next
    return error


def correct_spread(grid, tiles, smoothed, error_one):
    cells_x, cells_y, depth = smoothed.shape
    shape2 = (cells_x // 4, cells_y // 4, depth // 4)
    own = tiles[0].reshape(shape2[1], shape2[2], 2, shape2[0]).transpose(2, 3, 0, 1)
    rhs2, k2 = own[0], own[1]
    weights, diagonal = level_weights(with_faces(k2))
    parity = sum(lax.broadcasted_iota(jnp.int32, shape2, d) for d in range(3)) % 2
    error_two = jnp.where(parity == 0, rhs2 * 16.0 / diagonal, 0.0)
    total = neighbour_sum(with_faces(error_two), weights)
    error_two = jnp.where(parity == 1, (rhs2 * 16.0 + total) / diagonal, error_two)
    total = neighbour_sum(with_faces(error_two), weights)
    rhs3 = restrict(rhs2 - (diagonal * error_two - total) * 4.0**-2)
    merged = jnp.stack([rhs3, restrict(k2)])
    merged = lax.all_gather(merged, "gx", axis=1, tiled=True)
    merged = lax.all_gather(merged, "gy", axis=2, tiled=True)
    weights3, diagonal3 = level_weights(with_zeros(merged[1]))
    error_three = coarse_solve(merged[0], weights3, diagonal3)
    start_x = lax.axis_index("gx") * rhs3.shape[0]
    start_y = lax.axis_index("gy") * rhs3.shape[1]
    window = lax.dynamic_slice(
        with_zeros(error_three),
        (start_x, start_y, jnp.int32(0)),
        (rhs3.shape[0] + 2, rhs3.shape[1] + 2, rhs3.shape[2]),
    )
    finer = pad_depth(window)
    for axis in range(3):
        finer = prolong_axis(finer, axis)
    wide = with_faces(error_two + finer)
    wide = jnp.repeat(jnp.repeat(wide, 4, axis=1), 4, axis=2)
    wide = jnp.pad(wide, ((0, 0), (4, 4), (0, 0)))
    return pl.pallas_call(
        functools.partial(finish_kernel, grid),
        out_shape=jax.ShapeDtypeStruct(smoothed.shape, jnp.float32),
        scratch_shapes=last_scratch(cells_x, cells_y, depth),
        compiler_params=pltpu.CompilerParams(vmem_limit_bytes=VMEM_LIMIT),
        name="finish",
    )(wide, smoothed, error_one)


def on_device(pressure, source, coefficient):
    grid = (lax.axis_size("gx"), lax.axis_size("gy"))
    _, cells_y, depth = pressure.shape
    fits = grid[1] == 4 and cells_y == 32 and depth == 128
    own = (pressure, source, coefficient)
    block = stacked(*own)
    halo = fine_halo(own, block)
    copies = grid[0] * grid[1] if fits else 1
    smoothed, error_one, tiles = smooth(copies, block, halo)
    correct = correct_whole if fits else correct_spread
    return correct(grid, tiles, smoothed, error_one)


def solution(mesh):
    spec = P("gx", "gy", None)
    return jax.shard_map(on_device, mesh=mesh, in_specs=(spec, spec, spec), out_specs=spec, check_vma=False)
```

```python
import functools
import jax
import jax.numpy as jnp
from jax import lax
from jax.experimental import pallas as pl
from jax.experimental.pallas import tpu as pltpu
from jax.sharding import PartitionSpec as P

CSWEEPS = 4
REACH = 9
ORIGIN = 16
VMEM_LIMIT = 48 * 1024 * 1024


def y_rows(distance, array):
    rows = REACH if distance <= 2 else REACH + 2 - distance
    return rows - 1 if array == 1 else rows


def side_entries():
    pairs = [(0, d, (d, d + 1)) for d in range(1, REACH - 1, 2)] + [(0, REACH, (REACH,))]
    return pairs + [(1, d, (d,)) for d in range(1, REACH)] + [(2, d, (d,)) for d in range(1, REACH + 1)]


def x_plan(cells_y):
    first, second = {}, {}
    lengths = [0, 0]

    def put(message, plan, key, row, rows):
        plan.setdefault(key, []).append((row, rows, lengths[message]))
        lengths[message] += rows

    for array, distance, _ in side_entries():
        key = (array, distance)
        ends = y_rows(distance, array)
        put(0, first, key, 0, ends)
        put(0, first, key, cells_y - ends, ends)
        put(1, second, key, ends, cells_y - 2 * ends)
    return first, second, [-(-length // 8) * 8 for length in lengths]


def y_plan(cells_x):
    pieces = []
    start = 0
    inside = [(0, m) for m in range(cells_x // 2)] + [(a, x) for a in (1, 2) for x in range(cells_x)]
    chosen = [("inside", array, index, y_rows(0, array)) for array, index in inside]
    chosen += [("away", array, distance, y_rows(distance, array)) for array, distance, _ in side_entries()]
    for side, array, index, rows in chosen:
        pieces.append((side, array, index, rows, start))
        start += rows
    return pieces, -(-start // 8) * 8


def shifts(axis, step):
    count = lax.axis_size(axis)
    return [(i, i + step) for i in range(count) if 0 <= i + step < count]


def swap_pairs():
    return [(i, i ^ 1) for i in range(lax.axis_size("gx"))]


def x_pairs():
    count = lax.axis_size("gx")
    pairs = [(i, i + 1) for i in range(1, count - 1, 2)]
    return pairs + [(j, i) for i, j in pairs]


def inside_rows(member, own, partner, array, index, first, rows):
    cells_x = own[0].shape[0]
    here = pl.ds(first, rows)

    def plane(x):
        if x // cells_x == member:
            return own[array][x % cells_x, here, :]
        value = partner[array][x % cells_x, here, :]
        return value + value if array == 1 else value

    if array != 0:
        return plane(index)
    depth = own[0].shape[2]
    row = lax.broadcasted_iota(jnp.int32, (rows, depth), 0) + first
    lane = lax.broadcasted_iota(jnp.int32, (rows, depth), 1)
    return jnp.where(((row + lane) & 1) == 1, plane(2 * index), plane(2 * index + 1))


def for_member(body):
    me = lax.axis_index("gx") & 1
    for member in range(2):
        pl.when(me == member)(functools.partial(body, member))


def split_kernel(block, pp, pf, pk, first, second):
    cells_x, cells_y, _ = pp.shape
    p, f, k = views(block, cells_x)
    plans = x_plan(cells_y)

    def body(member):
        for plan, target in zip(plans, (first, second)):
            for (array, distance), pieces in plan.items():
                plane = 2 * cells_x - distance if member == 1 else distance - 1
                index = plane // 2 if array == 0 else plane
                for row, rows, start in pieces:
                    value = inside_rows(member, (p, f, k), (pp, pf, pk), array, index, row, rows)
                    target[pl.ds(start, rows), :] = value

    for_member(body)


def pack_kernel(block, received, to_up, to_down):
    cells_x, cells_y = block.shape[0] // 3, block.shape[1]
    own = views(block, cells_x)
    plan = x_plan(cells_y)[0]

    def piece(side, array, index, rows, row):
        if side == "inside":
            return inside_rows(0, own, None, array, index, row, rows)
        place = [s + row - r for r, count, s in plan[array, index] if r <= row and row + rows <= r + count][0]
        return received[pl.ds(place, rows), :]

    for side, array, index, rows, start in y_plan(cells_x)[0]:
        to_up[pl.ds(start, rows), :] = piece(side, array, index, rows, cells_y - rows)
        to_down[pl.ds(start, rows), :] = piece(side, array, index, rows, 0)


def far_kernel(received, rest, far):
    plans = x_plan(far.shape[1])
    for place, array in ((0, 0), (1, 2)):
        for plan, ref in zip(plans, (received, rest)):
            for row, rows, start in plan[array, 1]:
                far[place, pl.ds(row, rows), :] = ref[pl.ds(start, rows), :]


def stacked(pressure, source, coefficient):
    block = jnp.concatenate([pressure, source, coefficient], 0)
    cells_x = pressure.shape[0]
    plane = lax.broadcasted_iota(jnp.int32, block.shape, 0)
    return block * jnp.where((plane >= cells_x) & (plane < 2 * cells_x), 2.0, 1.0)


def views(block, cells_x):
    return tuple(block.at[pl.ds(n * cells_x, cells_x)] for n in range(3))


def fine_halo(own, block):
    cells_x, cells_y, depth = own[0].shape
    params = pltpu.CompilerParams(vmem_limit_bytes=VMEM_LIMIT)

    def packed(length):
        return jax.ShapeDtypeStruct((length, depth), jnp.float32)

    partner = tuple(lax.ppermute(v, "gx", swap_pairs()) for v in own)
    lengths = x_plan(cells_y)[2]
    first, second = pl.pallas_call(
        split_kernel, out_shape=[packed(n) for n in lengths], compiler_params=params, name="split_block"
    )(block, *partner)
    received = lax.ppermute(first, "gx", x_pairs())
    length = y_plan(cells_x)[1]
    planes = jax.ShapeDtypeStruct((2, cells_y, depth), jnp.float32)
    to_up, to_down = pl.pallas_call(
        pack_kernel, out_shape=[packed(length), packed(length)], compiler_params=params, name="pack_halo"
    )(block, received)
    below = lax.ppermute(to_up, "gy", shifts("gy", 1))
    above = lax.ppermute(to_down, "gy", shifts("gy", -1))
    rest = lax.ppermute(second, "gx", x_pairs())
    outermost = pl.pallas_call(far_kernel, out_shape=planes, compiler_params=params, name="far_planes")(received, rest)
    far = lax.ppermute(outermost, "gx", swap_pairs())
    above, rest = lax.optimization_barrier((above, rest))
    below, far = lax.optimization_barrier((below, far))
    p_below = lax.ppermute(below, "gx", swap_pairs())
    p_above = lax.ppermute(above, "gx", swap_pairs())
    return *partner, received, rest, far, below, above, p_below, p_above


def smooth_kernel(
    block, pp, pf, pk, received, rest, far, below, above, p_below, p_above,
    out, error_one, tiles,
    vp, vf, vk, wx, wy, zl, zh, dg, inv, va, vb,
    t0, t1, f1, k1, inv1, g1, h1, q2,
):
    cells_x, cells_y, depth = pp.shape
    planes = cells_x + 2 * REACH
    own_rows = pl.ds(ORIGIN, cells_y)
    top = ORIGIN - REACH + 1
    rows = cells_y + 2 * (REACH - 1)
    body = pl.ds(top, rows)

    windows = (vp, vf, vk)
    first_plan, second_plan, _ = x_plan(cells_y)

    def fill(array, x, first, value):
        if x < -REACH or x >= cells_x + REACH or (array == 1 and (x == -REACH or x == cells_x + REACH - 1)):
            return
        windows[array][REACH + x, pl.ds(ORIGIN + first, value.shape[0]), :] = value

    for x in range(cells_x):
        for array, ref in enumerate(views(block, cells_x)):
            fill(array, x, 0, ref[x])

    spans = {(array, distance): distances for array, distance, distances in side_entries()}

    def outside(side, distance):
        return -distance if side == "low" else cells_x - 1 + distance

    def fill_member(member):
        away, near = (("low", "high"), ("high", "low"))[member]
        for x in range(cells_x):
            for array, ref in enumerate((pp, pf, pk)):
                value = ref[x]
                fill(array, x + cells_x * (1 - 2 * member), 0, value + value if array == 1 else value)
        fill(0, outside(near, REACH), 0, far[0])
        fill(2, outside(near, REACH), 0, far[1])
        for plan, ref in ((first_plan, received), (second_plan, rest)):
            for (array, distance), pieces in plan.items():
                for row, count, start in pieces:
                    value = ref[pl.ds(start, count), :]
                    for each in spans[array, distance]:
                        fill(array, outside(away, each), row, value)

        towards_partner = cells_x * (1 - 2 * member)
        for before, after, is_partner in ((below, above, False), (p_below, p_above, True)):
            for side, array, index, count, start in y_plan(cells_x)[0]:
                if side == "inside":
                    xs = (2 * index, 2 * index + 1) if array == 0 else (index,)
                    xs = [x + towards_partner * is_partner for x in xs]
                elif is_partner:
                    xs = [outside(near, cells_x + each) for each in spans[array, index]]
                else:
                    xs = [outside(away, each) for each in spans[array, index]]
                for x in xs:
                    fill(array, x, -count, before[pl.ds(start, count), :])
                    fill(array, x, cells_y, after[pl.ds(start, count), :])

    for_member(fill_member)

    def lanes(count):
        return lax.broadcasted_iota(jnp.int32, (count, depth), 1)

    def rows_of(first, count):
        return lax.broadcasted_iota(jnp.int32, (count, depth), 0) + (first - ORIGIN)

    lane = lanes(rows)

    def weigh(plane, _):
        centre = vk[plane, body, :]
        west = centre + vk[plane - 1, body, :]
        wx[plane, body, :] = west
        east = centre + vk[plane + 1, body, :]
        south = centre + vk[plane, pl.ds(top - 1, rows), :]
        north = centre + vk[plane, pl.ds(top + 1, rows), :]
        wy[plane, body, :] = south
        wy[plane, pl.ds(top + rows, 1), :] = north[rows - 1:, :]
        down = jnp.where(lane > 0, pltpu.roll(centre, 1, 1), 0.0)
        up = jnp.where(lane < depth - 1, pltpu.roll(centre, depth - 1, 1), 0.0)
        total = west + east + south + north + (centre + down) + (centre + up)
        zl[plane, body, :] = jnp.where(lane > 0, centre + down, 0.0)
        zh[plane, body, :] = jnp.where(lane < depth - 1, centre + up, 0.0)
        dg[plane, body, :] = total
        inside = centre > 0.0
        inv[plane, body, :] = jnp.where(inside, 1.0 / jnp.where(inside, total, 1.0), 0.0)
        return 0

    lax.fori_loop(1, planes - 1, weigh, 0, unroll=True)
    wx[planes - 1, body, :] = vk[planes - 1, body, :] + vk[planes - 2, body, :]

    def stencil(v, plane, first, count):
        here = pl.ds(first, count)
        centre = v[plane, here, :]
        total = wx[plane, here, :] * v[plane - 1, here, :] + wx[plane + 1, here, :] * v[plane + 1, here, :]
        total += wy[plane, here, :] * v[plane, pl.ds(first - 1, count), :]
        total += wy[plane, pl.ds(first + 1, count), :] * v[plane, pl.ds(first + 1, count), :]
        total += zl[plane, here, :] * pltpu.roll(centre, 1, 1)
        total += zh[plane, here, :] * pltpu.roll(centre, depth - 1, 1)
        return total

    def relax(source_ref, target, reach):
        def one(plane, _):
            total = stencil(source_ref, plane, top, rows)
            target[plane, body, :] = inv[plane, body, :] * (vf[plane, body, :] + total)
            return 0

        lax.fori_loop(REACH - reach, REACH + cells_x + reach, one, 0, unroll=True)

    relax(vp, va, REACH - 1)
    relax(va, vb, REACH - 2)
    relax(vb, va, REACH - 3)
    relax(va, vb, REACH - 4)

    own_lane = lanes(cells_y)
    own_row = rows_of(ORIGIN, cells_y)
    for x in range(cells_x):
        even = ((own_row + own_lane + x) & 1) == 0
        out[x] = jnp.where(even, va[REACH + x, own_rows, :], vb[REACH + x, own_rows, :])

    planes_one = cells_x // 2
    first = ORIGIN - 4
    count = cells_y + 8
    lane = lanes(count)
    row = rows_of(first, count)

    def pair_lane(value, stride, lane):
        up = pltpu.roll(value, depth - stride, 1)
        down = pltpu.roll(value, stride, 1)
        return value + jnp.where((lane & stride) == 0, up, down)

    def pair_row(ref, index, first, count, stride, row):
        centre = ref[index, pl.ds(first, count), :]
        up = ref[index, pl.ds(first + stride, count), :]
        down = ref[index, pl.ds(first - stride, count), :]
        return centre + jnp.where((row & stride) == 0, up, down)

    def residual(plane_one, _):
        total = jnp.zeros((count, depth), jnp.float32)
        for half in range(2):
            plane = 2 * plane_one + REACH - 4 + half
            here = pl.ds(first, count)
            twice = vf[plane, here, :] - dg[plane, here, :] * va[plane, here, :] + stencil(vb, plane, first, count)
            even = ((row + lane + half) & 1) == 0
            total += jnp.where(even, twice, 0.0)
        t0[plane_one, pl.ds(first, count), :] = pair_lane(total, 1, lane)
        return 0

    lax.fori_loop(0, planes_one + 4, residual, 0, unroll=True)
    for x in range(planes_one + 4):
        f1[x, pl.ds(first, count), :] = 0.5 * pair_row(t0, x, first, count, 1, row)

    first_k = ORIGIN - 6
    count_k = cells_y + 16
    lane_k = lanes(count_k)
    row_k = rows_of(first_k, count_k)
    for x in range(planes_one + 6):
        plane = 2 * x + REACH - 6
        here = pl.ds(first_k, count_k)
        t1[x, here, :] = pair_lane(vk[plane, here, :] + vk[plane + 1, here, :], 1, lane_k)
    for x in range(planes_one + 6):
        k1[x, pl.ds(first_k, count_k), :] = 0.125 * pair_row(t1, x, first_k, count_k, 1, row_k)

    def down2(value, lane):
        return jnp.where(lane >= 2, pltpu.roll(value, 2, 1), 0.0)

    def up2(value, lane):
        return jnp.where(lane < depth - 2, pltpu.roll(value, depth - 2, 1), 0.0)

    here = pl.ds(first, count)
    for x in range(planes_one + 4):
        centre = k1[x + 1, here, :]
        total = 6.0 * centre + (k1[x, here, :] + k1[x + 2, here, :])
        total += k1[x + 1, pl.ds(first - 2, count), :] + k1[x + 1, pl.ds(first + 2, count), :]
        total += down2(centre, lane) + up2(centre, lane)
        inside = centre > 0.0
        inverse = jnp.where(inside, 1.0 / jnp.where(inside, total, 1.0), 0.0)
        inv1[x, here, :] = inverse
        g1[x, here, :] = inverse * f1[x, here, :]

    def stencil_one(v, x, v_x, first, count, lane):
        here = pl.ds(first, count)
        south = pl.ds(first - 2, count)
        north = pl.ds(first + 2, count)
        kc = k1[x, here, :]
        vc = v[v_x, here, :]
        total = (kc + k1[x - 1, here, :]) * v[v_x - 1, here, :] + (kc + k1[x + 1, here, :]) * v[v_x + 1, here, :]
        total += (kc + k1[x, south, :]) * v[v_x, south, :] + (kc + k1[x, north, :]) * v[v_x, north, :]
        total += (kc + down2(kc, lane)) * down2(vc, lane) + (kc + up2(kc, lane)) * up2(vc, lane)
        return total

    first_h = ORIGIN - 2
    count_h = cells_y + 8
    lane_h = lanes(count_h)
    row_h = rows_of(first_h, count_h)
    for x in range(planes_one + 2):
        here = pl.ds(first_h, count_h)
        total = stencil_one(g1, x + 2, x + 1, first_h, count_h, lane_h)
        odd = inv1[x + 1, here, :] * (f1[x + 1, here, :] + total)
        h1[x, here, :] = odd
        even_cell = ((x - 1 + (row_h >> 1) + (lane_h >> 1)) & 1) == 0
        error_one[x, pl.ds(first_h - 8, count_h), :] = jnp.where(even_cell, g1[x + 1, here, :], odd)

    own2 = own_lane
    row2 = own_row
    for x in range(planes_one // 2):
        sum_r = jnp.zeros((cells_y, depth), jnp.float32)
        for half in range(2):
            x1 = 2 * x + half
            total = stencil_one(h1, x1 + 3, x1 + 1, ORIGIN, cells_y, own2)
            even_cell = ((x1 + (row2 >> 1) + (own2 >> 1)) & 1) == 0
            sum_r += jnp.where(even_cell, total, 0.0)
        sum_k = k1[2 * x + 3, own_rows, :] + k1[2 * x + 4, own_rows, :]
        t0[x, own_rows, :] = pair_lane(sum_r, 2, own2)
        t1[x, own_rows, :] = pair_lane(sum_k, 2, own2)
    lane8 = lanes(cells_y // 4)
    tile = jnp.zeros((cells_y // 4, depth), jnp.float32)
    for x in range(planes_one // 2):
        q2[0] = (1.0 / 64.0) * pair_row(t0, x, ORIGIN, cells_y, 2, row2)
        q2[1] = 0.125 * pair_row(t1, x, ORIGIN, cells_y, 2, row2)
        for field in range(2):
            kept = q2[field, pl.ds(0, cells_y // 4, stride=4), :]
            tile = jnp.where((lane8 & 3) == 2 * field + x, kept, tile)
    tiles[...] = jnp.broadcast_to(tile[None], tiles.shape)


def smooth(copies, block, halo):
    cells_x, cells_y, depth = halo[0].shape
    planes = cells_x + 2 * REACH
    tall = cells_y + 2 * ORIGIN
    planes_one = cells_x // 2
    window = pltpu.VMEM((planes, tall, depth), jnp.float32)

    def level_one(count):
        return pltpu.VMEM((count, tall, depth), jnp.float32)

    return pl.pallas_call(
        smooth_kernel,
        out_shape=(
            jax.ShapeDtypeStruct((cells_x, cells_y, depth), jnp.float32),
            jax.ShapeDtypeStruct((planes_one + 2, cells_y + 16, depth), jnp.float32),
            jax.ShapeDtypeStruct((copies, cells_y // 4, depth), jnp.float32),
        ),
        scratch_shapes=[window] * 11
        + [
            level_one(planes_one + 4),
            level_one(planes_one + 6),
            level_one(planes_one + 4),
            level_one(planes_one + 6),
            level_one(planes_one + 4),
            level_one(planes_one + 4),
            level_one(planes_one + 2),
            pltpu.VMEM((2, cells_y, depth), jnp.float32),
        ],
        compiler_params=pltpu.CompilerParams(vmem_limit_bytes=VMEM_LIMIT),
        name="smooth",
    )(block, *halo)


def ring(value, shift, axis):
    return pltpu.roll(value, shift % value.shape[axis], axis)


def before_x(v):
    return jnp.concatenate([jnp.zeros_like(v[:1]), v[:-1]], 0)


def after_x(v):
    return jnp.concatenate([v[1:], jnp.zeros_like(v[:1])], 0)


class Places:
    def __init__(self, shape):
        self.row = lax.broadcasted_iota(jnp.int32, shape, 1)
        self.lane = lax.broadcasted_iota(jnp.int32, shape, 2)
        self.part = self.lane & 3
        self.depth = shape[2]

    def before_y(self, v, stride):
        turned = ring(v, stride, 1)
        return jnp.where(self.row >= stride, turned, ring(turned, 1, 2))

    def after_y(self, v, stride):
        turned = ring(v, -stride, 1)
        return jnp.where(self.row < 8 - stride, turned, ring(turned, -1, 2))

    def has_before_y(self, stride):
        return (self.row >= stride) | (self.part > 0)

    def has_after_y(self, stride):
        return (self.row < 8 - stride) | (self.part < 3)

    def has_before_z(self, stride):
        return self.lane >= 4 * stride

    def has_after_z(self, stride):
        return self.lane < self.depth - 4 * stride


def whole_weights(k, places, stride):
    west = k + before_x(k)
    east = k + after_x(k)
    masks = (
        places.has_before_y(stride),
        places.has_after_y(stride),
        places.has_before_z(stride),
        places.has_after_z(stride),
    )
    near = (
        places.before_y(k, stride),
        places.after_y(k, stride),
        ring(k, 4 * stride, 2),
        ring(k, -4 * stride, 2),
    )
    diagonal = west + east
    weights = [west, east]
    for mask, value in zip(masks, near):
        diagonal += k + jnp.where(mask, value, 0.0)
        weights.append(jnp.where(mask, k + value, 0.0))
    return weights, diagonal


def whole_sum(v, weights, places, stride):
    total = weights[0] * before_x(v) + weights[1] * after_x(v)
    total += weights[2] * places.before_y(v, stride) + weights[3] * places.after_y(v, stride)
    total += weights[4] * ring(v, 4 * stride, 2) + weights[5] * ring(v, -4 * stride, 2)
    return total


def whole_solve(k2, rhs2):
    planes = k2.shape[0]
    places = Places(k2.shape)
    weights, diagonal = whole_weights(k2, places, 1)
    parity = lax.broadcasted_iota(jnp.int32, k2.shape, 0) + places.row + (places.lane >> 2)
    even = (parity & 1) == 0
    inverse = 1.0 / diagonal
    scaled = 32.0 * rhs2
    even_values = inverse * scaled
    odd_values = inverse * (scaled + whole_sum(even_values, weights, places, 1))
    error_two = jnp.where(even, even_values, odd_values)
    left = jnp.where(even, whole_sum(odd_values, weights, places, 1), 0.0)

    half = places.row[: planes // 2] , places.lane[: planes // 2]
    first_row = (half[0] & 1) == 0
    first_lane = (half[1] & 4) == 0

    def coarse(v):
        v = v.reshape(planes // 2, 2, *v.shape[1:])
        v = v[:, 0] + v[:, 1]
        v = v + jnp.where(first_row, ring(v, -1, 1), ring(v, 1, 1))
        return v + jnp.where(first_lane, ring(v, -4, 2), ring(v, 4, 2))

    remain = (1.0 / 256.0) * coarse(left)
    k3 = 0.125 * coarse(k2)
    places3 = Places(k3.shape)
    weights3, diagonal3 = whole_weights(k3, places3, 2)

    def total(v):
        return jnp.sum(jnp.sum(v, axis=0, keepdims=True), axis=(1, 2), keepdims=True)

    def around(v):
        return (
            places3.before_y(v, 2), places3.after_y(v, 2), ring(v, 8, 2), ring(v, -8, 2),
        )

    def apply(v, sides):
        coupled = weights3[0] * before_x(v) + weights3[1] * after_x(v)
        coupled += weights3[2] * sides[0] + weights3[3] * sides[1]
        coupled += weights3[4] * sides[2] + weights3[5] * sides[3]
        return (diagonal3 * v - coupled) * (1.0 / 128.0)

    remain_sides = around(remain)
    direction, sides = remain, remain_sides
    image = apply(remain, remain_sides)
    image_sides = around(image)
    norm_now = total(remain * remain)
    error = error_before = error_after = jnp.zeros_like(remain)
    for repeat in range(CSWEEPS):
        alpha = norm_now / total(direction * image)
        error = error + alpha * direction
        error_before = error_before + alpha * sides[0]
        error_after = error_after + alpha * sides[1]
        if repeat == CSWEEPS - 1:
            break
        remain = remain - alpha * image
        remain_sides = [r - alpha * q for r, q in zip(remain_sides, image_sides)]
        applied = apply(remain, remain_sides)
        applied_sides = around(applied)
        norm_next = total(remain * remain)
        beta = norm_next / norm_now
        direction = remain + beta * direction
        sides = [r + beta * p for r, p in zip(remain_sides, sides)]
        image = applied + beta * image
        image_sides = [w + beta * q for w, q in zip(applied_sides, image_sides)]
        norm_now = norm_next

    near = jnp.where(
        first_row,
        jnp.where(places3.has_before_y(2), error_before, 0.0),
        jnp.where(places3.has_after_y(2), error_after, 0.0),
    )
    error = 0.75 * error + 0.25 * near
    lower = 0.75 * error + 0.25 * before_x(error)
    upper = 0.75 * error + 0.25 * after_x(error)
    fine = jnp.stack([lower, upper], 1).reshape(k2.shape)
    near = jnp.where(
        (places.lane & 4) == 0,
        jnp.where(places.has_before_z(1), ring(fine, 4, 2), 0.0),
        jnp.where(places.has_after_z(1), ring(fine, -4, 2), 0.0),
    )
    return error_two + (0.75 * fine + 0.25 * near)


def finish(grid, wide, smoothed, error_one, out, e1, e0):
    cells_x, cells_y, depth = smoothed.shape
    i, j = lax.axis_index("gx"), lax.axis_index("gy")
    first = 8 - 2
    count = cells_y + 8
    lane = lax.broadcasted_iota(jnp.int32, (count, depth), 1)
    row = lax.broadcasted_iota(jnp.int32, (count, depth), 0) - 2

    def widen_z(value, stride, lane):
        down = jnp.where(lane >= stride, pltpu.roll(value, stride, 1), 0.0)
        up = jnp.where(lane < depth - stride, pltpu.roll(value, depth - stride, 1), 0.0)
        return 0.75 * value + 0.25 * jnp.where((lane & stride) == 0, down, up)

    def widen_y(ref, index, first, count, stride, row):
        centre = ref[index, pl.ds(first, count), :]
        down = ref[index, pl.ds(first - stride, count), :]
        up = ref[index, pl.ds(first + stride, count), :]
        return 0.75 * centre + 0.25 * jnp.where((row & stride) == 0, down, up)

    low_row = jnp.where(j > 0, -cells_y, 0)
    high_row = jnp.where(j < grid[1] - 1, 2 * cells_y, cells_y)
    inside = (row >= low_row) & (row < high_row)
    planes_two = cells_x // 4 + 2
    mid = [widen_z(widen_y(wide, x, first, count, 2, row), 2, lane) for x in range(planes_two)]
    for x in range(cells_x // 2 + 2):
        centre = (x + 1) // 2
        near = centre + (1 if x % 2 == 0 else -1)
        value = jnp.where(inside, 0.75 * mid[centre] + 0.25 * mid[near], 0.0)
        if x == 0:
            value = jnp.where(i > 0, value, 0.0)
        if x == cells_x // 2 + 1:
            value = jnp.where(i < grid[0] - 1, value, 0.0)
        here = pl.ds(first, count)
        e1[x, here, :] = error_one[x, here, :] + value

    lane = lax.broadcasted_iota(jnp.int32, (cells_y, depth), 1)
    row = lax.broadcasted_iota(jnp.int32, (cells_y, depth), 0)
    for x in range(cells_x // 2 + 2):
        e0[x] = widen_z(widen_y(e1, x, 8, cells_y, 1, row), 1, lane)
    for x in range(cells_x):
        centre = x // 2 + 1
        near = centre + (-1 if x % 2 == 0 else 1)
        out[x] = smoothed[x] + (0.75 * e0[centre] + 0.25 * e0[near])


def correct_kernel(grid, gathered, smoothed, error_one, out, whole, strip, wide, e1, e0):
    cells_y = smoothed.shape[1]
    nx, ny = grid
    i, j = lax.axis_index("gx"), lax.axis_index("gy")
    lane = lax.broadcasted_iota(jnp.int32, (8, 128), 1) & 3
    fields = [[], []]
    for column in range(nx):
        parts = [gathered[column * ny + part] for part in range(ny)]
        for field in range(2):
            for x in range(2):
                place = 2 * field + x
                plane = None
                for part in range(ny):
                    turned = parts[part] if part == place else ring(parts[part], part - place, 1)
                    plane = turned if plane is None else jnp.where(lane == part, turned, plane)
                fields[field].append(plane)
    rhs2 = jnp.stack(fields[0], 0)
    k2 = jnp.stack(fields[1], 0)
    planes = 2 * nx
    whole[0] = jnp.zeros((8, 128), jnp.float32)
    whole[planes + 1] = jnp.zeros((8, 128), jnp.float32)
    whole[pl.ds(1, planes)] = whole_solve(k2, rhs2)

    masks = [[(j + side - lane) == shift for shift in range(-4, 5)] for side in (-1, 0, 1)]
    inside = (j > 0, True, j < ny - 1)
    for x in range(4):
        plane = whole[2 * i + x]
        turned = [plane if shift == 0 else ring(plane, -shift, 1) for shift in range(-4, 5)]
        for index in range(3):
            value = jnp.zeros_like(plane)
            for mask, each in zip(masks[index], turned):
                value = jnp.where(mask, each, value)
            strip[x, pl.ds(8 * index, 8), :] = value if index == 1 else jnp.where(inside[index], value, 0.0)
        for place in range(4):
            wide[x, pl.ds(4 + place, 8, stride=4), :] = strip[x, pl.ds(7, 8), :]
            wide[x, pl.ds(36 + place, 2, stride=4), :] = strip[x, pl.ds(15, 2), :]
    finish(grid, wide, smoothed, error_one, out, e1, e0)


def finish_kernel(grid, wide, smoothed, error_one, out, e1, e0):
    finish(grid, wide, smoothed, error_one, out, e1, e0)


def last_scratch(cells_x, cells_y, depth):
    count = cells_x // 2 + 2
    return [
        pltpu.VMEM((count, cells_y + 16, depth), jnp.float32),
        pltpu.VMEM((count, cells_y, depth), jnp.float32),
    ]


def correct_whole(grid, tiles, smoothed, error_one):
    gathered = lax.all_to_all(tiles, ("gx", "gy"), 0, 0, tiled=False)
    cells_x, cells_y, depth = smoothed.shape
    return pl.pallas_call(
        functools.partial(correct_kernel, grid),
        out_shape=jax.ShapeDtypeStruct(smoothed.shape, jnp.float32),
        scratch_shapes=[
            pltpu.VMEM((2 * grid[0] + 2, 8, depth), jnp.float32),
            pltpu.VMEM((4, 24, depth), jnp.float32),
            pltpu.VMEM((4, cells_y + 16, depth), jnp.float32),
        ]
        + last_scratch(cells_x, cells_y, depth),
        compiler_params=pltpu.CompilerParams(vmem_limit_bytes=VMEM_LIMIT),
        name="correct",
    )(gathered, smoothed, error_one)


def with_faces(shard):
    for axis, dim in (("gx", 0), ("gy", 1)):
        length = shard.shape[dim]
        last = lax.slice_in_dim(shard, length - 1, length, axis=dim)
        initial = lax.slice_in_dim(shard, 0, 1, axis=dim)
        before = lax.ppermute(last, axis, shifts(axis, 1))
        after = lax.ppermute(initial, axis, shifts(axis, -1))
        shard = jnp.concatenate([before, shard, after], axis=dim)
    return shard


def with_zeros(field):
    return jnp.pad(field, ((1, 1), (1, 1), (0, 0)))


def pad_depth(field):
    return jnp.pad(field, ((0, 0), (0, 0), (1, 1)))


def restrict(field):
    size_x, size_y, size_z = field.shape
    return field.reshape(size_x // 2, 2, size_y // 2, 2, size_z // 2, 2).mean(axis=(1, 3, 5))


def level_weights(coef_pad):
    c = pad_depth(coef_pad)
    wx = (c[1:, 1:-1, 1:-1] + c[:-1, 1:-1, 1:-1]) * 0.5
    wy = (c[1:-1, 1:, 1:-1] + c[1:-1, :-1, 1:-1]) * 0.5
    wz = (c[1:-1, 1:-1, 1:] + c[1:-1, 1:-1, :-1]) * 0.5
    diagonal = wx[1:] + wx[:-1] + wy[:, 1:] + wy[:, :-1] + wz[:, :, 1:] + wz[:, :, :-1]
    return (wx, wy, wz), diagonal


def neighbour_sum(field_pad, weights):
    wx, wy, wz = weights
    v = pad_depth(field_pad)
    total = wx[:-1] * v[:-2, 1:-1, 1:-1] + wx[1:] * v[2:, 1:-1, 1:-1]
    total = total + wy[:, :-1] * v[1:-1, :-2, 1:-1] + wy[:, 1:] * v[1:-1, 2:, 1:-1]
    return total + wz[:, :, :-1] * v[1:-1, 1:-1, :-2] + wz[:, :, 1:] * v[1:-1, 1:-1, 2:]


def prolong_axis(padded, axis):
    length = padded.shape[axis]
    middle = lax.slice_in_dim(padded, 1, length - 1, axis=axis)
    before = lax.slice_in_dim(padded, 0, length - 2, axis=axis)
    after = lax.slice_in_dim(padded, 2, length, axis=axis)
    joined = jnp.stack([0.75 * middle + 0.25 * before, 0.75 * middle + 0.25 * after], axis=axis + 1)
    shape = list(middle.shape)
    shape[axis] = 2 * shape[axis]
    return joined.reshape(shape)


def coarse_solve(rhs, weights, diagonal):
    error = jnp.zeros_like(rhs)
    remain = rhs
    direction = rhs
    norm_now = jnp.sum(remain * remain)
    for _ in range(CSWEEPS):
        image = (diagonal * direction - neighbour_sum(with_zeros(direction), weights)) * 4.0**-3
        alpha = norm_now / jnp.sum(direction * image)
        error = error + alpha * direction
        remain = remain - alpha * image
        norm_next = jnp.sum(remain * remain)
        direction = remain + norm_next / norm_now * direction
        norm_now = norm_next
    return error


def correct_spread(grid, tiles, smoothed, error_one):
    cells_x, cells_y, depth = smoothed.shape
    shape2 = (cells_x // 4, cells_y // 4, depth // 4)
    own = tiles[0].reshape(shape2[1], shape2[2], 2, shape2[0]).transpose(2, 3, 0, 1)
    rhs2, k2 = own[0], own[1]
    weights, diagonal = level_weights(with_faces(k2))
    parity = sum(lax.broadcasted_iota(jnp.int32, shape2, d) for d in range(3)) % 2
    error_two = jnp.where(parity == 0, rhs2 * 16.0 / diagonal, 0.0)
    total = neighbour_sum(with_faces(error_two), weights)
    error_two = jnp.where(parity == 1, (rhs2 * 16.0 + total) / diagonal, error_two)
    total = neighbour_sum(with_faces(error_two), weights)
    rhs3 = restrict(rhs2 - (diagonal * error_two - total) * 4.0**-2)
    merged = jnp.stack([rhs3, restrict(k2)])
    merged = lax.all_gather(merged, "gx", axis=1, tiled=True)
    merged = lax.all_gather(merged, "gy", axis=2, tiled=True)
    weights3, diagonal3 = level_weights(with_zeros(merged[1]))
    error_three = coarse_solve(merged[0], weights3, diagonal3)
    start_x = lax.axis_index("gx") * rhs3.shape[0]
    start_y = lax.axis_index("gy") * rhs3.shape[1]
    window = lax.dynamic_slice(
        with_zeros(error_three),
        (start_x, start_y, jnp.int32(0)),
        (rhs3.shape[0] + 2, rhs3.shape[1] + 2, rhs3.shape[2]),
    )
    finer = pad_depth(window)
    for axis in range(3):
        finer = prolong_axis(finer, axis)
    wide = with_faces(error_two + finer)
    wide = jnp.repeat(jnp.repeat(wide, 4, axis=1), 4, axis=2)
    wide = jnp.pad(wide, ((0, 0), (4, 4), (0, 0)))
    return pl.pallas_call(
        functools.partial(finish_kernel, grid),
        out_shape=jax.ShapeDtypeStruct(smoothed.shape, jnp.float32),
        scratch_shapes=last_scratch(cells_x, cells_y, depth),
        compiler_params=pltpu.CompilerParams(vmem_limit_bytes=VMEM_LIMIT),
        name="finish",
    )(wide, smoothed, error_one)


def on_device(pressure, source, coefficient):
    grid = (lax.axis_size("gx"), lax.axis_size("gy"))
    _, cells_y, depth = pressure.shape
    fits = grid[1] == 4 and cells_y == 32 and depth == 128
    own = (pressure, source, coefficient)
    block = stacked(*own)
    halo = fine_halo(own, block)
    copies = grid[0] * grid[1] if fits else 1
    smoothed, error_one, tiles = smooth(copies, block, halo)
    correct = correct_whole if fits else correct_spread
    return correct(grid, tiles, smoothed, error_one)


def solution(mesh):
    spec = P("gx", "gy", None)
    return jax.shard_map(on_device, mesh=mesh, in_specs=(spec, spec, spec), out_specs=spec, check_vma=False)
```
